128 devices in a mesh: dp: 16 (over x, z), mp: 8 (over y, core).
Axes of the slice: x: 4, y: 4, z: 4, core: 2. Of those that a mesh axis runs over, the one named last changes fastest.
Arguments:
- inputs: int32 [64, 512], P('dp'), may hold values from 0 to 255
- targets: int32 [64, 512], P('dp'), may hold values from 0 to 255
- valid_mask: int32 [64, 512], P('dp'), may hold values from 0 to 1
- memory: bfloat16 [2, 64, 512, 512], P(None, 'dp'), may hold values from -6 to 6
- attention_rank: int32 [2, 5, 8, 8], P(None, None, None, 'mp'), may hold values from 0 to 9
- feedforward_rank: int32 [2, 2, 8, 32], P(None, None, None, 'mp'), may hold values from 0 to 9
- attention_weight: float32 [2, 5, 512, 512], P(None, None, None, 'mp'), may hold values from -0.25 to 0.25
- attention_moment: float32 [2, 5, 512, 512], P(None, None, None, 'mp'), may hold values from -0.0034179688 to 0.0034179688
- attention_average: float32 [2, 5, 512, 512], P(None, None, None, 'mp'), may hold values from -0.25 to 0.25
- feedforward_weight: float32 [2, 2, 512, 2048], P(None, None, None, 'mp'), may hold values from -0.625 to 0.625
- feedforward_moment: float32 [2, 2, 512, 2048], P(None, None, None, 'mp'), may hold values from -0.0034179688 to 0.0034179688
- feedforward_average: float32 [2, 2, 512, 2048], P(None, None, None, 'mp'), may hold values from -0.625 to 0.625
- embedding_weight: float32 [256, 512], replicated, may hold values from -8 to 8
- embedding_moment: float32 [256, 512], replicated, may hold values from -0.0034179688 to 0.0034179688
- embedding_average: float32 [256, 512], replicated, may hold values from -8 to 8
- head_bias_weight: float32 [2, 2, 512], P(None, None, 'mp'), may hold values from -1.75 to 1.75
- head_bias_moment: float32 [2, 2, 512], P(None, None, 'mp'), may hold values from -0.0034179688 to 0.0034179688
- head_bias_average: float32 [2, 2, 512], P(None, None, 'mp'), may hold values from -1.75 to 1.75
- inner_bias_weight: float32 [2, 2048], P(None, 'mp'), may hold values from -0.625 to 0.625
- inner_bias_moment: float32 [2, 2048], P(None, 'mp'), may hold values from -0.0034179688 to 0.0034179688
- inner_bias_average: float32 [2, 2048], P(None, 'mp'), may hold values from -0.625 to 0.625
- norm_weight: float32 [2, 5, 512], replicated, as said below
- norm_moment: float32 [2, 5, 512], replicated, may hold values from -0.0034179688 to 0.0034179688
- norm_average: float32 [2, 5, 512], replicated, may hold values from -3 to 3
Outputs:
- ce_total: float32 [], replicated
- valid_count: float32 [], replicated
- new_memory: bfloat16 [2, 64, 512, 512], P(None, 'dp')
- attention_grad: float32 [2, 5, 512, 512], P(None, None, None, 'mp')
- attention_next: float32 [2, 5, 512, 512], P(None, None, None, 'mp')
- attention_moment_next: float32 [2, 5, 512, 512], P(None, None, None, 'mp')
- attention_average_next: float32 [2, 5, 512, 512], P(None, None, None, 'mp')
- feedforward_grad: float32 [2, 2, 512, 2048], P(None, None, None, 'mp')
- feedforward_next: float32 [2, 2, 512, 2048], P(None, None, None, 'mp')
- feedforward_moment_next: float32 [2, 2, 512, 2048], P(None, None, None, 'mp')
- feedforward_average_next: float32 [2, 2, 512, 2048], P(None, None, None, 'mp')
- embedding_next: float32 [256, 512], replicated
- embedding_moment_next: float32 [256, 512], replicated
- embedding_average_next: float32 [256, 512], replicated
- head_bias_next: float32 [2, 2, 512], P(None, None, 'mp')
- head_bias_moment_next: float32 [2, 2, 512], P(None, None, 'mp')
- head_bias_average_next: float32 [2, 2, 512], P(None, None, 'mp')
- inner_bias_next: float32 [2, 2048], P(None, 'mp')
- inner_bias_moment_next: float32 [2, 2048], P(None, 'mp')
- inner_bias_average_next: float32 [2, 2048], P(None, 'mp')
- norm_grad: float32 [2, 5, 512], replicated
- norm_next: float32 [2, 5, 512], replicated
- norm_moment_next: float32 [2, 5, 512], replicated
- norm_average_next: float32 [2, 5, 512], replicated
The draws below stay inside these ranges and needn't reach their ends.
Inputs may be any that keep to these rules, and one draw needn't show every extreme that they name: `norm_weight`: rows 0 and 2 of each layer are gains near 1, the others offsets and biases of both signs.
All inputs are finite; a program needn't handle non-finite values.
Results may differ from the reference program's by a relative error of at most 0.011.
Values may be sent and summed in bfloat16 or wider, within the bound.
A program may use at most 192 MiB of HBM per device.

```python
import math
import jax
import jax.numpy as jnp
import numpy as np
from jax import lax

D = 512
HEADS = 8
HD = 64
FF = 2048
VOCAB = 256
SEG = 512
MEM = 512
LAYERS = 2
BLK = 64
SEGS = 64
KLEN = 1024


def draw_norm_weight(key, part):
    noise = jax.random.normal(key, (LAYERS, 5, D), jnp.float32)
    rows_kind = jnp.arange(5)
    is_gain = ((rows_kind == 0) | (rows_kind == 2)).astype(jnp.float32)[None, :, None]
    return is_gain * (1.0 + 0.15 * noise) + (1.0 - is_gain) * (0.3 * noise)


def draw_valid_mask(key, part):
    total_rows = SEGS * SEG
    place = jnp.arange(total_rows, dtype=jnp.int32).reshape(SEGS, SEG)
    threshold = 200 + 700 * place // total_rows
    coins = jax.random.randint(key, (SEGS, SEG), 0, 1000, dtype=jnp.int32)
    return (coins < threshold).astype(jnp.int32)


def set_ends(result, own_key, smallest, largest):
    longest = result.shape.index(max(result.shape))
    spots = []
    for shift in (0, 1):
        where = [jax.random.randint(jax.random.fold_in(own_key, axis), (), 0, length) for axis, length in enumerate(result.shape)]
        where[longest] = (where[longest] + shift) % result.shape[longest]
        spots.append(tuple(where))
    return result.at[spots[0]].set(smallest).at[spots[1]].set(largest)


def block_scale(own_key, dims, pieces, least, high):
    gain = 1.0
    for position, parts in pieces:
        heights = jax.random.uniform(jax.random.fold_in(jax.random.fold_in(own_key, 6), position), (parts,), jnp.float32, least / len(pieces), high / len(pieces))
        gain = gain * jnp.repeat(jnp.exp(heights), dims[position] // parts).reshape((-1,) + (1,) * (len(dims) - 1 - position))
    return gain


def rank_bounds(amount, lean):
    portions = [(1 << 20) // math.isqrt(grade ** lean) + 1 for grade in range(1, amount + 1)]
    scale = 1 + sum(portions) // (1 << 30)
    return np.cumsum(np.array([max(1, weight // scale) for weight in portions]))


def skewed_ids(stream_key, shape, number_of, skew):
    listing = rank_bounds(number_of, skew)
    pick = jax.random.randint(jax.random.fold_in(stream_key, 1), shape, 0, int(listing[number_of - 1]))
    standing = jnp.searchsorted(jnp.asarray(listing, jnp.int32), pick, side="right")
    return jax.random.permutation(jax.random.fold_in(stream_key, 2), number_of)[standing].astype(jnp.int32)


def gaussian(stream_key, shape, scale, reach, shards=(), held_as=jnp.bfloat16):
    drawn = scale * jax.random.normal(stream_key, shape, jnp.float32)
    if shards:
        drawn = drawn * block_scale(stream_key, shape, shards, -0.22, 0.18)
    return jnp.clip(drawn, -reach, reach).astype(held_as)


def setup_inputs(seed: int = 0) -> dict:
    key_of = jax.random.split(jax.random.key(seed), 25)
    return {
        "inputs": set_ends(skewed_ids(key_of[0], (SEGS, SEG), VOCAB, 2), jax.random.fold_in(key_of[0], 3), 0, VOCAB - 1).astype(jnp.int32),
        "targets": set_ends(skewed_ids(key_of[1], (SEGS, SEG), VOCAB, 2), jax.random.fold_in(key_of[1], 3), 0, VOCAB - 1).astype(jnp.int32),
        "valid_mask": draw_valid_mask(jax.random.fold_in(key_of[24], 71), 0),
        "memory": gaussian(key_of[3], (LAYERS, SEGS, MEM, D), 1.0, 6.0, ((1, 16),)),
        "attention_rank": set_ends(jax.random.randint(key_of[4], (LAYERS, 5, D // BLK, D // BLK), 0, 10), jax.random.fold_in(key_of[4], 1), 0, 9).astype(jnp.int32),
        "feedforward_rank": set_ends(jax.random.randint(key_of[5], (LAYERS, 2, D // BLK, FF // BLK), 0, 10), jax.random.fold_in(key_of[5], 1), 0, 9).astype(jnp.int32),
        "attention_weight": gaussian(key_of[6], (LAYERS, 5, D, D), D ** -0.5, 0.25, ((3, 8),), jnp.float32),
        "attention_moment": gaussian(key_of[7], (LAYERS, 5, D, D), (0.1 / (SEGS * SEG) ** 0.5), 0.0034179688, ((3, 8),), jnp.float32),
        "attention_average": gaussian(key_of[8], (LAYERS, 5, D, D), D ** -0.5, 0.25, ((3, 8),), jnp.float32),
        "feedforward_weight": gaussian(key_of[9], (LAYERS, 2, D, FF), (D // 5) ** -0.5, 0.625, ((3, 8),), jnp.float32),
        "feedforward_moment": gaussian(key_of[10], (LAYERS, 2, D, FF), (0.1 / (SEGS * SEG) ** 0.5), 0.0034179688, ((3, 8),), jnp.float32),
        "feedforward_average": gaussian(key_of[11], (LAYERS, 2, D, FF), (D // 5) ** -0.5, 0.625, ((3, 8),), jnp.float32),
        "embedding_weight": gaussian(key_of[12], (VOCAB, D), 1.5, 8.0, (), jnp.float32),
        "embedding_moment": gaussian(key_of[13], (VOCAB, D), (0.1 / (SEGS * SEG) ** 0.5), 0.0034179688, (), jnp.float32),
        "embedding_average": gaussian(key_of[14], (VOCAB, D), 1.5, 8.0, (), jnp.float32),
        "head_bias_weight": gaussian(key_of[15], (LAYERS, 2, D), 0.3, 1.75, ((2, 8),), jnp.float32),
        "head_bias_moment": gaussian(key_of[16], (LAYERS, 2, D), (0.1 / (SEGS * SEG) ** 0.5), 0.0034179688, ((2, 8),), jnp.float32),
        "head_bias_average": gaussian(key_of[17], (LAYERS, 2, D), 0.3, 1.75, ((2, 8),), jnp.float32),
        "inner_bias_weight": gaussian(key_of[18], (LAYERS, FF), 0.1, 0.625, ((1, 8),), jnp.float32),
        "inner_bias_moment": gaussian(key_of[19], (LAYERS, FF), (0.1 / (SEGS * SEG) ** 0.5), 0.0034179688, ((1, 8),), jnp.float32),
        "inner_bias_average": gaussian(key_of[20], (LAYERS, FF), 0.1, 0.625, ((1, 8),), jnp.float32),
        "norm_weight": draw_norm_weight(jax.random.fold_in(key_of[24], 71), 0),
        "norm_moment": gaussian(key_of[22], (LAYERS, 5, D), (0.1 / (SEGS * SEG) ** 0.5), 0.0034179688, (), jnp.float32),
        "norm_average": gaussian(key_of[23], (LAYERS, 5, D), 0.5, 3.0, (), jnp.float32),
    }


@jax.custom_vjp
def low(v):
    return lax.optimization_barrier(v.astype(jnp.bfloat16)).astype(jnp.float32)

@jax.custom_vjp
def low_back(v):
    return v

def low_keep(v):
    return (low(v), None)

def low_pass(kept, grad):
    return (grad,)

def back_keep(v):
    return (v, None)

def back_low(kept, grad):
    return (low(grad),)
low.defvjp(low_keep, low_pass)
low_back.defvjp(back_keep, back_low)
PRECISE = lax.Precision.HIGHEST
EPSILON = 1e-05
MOMENTUM = 0.9
AVERAGE = 0.9
RATE = 0.3
PENALTY = 0.0001
WIDEN = 5.0

def rounded(value):
    return low_back(low(value))

def product(left_side, right_side):
    return jnp.dot(left_side, right_side, precision=PRECISE, preferred_element_type=jnp.float32)

def smooth_unit(value):
    return 0.5 * value * (1.0 + jnp.tanh(0.7978845608028654 * (value + 0.044715 * value * value * value)))

def positions(key_length, model_width):
    distance = jnp.arange(key_length).astype(jnp.float32)
    frequency = 1.0 / 10000.0 ** (jnp.arange(0, model_width, 2).astype(jnp.float32) / model_width)
    angles = distance[:, None] * frequency[None, :]
    return jnp.concatenate([jnp.sin(angles), jnp.cos(angles)], axis=1)

def expand(block_rank, block_size):
    return jnp.repeat(jnp.repeat(block_rank, block_size, axis=-2), block_size, axis=-1)

def layer_norm(values, norm_gain, norm_offset):
    centred = values - lax.optimization_barrier(jnp.mean(values, axis=-1, keepdims=True))
    spread = lax.optimization_barrier(jnp.mean(centred * centred, axis=-1, keepdims=True))
    return centred * lax.rsqrt(spread + EPSILON) * norm_gain + norm_offset

def attend(hidden_low, memory_low, weights, content_bias, position_bias, table_low, geometry):
    shift_index, allowed = geometry
    joined = jnp.concatenate([memory_low, hidden_low], axis=0)
    raw_query = low_back(product(hidden_low, weights[0]))
    query_u = rounded(raw_query + content_bias).reshape(SEG, HEADS, HD)
    query_w = rounded(raw_query + position_bias).reshape(SEG, HEADS, HD)
    key_rows = rounded(product(joined, weights[1])).reshape(KLEN, HEADS, HD)
    value_rows = rounded(product(joined, weights[2])).reshape(KLEN, HEADS, HD)
    rel_rows = rounded(product(table_low, weights[3])).reshape(KLEN, HEADS, HD)
    direct = jnp.einsum('she,khe->hsk', query_u, key_rows, precision=PRECISE)
    table_part = jnp.einsum('she,dhe->hsd', query_w, rel_rows, precision=PRECISE)
    shifted = jnp.take_along_axis(table_part, jnp.broadcast_to(shift_index, table_part.shape), axis=2)
    scores = low_back((direct + shifted) * HD ** (-0.5))
    scores = jnp.where(allowed, scores, -1e+30)
    probabilities = low(jax.nn.softmax(scores, axis=-1))
    mixed = rounded(jnp.einsum('hsk,khe->she', probabilities, value_rows, precision=PRECISE).reshape(SEG, D))
    return low_back(product(mixed, weights[4].T))

def segment(params, tokens_seg, targets_seg, valid_seg, memory_seg, geometry, table_low):
    attention_eff, feedforward_eff, embedding, head_bias, inner_bias, norms = params
    hidden = embedding[tokens_seg]
    kept_hidden = []
    for layer_idx in range(LAYERS):
        hidden_low = low(hidden)
        kept_hidden.append(hidden_low)
        weights = low(attention_eff[layer_idx])
        attended = attend(hidden_low, memory_seg[layer_idx], weights, head_bias[layer_idx, 0], head_bias[layer_idx, 1], table_low, geometry)
        middle = layer_norm(hidden + attended, norms[layer_idx, 0], norms[layer_idx, 1])
        middle_low = low(middle)
        inner_pre = low_back(product(middle_low, low(feedforward_eff[layer_idx, 0])) + inner_bias[layer_idx])
        active = low(smooth_unit(inner_pre))
        branch = low_back(product(active, low(feedforward_eff[layer_idx, 1]).T)) + norms[layer_idx, 4]
        hidden = layer_norm(middle + branch, norms[layer_idx, 2], norms[layer_idx, 3])
    logits = low_back(product(low(hidden), low(embedding).T) * D ** (-0.5))
    log_total = jax.nn.logsumexp(logits, axis=-1)
    picked = jnp.take_along_axis(logits, targets_seg[:, None], axis=1)[:, 0]
    return (jnp.sum(valid_seg * (log_total - picked)), jnp.stack(kept_hidden))

def advance(weight, moment, average, grad):
    moment_next = MOMENTUM * moment + grad
    direction = grad + MOMENTUM * moment_next
    trust_ratio = jnp.sqrt(jnp.sum(weight * weight)) / jnp.sqrt(jnp.sum(direction * direction))
    weight_next = weight - RATE * trust_ratio * direction
    return (weight_next, moment_next, AVERAGE * average + (1.0 - AVERAGE) * weight_next)

def reference(inputs, targets, valid_mask, memory, attention_rank, feedforward_rank, attention_weight, attention_moment, attention_average, feedforward_weight, feedforward_moment, feedforward_average, embedding_weight, embedding_moment, embedding_average, head_bias_weight, head_bias_moment, head_bias_average, inner_bias_weight, inner_bias_moment, inner_bias_average, norm_weight, norm_moment, norm_average):
    attention_a = expand(attention_rank < 2, BLK).astype(jnp.float32)
    attention_b = expand(attention_rank < 3, BLK).astype(jnp.float32)
    feedforward_a = expand(feedforward_rank < 2, BLK).astype(jnp.float32)
    feedforward_b = expand(feedforward_rank < 3, BLK).astype(jnp.float32)
    valid_float = valid_mask.astype(jnp.float32)
    valid_count = jnp.sum(valid_float)
    row_index = jnp.arange(SEG)[:, None]
    col_index = jnp.arange(KLEN)[None, :]
    distance = MEM + row_index - col_index
    geometry = (jnp.clip(distance, 0, KLEN - 1).astype(jnp.int32), distance >= 0)
    table_low = low(positions(KLEN, D))
    memory_seg = jnp.transpose(memory.astype(jnp.float32), (1, 0, 2, 3))

    def objective(attention_eff, feedforward_eff, embedding, head_bias, inner_bias, norms):
        params = (attention_eff, feedforward_eff, embedding, head_bias, inner_bias, norms)

        def per_segment(segment_item):
            return segment(params, segment_item[0], segment_item[1], segment_item[2], segment_item[3], geometry, table_low)
        ce_parts, kept_hidden = lax.map(jax.checkpoint(per_segment), (inputs, targets, valid_float, memory_seg))
        ce_sum = jnp.sum(ce_parts)
        return (ce_sum / valid_count, (kept_hidden, ce_sum))
    loss_ce, pullback, extras = jax.vjp(objective, attention_weight * attention_a, feedforward_weight * feedforward_a, embedding_weight, head_bias_weight, inner_bias_weight, norm_weight, has_aux=True)
    kept_hidden, ce_sum = extras
    grads = pullback(jnp.ones_like(loss_ce))
    attention_coef = attention_a + WIDEN * (attention_b - attention_a)
    feedforward_coef = feedforward_a + WIDEN * (feedforward_b - feedforward_a)

    def penalty_of(attention_all, feedforward_all):
        return PENALTY * (jnp.sum(attention_all * attention_all * attention_coef) + jnp.sum(feedforward_all * feedforward_all * feedforward_coef))
    penalty, penalty_back = jax.vjp(penalty_of, attention_weight, feedforward_weight)
    penalty_attention, penalty_feedforward = penalty_back(jnp.ones_like(penalty))
    attention_grad = attention_b * grads[0] + penalty_attention
    feedforward_grad = feedforward_b * grads[1] + penalty_feedforward
    attention_set = advance(attention_weight, attention_moment, attention_average, attention_grad)
    feedforward_set = advance(feedforward_weight, feedforward_moment, feedforward_average, feedforward_grad)
    embedding_set = advance(embedding_weight, embedding_moment, embedding_average, grads[2])
    head_bias_set = advance(head_bias_weight, head_bias_moment, head_bias_average, grads[3])
    inner_bias_set = advance(inner_bias_weight, inner_bias_moment, inner_bias_average, grads[4])
    norm_set = advance(norm_weight, norm_moment, norm_average, grads[5])
    new_memory = jnp.transpose(kept_hidden, (1, 0, 2, 3)).astype(jnp.bfloat16)
    return (ce_sum, valid_count, new_memory, attention_grad, attention_set[0], attention_set[1], attention_set[2], feedforward_grad, feedforward_set[0], feedforward_set[1], feedforward_set[2], embedding_set[0], embedding_set[1], embedding_set[2], head_bias_set[0], head_bias_set[1], head_bias_set[2], inner_bias_set[0], inner_bias_set[1], inner_bias_set[2], grads[5], norm_set[0], norm_set[1], norm_set[2])
```

```python
import functools

import jax
import jax.numpy as jnp
import numpy as np
from jax import lax
from jax.experimental import pallas as pl
from jax.experimental.pallas import tpu as pltpu
from jax.sharding import PartitionSpec as P

HD = 64
D = 512
FF = 2048
SEG = 512
KLEN = 1024
OWN = 256
HEADS = 8
VOCAB = 256
MP = 8

EPSILON = 1e-05
MOMENTUM = 0.9
AVERAGE = 0.9
RATE = 0.3
PENALTY = 0.0001
WIDEN = 5.0
F32 = jnp.float32
BF16 = jnp.bfloat16
SCALE = HD ** (-0.5)


def dot_nn(a, b):
    return lax.dot_general(a, b, (((1,), (0,)), ((), ())), preferred_element_type=F32)


def dot_nt(a, b):
    return lax.dot_general(a, b, (((1,), (1,)), ((), ())), preferred_element_type=F32)


def smooth_unit(v):
    return 0.5 * v * (1.0 + jnp.tanh(0.7978845608028654 * (v + 0.044715 * v * v * v)))


def smooth_both(v):
    squared = v * v
    t = jnp.tanh(0.7978845608028654 * (v + 0.044715 * squared * v))
    half = 0.5 * (1.0 + t)
    slope = half + 0.5 * v * (1.0 - t * t) * (
        0.7978845608028654 * (1.0 + 3.0 * 0.044715 * squared)
    )
    return v * half, slope


def tables():
    freq = (1.0 / 10000.0 ** (np.arange(0, D, 2).astype(np.float32) / np.float32(D))).astype(
        np.float32
    )
    turned = []
    for half in range(2):
        distance = (SEG + half * OWN - np.arange(KLEN)) % KLEN
        angle = (distance.astype(np.float32)[:, None] * freq[None, :]).astype(np.float64)
        turned.append(np.concatenate([np.sin(angle), np.cos(angle)], axis=1).astype(np.float32))
    return jnp.asarray(np.stack(turned), BF16)


def norm_forward(values):
    centred = values - jnp.mean(values, axis=-1, keepdims=True)
    inverse = lax.rsqrt(jnp.mean(centred * centred, axis=-1, keepdims=True) + EPSILON)
    return centred * inverse, inverse


def norm_backward(grad, normed, inverse, gain):
    scaled = grad * gain
    grad_in = inverse * (
        scaled
        - jnp.mean(scaled, axis=-1, keepdims=True)
        - normed * jnp.mean(scaled * normed, axis=-1, keepdims=True)
    )
    return (
        grad_in,
        jnp.sum(grad * normed, axis=0, keepdims=True),
        jnp.sum(grad, axis=0, keepdims=True),
    )


def transposed(value):
    return value.astype(F32).T


def forward_kernel(
    offset_ref,
    hidden_ref,
    low_ref,
    memory_ref,
    att_ref,
    ff_ref,
    bias_ref,
    inner_bias_ref,
    norm_ref,
    table_ref,
    out_ref,
    prob_ref,
    query_u_ref,
    query_w_ref,
    mixed_ref,
    normed_one_ref,
    inverse_one_ref,
    normed_two_ref,
    inverse_two_ref,
    keys_ref,
    values_ref,
    rel_ref,
    score_ref,
    low_prob_ref,
    part_ref,
):
    own_low = hidden_ref[...].astype(BF16)
    query = dot_nt(own_low, att_ref[0])
    query_u_ref[...] = (query + bias_ref[0:1, :]).astype(BF16)
    query_w_ref[...] = (query + bias_ref[1:2, :]).astype(BF16)
    for half, source in ((0, memory_ref), (1, low_ref)):
        rows = source[...]
        cols = slice(half * SEG, (half + 1) * SEG)
        keys_ref[:, cols] = dot_nt(att_ref[1], rows).astype(BF16)
        values = dot_nt(rows, att_ref[2]).astype(BF16)
        values_ref[0, cols, :] = values[:, 0:256]
        values_ref[1, cols, :] = values[:, 256:512]
    rel_ref[...] = dot_nt(att_ref[3], table_ref[...]).astype(BF16)
    offset = offset_ref[0]
    lane_head = lax.broadcasted_iota(jnp.int32, (OWN, 256), 1) // HD
    part_ref[...] = jnp.zeros_like(part_ref)

    def head(h, carry):
        group = h // 4
        mine = lane_head == h % 4
        lanes = pl.ds(pl.multiple_of(group * 256, 256), 256)
        query_u = jnp.where(mine, query_u_ref[:, lanes].astype(F32), 0.0).astype(BF16)
        query_w = jnp.where(mine, query_w_ref[:, lanes].astype(F32), 0.0).astype(BF16)
        score_ref[...] = dot_nn(query_w, rel_ref[lanes, :])
        prob_ref[h] = dot_nn(query_u, keys_ref[lanes, :])
        for b in range(0, OWN, ROWS):
            rows = slice(b, b + ROWS)
            moved = pltpu.roll(score_ref[rows, :], b, 1, stride=1, stride_axis=0)
            score = (prob_ref[h, rows, :] + moved) * SCALE
            key_id = lax.broadcasted_iota(jnp.int32, (ROWS, KLEN), 1)
            query_id = lax.broadcasted_iota(jnp.int32, (ROWS, KLEN), 0) + (offset + b + SEG)
            score = jnp.where(key_id <= query_id, score, -1e30)
            expo = jnp.exp(score - jnp.max(score, axis=-1, keepdims=True))
            prob = expo * (1.0 / jnp.sum(expo, axis=-1, keepdims=True))
            prob_ref[h, rows, :] = prob
            low_prob_ref[rows, :] = prob.astype(BF16)
        mixed = dot_nn(low_prob_ref[...], values_ref[group])
        part_ref[group] = part_ref[group] + jnp.where(mine, mixed, 0.0)
        return carry

    lax.fori_loop(0, HEADS, head, 0)
    mixed_ref[:, 0:256] = part_ref[0].astype(BF16)
    mixed_ref[:, 256:512] = part_ref[1].astype(BF16)
    attended = dot_nn(mixed_ref[...], att_ref[4])
    normed_one, inverse_one = norm_forward(hidden_ref[...] + attended)
    normed_one_ref[...] = normed_one
    inverse_one_ref[...] = inverse_one
    middle = normed_one * norm_ref[0:1, :] + norm_ref[1:2, :]
    middle_low = middle.astype(BF16)

    def units(m, branch):
        inner = dot_nn(middle_low, ff_ref[0, m]) + inner_bias_ref[m]
        return branch + dot_nt(smooth_unit(inner).astype(BF16), ff_ref[1, m])

    branch = lax.fori_loop(0, MP, units, jnp.zeros((OWN, D), F32))
    normed_two, inverse_two = norm_forward(middle + (branch + norm_ref[4:5, :]))
    normed_two_ref[...] = normed_two
    inverse_two_ref[...] = inverse_two
    out_ref[...] = normed_two * norm_ref[2:3, :] + norm_ref[3:4, :]


ROWS = 64
VMEM_SPEC = pl.BlockSpec(memory_space=pltpu.VMEM)
SMEM_SPEC = pl.BlockSpec(memory_space=pltpu.SMEM)
VMEM_LIMIT = 60 * 1024 * 1024


def layer_forward(offset, hidden, low, memory, att, ff, bias, inner_bias, norms, table):
    shapes = [
        ((OWN, D), F32),
        ((HEADS, OWN, KLEN), F32),
        ((OWN, D), BF16),
        ((OWN, D), BF16),
        ((OWN, D), BF16),
        ((OWN, D), F32),
        ((OWN, 1), F32),
        ((OWN, D), F32),
        ((OWN, 1), F32),
    ]
    return pl.pallas_call(
        forward_kernel,
        out_shape=[jax.ShapeDtypeStruct(s, t) for s, t in shapes],
        in_specs=[SMEM_SPEC] + [VMEM_SPEC] * 9,
        out_specs=[VMEM_SPEC] * len(shapes),
        scratch_shapes=[
            pltpu.VMEM((D, KLEN), BF16),
            pltpu.VMEM((2, KLEN, 256), BF16),
            pltpu.VMEM((D, KLEN), BF16),
            pltpu.VMEM((OWN, KLEN), F32),
            pltpu.VMEM((OWN, KLEN), BF16),
            pltpu.VMEM((2, OWN, 256), F32),
        ],
        compiler_params=pltpu.CompilerParams(vmem_limit_bytes=VMEM_LIMIT),
        name="layer_forward",
    )(offset, hidden, low, memory, att, ff, bias, inner_bias, norms, table)


def backward_kernel(
    offset_ref,
    grad_ref,
    hidden_ref,
    low_ref,
    memory_ref,
    att_ref,
    ff_ref,
    inner_bias_ref,
    norm_ref,
    table_ref,
    prob_ref,
    query_u_ref,
    query_w_ref,
    mixed_ref,
    normed_one_ref,
    inverse_one_ref,
    normed_two_ref,
    inverse_two_ref,
    grad_own_ref,
    kept_ref,
    sent_ref,
    grad_att_ref,
    grad_kv_ref,
    grad_ff_ref,
    grad_bias_ref,
    grad_inner_bias_ref,
    grad_norm_ref,
    keys_ref,
    values_ref,
    rel_ref,
    gmix_ref,
    gmix_t_ref,
    query_t_ref,
    flip_t_ref,
    prob_grad_ref,
    score_grad_ref,
    low_prob_ref,
    turned_ref,
    gquery_ref,
    gkv_ref,
    grel_ref,
):
    own_low = hidden_ref[...].astype(BF16)
    gsum_two, ggain_two, goffset_two = norm_backward(
        grad_ref[...], normed_two_ref[...], inverse_two_ref[...], norm_ref[2:3, :]
    )
    middle = normed_one_ref[...] * norm_ref[0:1, :] + norm_ref[1:2, :]
    middle_low = middle.astype(BF16)
    middle_t = transposed(middle_low).astype(BF16)
    gbranch = gsum_two.astype(BF16)
    gbranch_t = transposed(gbranch).astype(BF16)

    def units(m, gmiddle):
        inner = dot_nn(middle_low, ff_ref[0, m]) + inner_bias_ref[m]
        active, slope = smooth_both(inner)
        ginner = (dot_nn(gbranch, ff_ref[1, m]) * slope).astype(BF16)
        grad_ff_ref[0, m] = dot_nn(middle_t, ginner).astype(BF16)
        grad_ff_ref[1, m] = dot_nn(gbranch_t, active.astype(BF16)).astype(BF16)
        grad_inner_bias_ref[m] = jnp.sum(ginner.astype(F32), axis=0, keepdims=True)
        return gmiddle + dot_nt(ginner, ff_ref[0, m])

    gmiddle = lax.fori_loop(0, MP, units, gsum_two)
    gsum_one, ggain_one, goffset_one = norm_backward(
        gmiddle, normed_one_ref[...], inverse_one_ref[...], norm_ref[0:1, :]
    )
    grad_norm_ref[0:1, :] = ggain_one
    grad_norm_ref[1:2, :] = goffset_one
    grad_norm_ref[2:3, :] = ggain_two
    grad_norm_ref[3:4, :] = goffset_two
    grad_norm_ref[4:5, :] = jnp.sum(gsum_two, axis=0, keepdims=True)
    grad_norm_ref[5:8, :] = jnp.zeros((3, D), F32)
    grad_own_ref[...] = gsum_one
    gattended = gsum_one.astype(BF16)
    grad_att_ref[4] = dot_nn(transposed(mixed_ref[...]).astype(BF16), gattended).astype(BF16)
    gmix = dot_nt(gattended, att_ref[4])
    gmix_ref[...] = gmix.astype(BF16)
    gmix_t_ref[...] = gmix.T.astype(BF16)
    query_t_ref[...] = transposed(query_u_ref[...]).astype(BF16)
    flip = (
        lax.broadcasted_iota(jnp.int32, (OWN, OWN), 0)
        + lax.broadcasted_iota(jnp.int32, (OWN, OWN), 1)
        == OWN - 1
    )
    flip = jnp.where(flip, 1.0, 0.0).astype(BF16)
    flip_t_ref[...] = dot_nn(transposed(query_w_ref[...]).astype(BF16), flip).astype(BF16)
    for half, source in ((0, memory_ref), (1, low_ref)):
        rows = source[...]
        cols = slice(half * SEG, (half + 1) * SEG)
        values_ref[:, cols] = dot_nt(att_ref[2], rows).astype(BF16)
        keys = dot_nt(rows, att_ref[1]).astype(BF16)
        keys_ref[0, cols, :] = keys[:, 0:256]
        keys_ref[1, cols, :] = keys[:, 256:512]
    rel = dot_nt(table_ref[...], att_ref[3]).astype(BF16)
    rel_ref[0] = rel[:, 0:256]
    rel_ref[1] = rel[:, 256:512]
    gquery_ref[...] = jnp.zeros_like(gquery_ref)
    lane_head = lax.broadcasted_iota(jnp.int32, (OWN, 256), 1) // HD

    def head(h, carry):
        group = h // 4
        mine = lane_head == h % 4
        lanes = pl.ds(pl.multiple_of(group * 256, 256), 256)
        row = pl.ds(pl.multiple_of(h * HD, HD), HD)
        gmix_h = jnp.where(mine, gmix_ref[:, lanes].astype(F32), 0.0).astype(BF16)
        prob_grad_ref[...] = dot_nn(gmix_h, values_ref[lanes, :])
        for b in range(0, OWN, ROWS):
            rows = slice(b, b + ROWS)
            prob = prob_ref[h, rows, :]
            gprob = prob_grad_ref[rows, :]
            inner = jnp.sum(prob * gprob, axis=-1, keepdims=True)
            score_grad_ref[rows, :] = (prob * (gprob - inner)).astype(BF16)
            low_prob_ref[rows, :] = prob.astype(BF16)
        sgrad = score_grad_ref[...]
        gquery_ref[0, group] = gquery_ref[0, group] + jnp.where(
            mine, dot_nn(sgrad, keys_ref[group]), 0.0
        )
        gkv_ref[0, row, :] = dot_nn(query_t_ref[row, :], sgrad) * SCALE
        gkv_ref[1, row, :] = dot_nn(gmix_t_ref[row, :], low_prob_ref[...])
        flipped = dot_nn(flip, sgrad).astype(BF16)
        turned_ref[...] = pltpu.roll(flipped, KLEN - OWN + 1, 1, stride=1, stride_axis=0)
        gquery_ref[1, group] = gquery_ref[1, group] + jnp.where(
            mine, dot_nn(turned_ref[...], rel_ref[group]), 0.0
        )
        grel_ref[row, :] = (dot_nn(flip_t_ref[row, :], turned_ref[...]) * SCALE).astype(BF16)
        return carry

    lax.fori_loop(0, HEADS, head, 0)
    for group in range(2):
        lanes = slice(group * 256, (group + 1) * 256)
        gquery_u = (gquery_ref[0, group] * SCALE).astype(BF16)
        gquery_w = dot_nn(flip, (gquery_ref[1, group] * SCALE).astype(BF16))
        grad_bias_ref[0:1, lanes] = jnp.sum(gquery_u.astype(F32), axis=0, keepdims=True)
        grad_bias_ref[1:2, lanes] = jnp.sum(gquery_w, axis=0, keepdims=True)
        gquery = gquery_u.astype(F32) + gquery_w
        grad_att_ref[0, lanes, :] = dot_nn(gquery.T.astype(BF16), own_low).astype(BF16)
        grad_own_ref[...] += dot_nn(gquery.astype(BF16), att_ref[0, lanes, :])
    grad_att_ref[3] = dot_nn(grel_ref[...], table_ref[...]).astype(BF16)
    mine_at = pl.ds(pl.multiple_of(SEG + offset_ref[0], OWN), OWN)
    theirs_at = pl.ds(pl.multiple_of(SEG + OWN - offset_ref[0], OWN), OWN)
    for index in range(2):
        grad_kv_ref[index] = dot_nn(gkv_ref[index, :, 0:SEG].astype(BF16), memory_ref[...])
        kept_ref[index] = gkv_ref[index, :, mine_at]
        sent_ref[index] = gkv_ref[index, :, theirs_at]


def layer_backward(
    offset, grad, hidden, low, memory, att, ff, inner_bias, norms, table, saved
):
    shapes = [
        ((OWN, D), F32),
        ((2, D, OWN), F32),
        ((2, D, OWN), F32),
        ((5, D, D), BF16),
        ((2, D, D), F32),
        ((2, MP, D, 256), BF16),
        ((2, D), F32),
        ((MP, 1, 256), F32),
        ((8, D), F32),
    ]
    return pl.pallas_call(
        backward_kernel,
        out_shape=[jax.ShapeDtypeStruct(s, t) for s, t in shapes],
        in_specs=[SMEM_SPEC] + [VMEM_SPEC] * 17,
        out_specs=[VMEM_SPEC] * len(shapes),
        scratch_shapes=[
            pltpu.VMEM((2, KLEN, 256), BF16),
            pltpu.VMEM((D, KLEN), BF16),
            pltpu.VMEM((2, KLEN, 256), BF16),
            pltpu.VMEM((OWN, D), BF16),
            pltpu.VMEM((D, OWN), BF16),
            pltpu.VMEM((D, OWN), BF16),
            pltpu.VMEM((D, OWN), BF16),
            pltpu.VMEM((OWN, KLEN), F32),
            pltpu.VMEM((OWN, KLEN), BF16),
            pltpu.VMEM((OWN, KLEN), BF16),
            pltpu.VMEM((OWN, KLEN), BF16),
            pltpu.VMEM((2, 2, OWN, 256), F32),
            pltpu.VMEM((2, D, KLEN), F32),
            pltpu.VMEM((D, KLEN), BF16),
        ],
        compiler_params=pltpu.CompilerParams(vmem_limit_bytes=VMEM_LIMIT),
        name="layer_backward",
    )(offset, grad, hidden, low, memory, att, ff, inner_bias, norms, table, *saved)


def finish_kernel(
    grad_own_ref, kept_ref, got_ref, hidden_ref, att_ref, grad_kv_ref, grad_ref, out_ref
):
    own_low = hidden_ref[...].astype(BF16)
    grad = grad_own_ref[...]
    for index in range(2):
        total = (kept_ref[index] + got_ref[index]).astype(BF16)
        out_ref[index] = (grad_kv_ref[index] + dot_nn(total, own_low)).astype(BF16)
        grad = grad + dot_nn(transposed(total).astype(BF16), att_ref[1 + index])
    grad_ref[...] = grad


def layer_finish(grad_own, kept, got, hidden, att, grad_kv):
    return pl.pallas_call(
        finish_kernel,
        out_shape=[
            jax.ShapeDtypeStruct((OWN, D), F32),
            jax.ShapeDtypeStruct((2, D, D), BF16),
        ],
        in_specs=[VMEM_SPEC] * 6,
        out_specs=[VMEM_SPEC] * 2,
        compiler_params=pltpu.CompilerParams(vmem_limit_bytes=VMEM_LIMIT),
        name="layer_finish",
    )(grad_own, kept, got, hidden, att, grad_kv)


def expand(block_rank, block_size):
    return jnp.repeat(jnp.repeat(block_rank, block_size, axis=-2), block_size, axis=-1).astype(F32)


def ring(shift):
    return [(y * 2 + c, ((y + shift) % 4) * 2 + c) for y in range(4) for c in range(2)]


PAIR = [(i, i ^ 1) for i in range(MP)]


def gather_mp(value, place, core):
    here = jnp.stack([value] + [lax.ppermute(value, "mp", ring(s)) for s in (1, 2, 3)])
    there = lax.ppermute(here, "mp", PAIR)
    even = jnp.where(core == 0, here, there)
    odd = jnp.where(core == 0, there, here)
    both = jnp.stack([even, odd], axis=1)
    turned = jnp.concatenate([both[::-1], both[:0:-1]])
    return lax.dynamic_slice_in_dim(turned, 3 - place, 4, 0).reshape((MP,) + value.shape)


def scatter_mp(value, place, core):
    shaped = value.reshape((4, 2) + value.shape[1:])
    mine = lax.dynamic_index_in_dim(shaped, core, 1, False)
    theirs = lax.dynamic_index_in_dim(shaped, 1 - core, 1, False)
    both = mine.astype(F32) + lax.ppermute(theirs, "mp", PAIR).astype(F32)
    total = lax.dynamic_index_in_dim(both, place, 0, False)
    low = both.astype(BF16)
    for s in (1, 2, 3):
        part = lax.dynamic_index_in_dim(low, (place + s) % 4, 0, False)
        total = total + lax.ppermute(part, "mp", ring(s)).astype(F32)
    return total


def body(
    inputs,
    targets,
    valid_mask,
    memory,
    attention_rank,
    feedforward_rank,
    attention_weight,
    attention_moment,
    attention_average,
    feedforward_weight,
    feedforward_moment,
    feedforward_average,
    embedding_weight,
    embedding_moment,
    embedding_average,
    head_bias_weight,
    head_bias_moment,
    head_bias_average,
    inner_bias_weight,
    inner_bias_moment,
    inner_bias_average,
    norm_weight,
    norm_moment,
    norm_average,
):
    layers = attention_weight.shape[0]
    segments = inputs.shape[0]
    device = lax.axis_index("mp")
    place, core = device // 2, device % 2
    start = core * OWN
    valid_count = lax.psum(jnp.sum(valid_mask.astype(F32)), "dp")
    attention_a = expand(attention_rank < 2, D // attention_rank.shape[2])
    attention_b = expand(attention_rank < 3, D // attention_rank.shape[2])
    feedforward_a = expand(feedforward_rank < 2, D // feedforward_rank.shape[2])
    feedforward_b = expand(feedforward_rank < 3, D // feedforward_rank.shape[2])
    attention_eff = (attention_weight * attention_a).astype(BF16).transpose(0, 1, 3, 2)
    feedforward_eff = (feedforward_weight * feedforward_a).astype(BF16)

    att_all = []
    ff_all = []
    for l in range(layers):
        got = gather_mp(attention_eff[l], place, core)
        att_all.append(got.transpose(1, 0, 2, 3).reshape(5, D, D))
        got = gather_mp(feedforward_eff[l], place, core)
        ff_all.append(got.transpose(1, 0, 2, 3))
    bias_pack = jnp.concatenate(
        [head_bias_weight.reshape(layers, 128), inner_bias_weight], axis=1
    )
    bias_got = gather_mp(bias_pack, place, core)
    bias_all = [
        bias_got[:, l, :128].reshape(MP, 2, HD).transpose(1, 0, 2).reshape(2, D)
        for l in range(layers)
    ]
    inner_bias_all = [bias_got[:, l, 128:].reshape(MP, 1, 256) for l in range(layers)]

    table = lax.dynamic_index_in_dim(tables(), core, 0, False)
    vocab_ids = jnp.arange(VOCAB)
    embedding_low = embedding_weight.astype(BF16)
    onehot_all = (inputs.reshape(-1)[:, None] == vocab_ids[None, :]).astype(BF16)
    memory_zero = dot_nn(onehot_all, embedding_low).astype(BF16).reshape(segments, SEG, D)
    tokens = lax.dynamic_index_in_dim(inputs, place, 0, False)
    own_tokens = lax.dynamic_slice_in_dim(tokens, start, OWN, 0)
    own_targets = lax.dynamic_slice_in_dim(
        lax.dynamic_index_in_dim(targets, place, 0, False), start, OWN, 0
    )
    own_valid = lax.dynamic_slice_in_dim(
        lax.dynamic_index_in_dim(valid_mask, place, 0, False), start, OWN, 0
    ).astype(F32)
    onehot_own = (own_tokens[:, None] == vocab_ids[None, :]).astype(F32)
    hidden = jnp.dot(onehot_own, embedding_weight, precision=lax.Precision.HIGHEST)
    low = lax.dynamic_index_in_dim(memory_zero, place, 0, False)
    own_memory = lax.dynamic_index_in_dim(memory, place, 1, False)
    offset = start.reshape(1)

    states = []
    for l in range(layers):
        if l > 0:
            own_low = hidden.astype(BF16)
            other = lax.ppermute(own_low, "mp", PAIR)
            low = jnp.where(
                core == 0,
                jnp.concatenate([own_low, other]),
                jnp.concatenate([other, own_low]),
            )
            memory_one = gather_mp(own_low, place, core).reshape(segments, SEG, D)
        result = layer_forward(
            offset,
            hidden,
            low,
            own_memory[l],
            att_all[l],
            ff_all[l],
            bias_all[l],
            inner_bias_all[l],
            norm_weight[l],
            table,
        )
        states.append((hidden, low, result[1:]))
        hidden = result[0]

    final_low = hidden.astype(BF16)
    logit_scale = D ** (-0.5)
    logits = dot_nt(final_low, embedding_low) * logit_scale
    onehot_out = (own_targets[:, None] == vocab_ids[None, :]).astype(F32)
    peak = jnp.max(logits, axis=-1, keepdims=True)
    log_total = peak + jnp.log(jnp.sum(jnp.exp(logits - peak), axis=-1, keepdims=True))
    picked = jnp.sum(logits * onehot_out, axis=-1)
    ce_total = lax.psum(jnp.sum(own_valid * (log_total[:, 0] - picked)), ("dp", "mp"))
    grad_logits = (
        own_valid[:, None] * (jnp.exp(logits - log_total) - onehot_out) / valid_count
    ).astype(BF16)
    grad_hidden = dot_nn(grad_logits, embedding_low) * logit_scale
    grad_embedding = (
        lax.dot_general(grad_logits, final_low, (((0,), (0,)), ((), ())), preferred_element_type=F32)
        * logit_scale
    )

    grads = [None] * layers
    for l in reversed(range(layers)):
        layer_hidden, layer_low, saved = states[l]
        grad_own, kept, sent, grad_att, grad_kv, *rest = layer_backward(
            offset,
            grad_hidden,
            layer_hidden,
            layer_low,
            own_memory[l],
            att_all[l],
            ff_all[l],
            inner_bias_all[l],
            norm_weight[l],
            table,
            saved,
        )
        got = lax.ppermute(sent, "mp", PAIR)
        grad_hidden, grad_kv = layer_finish(
            grad_own, kept, got, layer_hidden, att_all[l], grad_kv
        )
        grad_att = jnp.concatenate([grad_att[0:1], grad_kv, grad_att[3:5]])
        grads[l] = (grad_att, *rest)
    grad_embedding = grad_embedding + lax.dot_general(
        onehot_own, grad_hidden, (((0,), (0,)), ((), ())), precision=lax.Precision.HIGHEST
    )

    small = jnp.zeros((MP, 48, D), F32)
    small = small.at[:, 0:32].set(grad_embedding.reshape(MP, 32, D))
    small = small.at[:, 32, 0:256].set(
        jnp.stack([g[2].reshape(2, MP, HD).transpose(1, 0, 2) for g in grads], axis=1).reshape(
            MP, 256
        )
    )
    small = small.at[:, 33].set(
        jnp.stack([g[3].reshape(MP, 256) for g in grads], axis=1).reshape(MP, 512)
    )
    small = small.at[:, 34:36].set(
        jnp.concatenate([g[4] for g in grads], axis=0).reshape(MP, 2, D)
    )
    grad_attention = jnp.stack(
        [scatter_mp(g[0].reshape(5, MP, HD, D).transpose(1, 0, 2, 3), place, core) for g in grads]
    )
    grad_feedforward = jnp.stack(
        [scatter_mp(g[1].transpose(1, 0, 2, 3), place, core) for g in grads]
    )
    grad_small = scatter_mp(small.astype(BF16), place, core)
    grad_attention, grad_feedforward, grad_small = lax.psum(
        (grad_attention.astype(BF16), grad_feedforward.astype(BF16), grad_small.astype(BF16)), "dp"
    )
    small_all = gather_mp(grad_small, place, core).astype(F32)
    grad_embedding = small_all[:, 0:32].reshape(VOCAB, D)
    grad_norm = small_all[:, 34:36].reshape(2, 8, D)[:, 0:5]
    grad_small = grad_small.astype(F32)
    grad_head_bias = grad_small[32, 0:256].reshape(layers, 2, HD)
    grad_inner_bias = grad_small[33].reshape(layers, 256)
    grad_attention = grad_attention.astype(F32).transpose(0, 1, 3, 2)
    grad_feedforward = grad_feedforward.astype(F32)

    attention_coef = attention_a + WIDEN * (attention_b - attention_a)
    feedforward_coef = feedforward_a + WIDEN * (feedforward_b - feedforward_a)
    grad_attention = (
        attention_b * grad_attention + 2.0 * PENALTY * attention_weight * attention_coef
    )
    grad_feedforward = (
        feedforward_b * grad_feedforward + 2.0 * PENALTY * feedforward_weight * feedforward_coef
    )
    groups = [
        (attention_weight, attention_moment, attention_average, grad_attention),
        (feedforward_weight, feedforward_moment, feedforward_average, grad_feedforward),
        (head_bias_weight, head_bias_moment, head_bias_average, grad_head_bias),
        (inner_bias_weight, inner_bias_moment, inner_bias_average, grad_inner_bias),
        (embedding_weight, embedding_moment, embedding_average, grad_embedding),
        (norm_weight, norm_moment, norm_average, grad_norm),
    ]
    moments_next = [MOMENTUM * entry[1] + entry[3] for entry in groups]
    directions = [entry[3] + MOMENTUM * moment for entry, moment in zip(groups, moments_next)]
    local_sums = jnp.stack(
        [jnp.sum(entry[0] * entry[0]) for entry in groups[:4]]
        + [jnp.sum(direction * direction) for direction in directions[:4]]
    )
    totals = lax.psum(local_sums, "mp")
    weight_squares = [totals[i] for i in range(4)] + [
        jnp.sum(entry[0] * entry[0]) for entry in groups[4:]
    ]
    direction_squares = [totals[4 + i] for i in range(4)] + [
        jnp.sum(direction * direction) for direction in directions[4:]
    ]
    results = []
    for i in range(6):
        weight, moment, average, grad = groups[i]
        trust_ratio = jnp.sqrt(weight_squares[i]) / jnp.sqrt(direction_squares[i])
        weight_next = weight - RATE * trust_ratio * directions[i]
        results.append(
            (weight_next, moments_next[i], AVERAGE * average + (1.0 - AVERAGE) * weight_next)
        )
    new_memory = jnp.stack([memory_zero, memory_one])
    return (
        ce_total,
        valid_count,
        new_memory,
        grad_attention,
        *results[0],
        grad_feedforward,
        *results[1],
        *results[4],
        *results[2],
        *results[3],
        grad_norm,
        *results[5],
    )


def solution(mesh):
    rows = P("dp", None)
    matrix = P(None, None, None, "mp")
    split_two = P(None, None, "mp")
    split_one = P(None, "mp")
    whole = P()
    return jax.shard_map(
        body,
        mesh=mesh,
        in_specs=(
            (rows,) * 3
            + (P(None, "dp", None, None),)
            + (matrix,) * 8
            + (whole,) * 3
            + (split_two,) * 3
            + (split_one,) * 3
            + (whole,) * 3
        ),
        out_specs=(
            (whole,) * 2
            + (P(None, "dp", None, None),)
            + (matrix,) * 8
            + (whole,) * 3
            + (split_two,) * 3
            + (split_one,) * 3
            + (whole,) * 4
        ),
        check_vma=False,
    )
```

```python
import functools

import jax
import jax.numpy as jnp
import numpy as np
from jax import lax
from jax.experimental import pallas as pl
from jax.experimental.pallas import tpu as pltpu
from jax.sharding import PartitionSpec as P

HD = 64
D = 512
FF = 2048
SEG = 512
KLEN = 1024
OWN = 256
HEADS = 8
VOCAB = 256
MP = 8

EPSILON = 1e-05
MOMENTUM = 0.9
AVERAGE = 0.9
RATE = 0.3
PENALTY = 0.0001
WIDEN = 5.0
F32 = jnp.float32
BF16 = jnp.bfloat16
SCALE = HD ** (-0.5)


def dot_nn(a, b):
    return lax.dot_general(a, b, (((1,), (0,)), ((), ())), preferred_element_type=F32)


def dot_nt(a, b):
    return lax.dot_general(a, b, (((1,), (1,)), ((), ())), preferred_element_type=F32)


def smooth_unit(v):
    return 0.5 * v * (1.0 + jnp.tanh(0.7978845608028654 * (v + 0.044715 * v * v * v)))


def smooth_both(v):
    squared = v * v
    t = jnp.tanh(0.7978845608028654 * (v + 0.044715 * squared * v))
    half = 0.5 * (1.0 + t)
    slope = half + 0.5 * v * (1.0 - t * t) * (
        0.7978845608028654 * (1.0 + 3.0 * 0.044715 * squared)
    )
    return v * half, slope


def tables():
    freq = (1.0 / 10000.0 ** (np.arange(0, D, 2).astype(np.float32) / np.float32(D))).astype(
        np.float32
    )
    turned = []
    for half in range(2):
        distance = (SEG + half * OWN - np.arange(KLEN)) % KLEN
        angle = (distance.astype(np.float32)[:, None] * freq[None, :]).astype(np.float64)
        turned.append(np.concatenate([np.sin(angle), np.cos(angle)], axis=1).astype(np.float32))
    return jnp.asarray(np.stack(turned), BF16)


def norm_forward(values):
    centred = values - jnp.mean(values, axis=-1, keepdims=True)
    inverse = lax.rsqrt(jnp.mean(centred * centred, axis=-1, keepdims=True) + EPSILON)
    return centred * inverse, inverse


def norm_backward(grad, normed, inverse, gain):
    scaled = grad * gain
    grad_in = inverse * (
        scaled
        - jnp.mean(scaled, axis=-1, keepdims=True)
        - normed * jnp.mean(scaled * normed, axis=-1, keepdims=True)
    )
    return (
        grad_in,
        jnp.sum(grad * normed, axis=0, keepdims=True),
        jnp.sum(grad, axis=0, keepdims=True),
    )


def transposed(value):
    return value.astype(F32).T


ROWS = 64
VMEM_SPEC = pl.BlockSpec(memory_space=pltpu.VMEM)
SMEM_SPEC = pl.BlockSpec(memory_space=pltpu.SMEM)
VMEM_LIMIT = 60 * 1024 * 1024


def backward_kernel(
    offset_ref,
    grad_ref,
    hidden_ref,
    low_ref,
    memory_ref,
    att_ref,
    ff_ref,
    inner_bias_ref,
    norm_ref,
    table_ref,
    prob_ref,
    query_u_ref,
    query_w_ref,
    mixed_ref,
    normed_one_ref,
    inverse_one_ref,
    normed_two_ref,
    inverse_two_ref,
    grad_own_ref,
    kept_ref,
    sent_ref,
    grad_att_ref,
    grad_kv_ref,
    grad_ff_ref,
    grad_bias_ref,
    grad_inner_bias_ref,
    grad_norm_ref,
    keys_ref,
    values_ref,
    rel_ref,
    gmix_ref,
    gmix_t_ref,
    query_t_ref,
    flip_t_ref,
    prob_grad_ref,
    score_grad_ref,
    low_prob_ref,
    turned_ref,
    gquery_ref,
    gkv_ref,
    grel_ref,
):
    own_low = hidden_ref[...].astype(BF16)
    gsum_two, ggain_two, goffset_two = norm_backward(
        grad_ref[...], normed_two_ref[...], inverse_two_ref[...], norm_ref[2:3, :]
    )
    middle = normed_one_ref[...] * norm_ref[0:1, :] + norm_ref[1:2, :]
    middle_low = middle.astype(BF16)
    middle_t = transposed(middle_low).astype(BF16)
    gbranch = gsum_two.astype(BF16)
    gbranch_t = transposed(gbranch).astype(BF16)

    def units(m, gmiddle):
        inner = dot_nn(middle_low, ff_ref[0, m]) + inner_bias_ref[m]
        active, slope = smooth_both(inner)
        ginner = (dot_nn(gbranch, ff_ref[1, m]) * slope).astype(BF16)
        grad_ff_ref[0, m] = dot_nn(middle_t, ginner).astype(BF16)
        grad_ff_ref[1, m] = dot_nn(gbranch_t, active.astype(BF16)).astype(BF16)
        grad_inner_bias_ref[m] = jnp.sum(ginner.astype(F32), axis=0, keepdims=True)
        return gmiddle + dot_nt(ginner, ff_ref[0, m])

    gmiddle = lax.fori_loop(0, MP, units, gsum_two)
    gsum_one, ggain_one, goffset_one = norm_backward(
        gmiddle, normed_one_ref[...], inverse_one_ref[...], norm_ref[0:1, :]
    )
    grad_norm_ref[0:1, :] = ggain_one
    grad_norm_ref[1:2, :] = goffset_one
    grad_norm_ref[2:3, :] = ggain_two
    grad_norm_ref[3:4, :] = goffset_two
    grad_norm_ref[4:5, :] = jnp.sum(gsum_two, axis=0, keepdims=True)
    grad_norm_ref[5:8, :] = jnp.zeros((3, D), F32)
    grad_own_ref[...] = gsum_one
    gattended = gsum_one.astype(BF16)
    grad_att_ref[4] = dot_nn(transposed(mixed_ref[...]).astype(BF16), gattended).astype(BF16)
    gmix = dot_nt(gattended, att_ref[4])
    gmix_ref[...] = gmix.astype(BF16)
    gmix_t_ref[...] = gmix.T.astype(BF16)
    query_t_ref[...] = transposed(query_u_ref[...]).astype(BF16)
    flip = (
        lax.broadcasted_iota(jnp.int32, (OWN, OWN), 0)
        + lax.broadcasted_iota(jnp.int32, (OWN, OWN), 1)
        == OWN - 1
    )
    flip = jnp.where(flip, 1.0, 0.0).astype(BF16)
    flip_t_ref[...] = dot_nn(transposed(query_w_ref[...]).astype(BF16), flip).astype(BF16)
    for half, source in ((0, memory_ref), (1, low_ref)):
        rows = source[...]
        cols = slice(half * SEG, (half + 1) * SEG)
        values_ref[:, cols] = dot_nt(att_ref[2], rows).astype(BF16)
        keys = dot_nt(rows, att_ref[1]).astype(BF16)
        keys_ref[0, cols, :] = keys[:, 0:256]
        keys_ref[1, cols, :] = keys[:, 256:512]
    rel = dot_nt(table_ref[...], att_ref[3]).astype(BF16)
    rel_ref[0] = rel[:, 0:256]
    rel_ref[1] = rel[:, 256:512]
    gquery_ref[...] = jnp.zeros_like(gquery_ref)
    lane_head = lax.broadcasted_iota(jnp.int32, (OWN, 256), 1) // HD

    def head(h, carry):
        group = h // 4
        mine = lane_head == h % 4
        lanes = pl.ds(pl.multiple_of(group * 256, 256), 256)
        row = pl.ds(pl.multiple_of(h * HD, HD), HD)
        gmix_h = jnp.where(mine, gmix_ref[:, lanes].astype(F32), 0.0).astype(BF16)
        prob_grad_ref[...] = dot_nn(gmix_h, values_ref[lanes, :])
        for b in range(0, OWN, ROWS):
            rows = slice(b, b + ROWS)
            prob = prob_ref[h, rows, :]
            gprob = prob_grad_ref[rows, :]
            inner = jnp.sum(prob * gprob, axis=-1, keepdims=True)
            score_grad_ref[rows, :] = (prob * (gprob - inner)).astype(BF16)
            low_prob_ref[rows, :] = prob.astype(BF16)
        sgrad = score_grad_ref[...]
        gquery_ref[0, group] = gquery_ref[0, group] + jnp.where(
            mine, dot_nn(sgrad, keys_ref[group]), 0.0
        )
        gkv_ref[0, row, :] = dot_nn(query_t_ref[row, :], sgrad) * SCALE
        gkv_ref[1, row, :] = dot_nn(gmix_t_ref[row, :], low_prob_ref[...])
        flipped = dot_nn(flip, sgrad).astype(BF16)
        turned_ref[...] = pltpu.roll(flipped, KLEN - OWN + 1, 1, stride=1, stride_axis=0)
        gquery_ref[1, group] = gquery_ref[1, group] + jnp.where(
            mine, dot_nn(turned_ref[...], rel_ref[group]), 0.0
        )
        grel_ref[row, :] = (dot_nn(flip_t_ref[row, :], turned_ref[...]) * SCALE).astype(BF16)
        return carry

    lax.fori_loop(0, HEADS, head, 0)
    for group in range(2):
        lanes = slice(group * 256, (group + 1) * 256)
        gquery_u = (gquery_ref[0, group] * SCALE).astype(BF16)
        gquery_w = dot_nn(flip, (gquery_ref[1, group] * SCALE).astype(BF16))
        grad_bias_ref[0:1, lanes] = jnp.sum(gquery_u.astype(F32), axis=0, keepdims=True)
        grad_bias_ref[1:2, lanes] = jnp.sum(gquery_w, axis=0, keepdims=True)
        gquery = gquery_u.astype(F32) + gquery_w
        grad_att_ref[0, lanes, :] = dot_nn(gquery.T.astype(BF16), own_low).astype(BF16)
        grad_own_ref[...] += dot_nn(gquery.astype(BF16), att_ref[0, lanes, :])
    grad_att_ref[3] = dot_nn(grel_ref[...], table_ref[...]).astype(BF16)
    mine_at = pl.ds(pl.multiple_of(SEG + offset_ref[0], OWN), OWN)
    theirs_at = pl.ds(pl.multiple_of(SEG + OWN - offset_ref[0], OWN), OWN)
    for index in range(2):
        grad_kv_ref[index] = dot_nn(gkv_ref[index, :, 0:SEG].astype(BF16), memory_ref[...])
        kept_ref[index] = gkv_ref[index, :, mine_at]
        sent_ref[index, 0:256, :] = gkv_ref[index, 256:512, theirs_at]
        sent_ref[index, 256:512, :] = gkv_ref[index, 0:256, theirs_at]


def layer_backward(
    offset, grad, hidden, low, memory, att, ff, inner_bias, norms, table, saved
):
    shapes = [
        ((OWN, D), F32),
        ((2, D, OWN), F32),
        ((2, D, OWN), F32),
        ((5, D, D), BF16),
        ((2, D, D), F32),
        ((2, MP, D, 256), BF16),
        ((2, D), F32),
        ((MP, 1, 256), F32),
        ((8, D), F32),
    ]
    return pl.pallas_call(
        backward_kernel,
        out_shape=[jax.ShapeDtypeStruct(s, t) for s, t in shapes],
        in_specs=[SMEM_SPEC] + [VMEM_SPEC] * 17,
        out_specs=[VMEM_SPEC] * len(shapes),
        scratch_shapes=[
            pltpu.VMEM((2, KLEN, 256), BF16),
            pltpu.VMEM((D, KLEN), BF16),
            pltpu.VMEM((2, KLEN, 256), BF16),
            pltpu.VMEM((OWN, D), BF16),
            pltpu.VMEM((D, OWN), BF16),
            pltpu.VMEM((D, OWN), BF16),
            pltpu.VMEM((D, OWN), BF16),
            pltpu.VMEM((OWN, KLEN), F32),
            pltpu.VMEM((OWN, KLEN), BF16),
            pltpu.VMEM((OWN, KLEN), BF16),
            pltpu.VMEM((OWN, KLEN), BF16),
            pltpu.VMEM((2, 2, OWN, 256), F32),
            pltpu.VMEM((2, D, KLEN), F32),
            pltpu.VMEM((D, KLEN), BF16),
        ],
        compiler_params=pltpu.CompilerParams(vmem_limit_bytes=VMEM_LIMIT),
        name="layer_backward",
    )(offset, grad, hidden, low, memory, att, ff, inner_bias, norms, table, *saved)


def finish_kernel(
    grad_own_ref, kept_ref, got_ref, hidden_ref, att_ref, grad_kv_ref, grad_ref, out_ref
):
    own_low = hidden_ref[...].astype(BF16)
    grad = grad_own_ref[...]
    for index in range(2):
        total = (kept_ref[index] + got_ref[index]).astype(BF16)
        out_ref[index] = (grad_kv_ref[index] + dot_nn(total, own_low)).astype(BF16)
        grad = grad + dot_nn(transposed(total).astype(BF16), att_ref[1 + index])
    grad_ref[...] = grad


def layer_finish(grad_own, kept, got, hidden, att, grad_kv):
    return pl.pallas_call(
        finish_kernel,
        out_shape=[
            jax.ShapeDtypeStruct((OWN, D), F32),
            jax.ShapeDtypeStruct((2, D, D), BF16),
        ],
        in_specs=[VMEM_SPEC] * 6,
        out_specs=[VMEM_SPEC] * 2,
        compiler_params=pltpu.CompilerParams(vmem_limit_bytes=VMEM_LIMIT),
        name="layer_finish",
    )(grad_own, kept, got, hidden, att, grad_kv)


def expand(block_rank, block_size):
    return jnp.repeat(jnp.repeat(block_rank, block_size, axis=-2), block_size, axis=-1).astype(F32)


PAIR = [(i, i ^ 1) for i in range(MP)]
ANY_SPEC = pl.BlockSpec(memory_space=pl.ANY)
MESH = pl.DeviceIdType.MESH

ATT, FFN, SMALL = 0, 1, 2
GROUPS = (
    (ATT, 0, (("z", 0, 3), ("x", 3, 5)), 16),
    (FFN, 0, (("z", 0, 1), ("x", 1, 2)), 128),
    (ATT, 1, (("z", 0, 2), ("x", 2, 5)), 16),
    (FFN, 1, (("z", 0, 1), ("x", 1, 2)), 128),
)
SMALL_GROUP = (SMALL, 0, (("z", 0, 1),), 16)


class Place:
    def __init__(self):
        dp, mp = lax.axis_index("dp"), lax.axis_index("mp")
        self.x, self.z = dp // 4, dp % 4
        self.y, self.core = mp // 2, mp % 2

    def device(self, x=None, z=None, y=None, core=None):
        x = self.x if x is None else x
        z = self.z if z is None else z
        y = self.y if y is None else y
        core = self.core if core is None else core
        return {"dp": x * 4 + z, "mp": y * 2 + core}

    def along(self, axis, shift):
        return self.device(**{axis: (getattr(self, axis) + shift + 4) % 4})

    def sibling(self):
        return self.device(core=1 - self.core)

    def greet(self):
        partners = [self.along(axis, s) for axis in "xzy" for s in (1, 2, 3)] + [self.sibling()]
        barrier = pltpu.get_barrier_semaphore()
        for partner in partners:
            pl.semaphore_signal(barrier, inc=1, device_id=partner, device_id_type=MESH)
        pl.semaphore_wait(barrier, len(partners))


def send(source, target, sems, index, device):
    copy = pltpu.make_async_remote_copy(
        src_ref=source,
        dst_ref=target,
        send_sem=sems[0].at[index],
        recv_sem=sems[1].at[index],
        device_id=device,
        device_id_type=MESH,
    )
    copy.start()
    return copy


class Weights:
    def __init__(self, here, sources, targets, sems, local_sem):
        self.here, self.sources, self.targets = here, sources, targets
        self.sems, self.local_sem = sems, local_sem
        self.copies = [[None] * len(GROUPS) for _ in range(3)]
        self.local = [None] * len(GROUPS)

    def slice_at(self, axis, rows):
        return pl.ds(pl.multiple_of(getattr(self.here, axis) * rows, rows), rows)

    def one(self, g):
        kind, layer, parts, rows = GROUPS[g]
        source, target = self.sources[kind].at[layer], self.targets[kind].at[layer]
        self.local[g] = pltpu.make_async_copy(source, target.at[:, 0, 0], self.local_sem.at[g])
        self.local[g].start()
        self.copies[0][g] = [
            send(
                source.at[low:high, self.slice_at(axis, rows)],
                target.at[low:high, 0, r, self.slice_at(axis, rows)],
                self.sems[0],
                g * 6 + p * 3 + r - 1,
                self.here.along("y", -r),
            )
            for p, (axis, low, high) in enumerate(parts)
            for r in (1, 2, 3)
        ]

    def two(self, g):
        kind, layer, parts, rows = GROUPS[g]
        target = self.targets[kind].at[layer]
        for copy in self.copies[0][g]:
            copy.wait_recv()
        self.copies[1][g] = []
        for p, (axis, low, high) in enumerate(parts):
            part = target.at[low:high, 0, 1:4, self.slice_at(axis, rows)]
            for s in (1, 2, 3):
                self.copies[1][g].append(
                    send(part, part, self.sems[1], g * 6 + p * 3 + s - 1, self.here.along(axis, s))
                )

    def three(self, g):
        kind, layer, _, _ = GROUPS[g]
        target = self.targets[kind].at[layer]
        for copy in self.copies[1][g]:
            copy.wait_recv()
        self.local[g].wait()
        self.copies[2][g] = [
            send(target.at[:, 0], target.at[:, 1], self.sems[2], g, self.here.sibling())
        ]

    def load(self, g, buffer, sem):
        kind, layer, _, _ = GROUPS[g]
        self.copies[2][g][0].wait_recv()
        copy = pltpu.make_async_copy(self.targets[kind].at[layer], buffer, sem)
        copy.start()
        return copy

    def end(self):
        for stage in self.copies:
            for copies in stage:
                for copy in copies:
                    copy.wait_send()


def forward_step(
    att_ref,
    ff_ref,
    bias_ref,
    count_ref,
    embedding_ref,
    inputs_ref,
    targets_ref,
    valid_ref,
    memory_ref,
    norm_ref,
    table_hbm,
    att_out,
    ff_out,
    new_memory_ref,
    prob_out,
    bias_out,
    count_out,
    hidden_out,
    low_out,
    query_u_out,
    query_w_out,
    mixed_out,
    normed_one_out,
    inverse_one_out,
    normed_two_out,
    inverse_two_out,
    grad_ref,
    grad_embedding_ref,
    ce_ref,
    count_z,
    count_x,
    att_w,
    ff_w,
    memory_w,
    table_ref,
    turned_ref,
    embed_ref,
    keys_ref,
    values_ref,
    rel_ref,
    score_ref,
    prob_ref,
    low_prob_ref,
    part_ref,
    hidden_ref,
    first_send,
    first_recv,
    second_send,
    second_recv,
    third_send,
    third_recv,
    extra_send,
    extra_recv,
    local_sem,
    load_sem,
    prob_sem,
):
    here = Place()
    here.greet()
    extra = (extra_send, extra_recv)
    weights = Weights(
        here,
        (att_ref, ff_ref),
        (att_out, ff_out),
        ((first_send, first_recv), (second_send, second_recv), (third_send, third_recv)),
        local_sem,
    )
    weights.one(0)
    count_z[here.z] = count_ref[...]
    count_copies = [
        send(count_ref, count_z.at[here.z], extra, s - 1, here.along("z", s)) for s in (1, 2, 3)
    ]
    bias_copies = [
        send(bias_ref, bias_out.at[0, r], extra, 2 + r, here.along("y", -r)) for r in (1, 2, 3)
    ]
    bias_out[0, 0] = bias_ref[...]
    for g in (1, 2, 3):
        weights.one(g)
    loads = [
        pltpu.make_async_copy(table_hbm.at[here.core], table_ref, load_sem.at[0]),
        pltpu.make_async_copy(memory_ref.at[0, here.y], memory_w.at[0], load_sem.at[1]),
        pltpu.make_async_copy(memory_ref.at[1, here.y], memory_w.at[1], load_sem.at[2]),
    ]
    for copy in loads:
        copy.start()

    own_rows = pl.ds(pl.multiple_of(here.core * OWN, OWN), OWN)
    turned_ref[...] = jnp.zeros_like(turned_ref)
    turned_ref[0:4, :] = inputs_ref[...].astype(F32)
    turned_ref[8:12, :] = targets_ref[...].astype(F32)
    turned_ref[16:20, :] = valid_ref[...].astype(F32)
    columns = turned_ref[...].T
    turned_ref[:, 0:128] = columns[0:128]
    turned_ref[:, 128:256] = columns[128:256]
    turned_ref[:, 256:384] = columns[256:384]
    turned_ref[:, 384:512] = columns[384:512]
    embedding = embedding_ref[...]
    embedding_low = embedding.astype(BF16)
    vocab_id = lax.broadcasted_iota(jnp.int32, (128, VOCAB), 1).astype(F32)

    def onehot(column):
        return jnp.where(column == vocab_id, 1.0, 0.0)

    for segment in range(4):
        for b in range(4):
            tokens = turned_ref[:, b * 128 + segment : b * 128 + segment + 1]
            embed_ref[segment, b * 128 : (b + 1) * 128, :] = dot_nn(
                onehot(tokens).astype(BF16), embedding_low
            ).astype(BF16)
    memory_zero = pltpu.make_async_copy(embed_ref, new_memory_ref.at[0], load_sem.at[3])
    memory_zero.start()
    weights.two(0)
    low_out[0] = embed_ref[here.y]
    rest_one = embedding - embedding_low.astype(F32)
    middle_part = rest_one.astype(BF16)
    rest_two = (rest_one - middle_part.astype(F32)).astype(BF16)
    lane = lax.broadcasted_iota(jnp.int32, (128, 128), 1)
    own_targets, own_valid = [], []
    for b in range(2):
        block = turned_ref[:, pl.ds(pl.multiple_of(here.core * 256 + b * 128, 128), 128)]

        def column(at):
            return jnp.sum(jnp.where(lane == here.y + at, block, 0.0), axis=1, keepdims=True)

        mine = onehot(column(0)).astype(BF16)
        hidden_ref[b * 128 : (b + 1) * 128, :] = (
            dot_nn(mine, embedding_low) + dot_nn(mine, middle_part)
        ) + dot_nn(mine, rest_two)
        own_targets.append(onehot(column(8)))
        own_valid.append(column(16))
    weights.three(0)
    for copy in bias_copies:
        copy.wait_recv()
    bias_last = send(bias_out.at[0], bias_out.at[1], extra, 6, here.sibling())
    for copy in count_copies:
        copy.wait_recv()
    count_x[here.x] = (count_z[0] + count_z[1]) + (count_z[2] + count_z[3])
    count_last = [
        send(count_x.at[here.x], count_x.at[here.x], extra, 6 + s, here.along("x", s))
        for s in (1, 2, 3)
    ]
    weights.two(1)
    for copy in loads:
        copy.wait()
    bias_last.wait_recv()
    pending = []
    offset = here.core * OWN
    lane_head = lax.broadcasted_iota(jnp.int32, (OWN, 256), 1) // HD

    def project(layer):
        own_low = hidden_ref[...].astype(BF16)
        query = dot_nt(own_low, att_w[layer, 0].reshape(D, D))
        for which, target in ((0, query_u_out), (1, query_w_out)):
            bias = jnp.concatenate(
                [
                    bias_out[cc, r, 3 * layer : 3 * layer + 1, which * HD : (which + 1) * HD]
                    for cc in range(2)
                    for r in range(4)
                ],
                axis=1,
            )
            target[layer] = (query + bias).astype(BF16)
        key_w, value_w = att_w[layer, 1].reshape(D, D), att_w[layer, 2].reshape(D, D)
        for half in range(2):
            rows = memory_w[layer] if half == 0 else low_out[layer]
            cols = slice(half * SEG, (half + 1) * SEG)
            keys_ref[:, cols] = dot_nt(key_w, rows).astype(BF16)
            values = dot_nt(rows, value_w).astype(BF16)
            values_ref[0, cols, :] = values[:, 0:256]
            values_ref[1, cols, :] = values[:, 256:512]
        rel_ref[...] = dot_nt(att_w[layer, 3].reshape(D, D), table_ref[...]).astype(BF16)
        part_ref[...] = jnp.zeros_like(part_ref)

    def head(layer):
        def run(h, carry):
            group = h // 4
            slot = h % 2
            mine = lane_head == h % 4
            lanes = pl.ds(pl.multiple_of(group * 256, 256), 256)
            query_u = jnp.where(mine, query_u_out[layer, :, lanes].astype(F32), 0.0).astype(BF16)
            query_w = jnp.where(mine, query_w_out[layer, :, lanes].astype(F32), 0.0).astype(BF16)
            score_ref[...] = dot_nn(query_w, rel_ref[lanes, :])

            @pl.when(h >= 2)
            def _():
                pltpu.make_async_copy(
                    prob_ref.at[slot], prob_out.at[layer, h], prob_sem.at[slot]
                ).wait()

            prob_ref[slot] = dot_nn(query_u, keys_ref[lanes, :])
            for b in range(0, OWN, ROWS):
                rows = slice(b, b + ROWS)
                moved = pltpu.roll(score_ref[rows, :], b, 1, stride=1, stride_axis=0)
                score = (prob_ref[slot, rows, :] + moved) * SCALE
                key_id = lax.broadcasted_iota(jnp.int32, (ROWS, KLEN), 1)
                query_id = lax.broadcasted_iota(jnp.int32, (ROWS, KLEN), 0) + (offset + b + SEG)
                score = jnp.where(key_id <= query_id, score, -1e30)
                expo = jnp.exp(score - jnp.max(score, axis=-1, keepdims=True))
                prob = expo * (1.0 / jnp.sum(expo, axis=-1, keepdims=True))
                prob_ref[slot, rows, :] = prob
                low_prob_ref[rows, :] = prob.astype(BF16)
            pltpu.make_async_copy(
                prob_ref.at[slot], prob_out.at[layer, h], prob_sem.at[slot]
            ).start()
            mixed = dot_nn(low_prob_ref[...], values_ref[group])
            part_ref[group] = part_ref[group] + jnp.where(mine, mixed, 0.0)
            return carry

        return run

    def attend(layer):
        for slot in range(2):
            pltpu.make_async_copy(
                prob_ref.at[slot], prob_out.at[layer, 6 + slot], prob_sem.at[slot]
            ).wait()
        mixed_out[layer, :, 0:256] = part_ref[0].astype(BF16)
        mixed_out[layer, :, 256:512] = part_ref[1].astype(BF16)
        attended = dot_nn(mixed_out[layer], att_w[layer, 4].reshape(D, D))
        normed_one, inverse_one = norm_forward(hidden_ref[...] + attended)
        normed_one_out[layer] = normed_one
        inverse_one_out[layer] = inverse_one
        return normed_one * norm_ref[layer, 0:1, :] + norm_ref[layer, 1:2, :]

    def feed(layer, middle):
        middle_low = middle.astype(BF16)
        branch = jnp.zeros((OWN, D), F32)
        for cc in range(2):
            for r in range(4):
                bias = jnp.concatenate(
                    [bias_out[cc, r, 3 * layer + 1 + i : 3 * layer + 2 + i, :] for i in range(2)],
                    axis=1,
                )
                inner = dot_nn(middle_low, ff_w[layer, 0, cc, r]) + bias
                branch = branch + dot_nt(smooth_unit(inner).astype(BF16), ff_w[layer, 1, cc, r])
        normed_two, inverse_two = norm_forward(middle + (branch + norm_ref[layer, 4:5, :]))
        normed_two_out[layer] = normed_two
        inverse_two_out[layer] = inverse_two
        hidden_ref[...] = normed_two * norm_ref[layer, 2:3, :] + norm_ref[layer, 3:4, :]

    weights.load(0, att_w.at[0], load_sem.at[4]).wait()
    hidden_out[0] = hidden_ref[...]
    project(0)
    lax.fori_loop(0, 4, head(0), 0)
    weights.three(1)
    weights.two(2)
    lax.fori_loop(4, 8, head(0), 0)
    middle = attend(0)
    weights.three(2)
    weights.two(3)
    weights.load(1, ff_w.at[0], load_sem.at[5]).wait()
    feed(0, middle)
    hidden_out[1] = hidden_ref[...]
    low_out[1, own_rows, :] = hidden_ref[...].astype(BF16)
    own_low = low_out.at[1, own_rows]
    swap = send(own_low, own_low, extra, 10, here.sibling())
    spread_at = new_memory_ref.at[1, here.y, own_rows]
    spread = [send(own_low, spread_at, extra, 10 + s, here.along("y", s)) for s in (1, 2, 3)]
    spread_own = pltpu.make_async_copy(own_low, spread_at, load_sem.at[6])
    spread_own.start()
    attention_one = weights.load(2, att_w.at[1], load_sem.at[7])
    swap.wait_recv()
    attention_one.wait()
    project(1)
    lax.fori_loop(0, 4, head(1), 0)
    weights.three(3)
    for copy in spread:
        copy.wait_recv()
    spread_own.wait()
    spread_all = new_memory_ref.at[1, :, own_rows]
    spread_last = send(spread_all, spread_all, extra, 14, here.sibling())
    lax.fori_loop(4, 8, head(1), 0)
    middle = attend(1)
    weights.load(3, ff_w.at[1], load_sem.at[5]).wait()
    feed(1, middle)
    for copy in count_last:
        copy.wait_recv()
    count_all = (count_x[0] + count_x[1]) + (count_x[2] + count_x[3])
    count_out[...] = count_all

    final_low = hidden_ref[...].astype(BF16)
    logit_scale = D ** (-0.5)
    logits = dot_nt(final_low, embedding_low) * logit_scale
    picked = jnp.concatenate(own_targets, axis=0)
    valid = jnp.concatenate(own_valid, axis=0)
    peak = jnp.max(logits, axis=-1, keepdims=True)
    log_total = peak + jnp.log(jnp.sum(jnp.exp(logits - peak), axis=-1, keepdims=True))
    losses = valid * (log_total - jnp.sum(logits * picked, axis=-1, keepdims=True))
    ce_ref[...] = jnp.broadcast_to(jnp.sum(losses, axis=0, keepdims=True), (8, 128))
    grad_logits = (valid * (jnp.exp(logits - log_total) - picked) / count_all[0:1, 0:1]).astype(
        BF16
    )
    grad_ref[...] = dot_nn(grad_logits, embedding_low) * logit_scale
    grad_embedding_ref[...] = (
        dot_nn(transposed(grad_logits).astype(BF16), final_low) * logit_scale
    )
    memory_zero.wait()
    spread_last.wait()
    for copy in count_copies + bias_copies + [bias_last] + count_last + [swap] + spread:
        copy.wait_send()
    weights.end()


def forward_all(
    att, ff, bias, count, embedding, inputs, targets, valid, memory, norms, table
):
    vmem, hbm = VMEM_SPEC, ANY_SPEC
    outs = [
        (hbm, (2, 5, 2, 4, HD, D), BF16),
        (hbm, (2, 2, 2, 4, D, 256), BF16),
        (hbm, (2, 4, SEG, D), BF16),
        (hbm, (2, HEADS, OWN, KLEN), F32),
        (vmem, (2, 4, 8, 128), F32),
        (vmem, (8, 128), F32),
        (vmem, (2, OWN, D), F32),
        (vmem, (2, SEG, D), BF16),
        (vmem, (2, OWN, D), BF16),
        (vmem, (2, OWN, D), BF16),
        (vmem, (2, OWN, D), BF16),
        (vmem, (2, OWN, D), F32),
        (vmem, (2, OWN, 1), F32),
        (vmem, (2, OWN, D), F32),
        (vmem, (2, OWN, 1), F32),
        (vmem, (OWN, D), F32),
        (vmem, (VOCAB, D), F32),
        (vmem, (8, 128), F32),
    ]
    return pl.pallas_call(
        forward_step,
        out_shape=[jax.ShapeDtypeStruct(s, t) for _, s, t in outs],
        in_specs=[hbm, hbm, vmem, vmem, vmem, vmem, vmem, vmem, hbm, vmem, hbm],
        out_specs=[m for m, _, _ in outs],
        scratch_shapes=[
            pltpu.VMEM((4, 8, 128), F32),
            pltpu.VMEM((4, 8, 128), F32),
            pltpu.VMEM((2, 5, 2, 4, HD, D), BF16),
            pltpu.VMEM((2, 2, 2, 4, D, 256), BF16),
            pltpu.VMEM((2, SEG, D), BF16),
            pltpu.VMEM((KLEN, D), BF16),
            pltpu.VMEM((128, SEG), F32),
            pltpu.VMEM((4, SEG, D), BF16),
            pltpu.VMEM((D, KLEN), BF16),
            pltpu.VMEM((2, KLEN, 256), BF16),
            pltpu.VMEM((D, KLEN), BF16),
            pltpu.VMEM((OWN, KLEN), F32),
            pltpu.VMEM((2, OWN, KLEN), F32),
            pltpu.VMEM((OWN, KLEN), BF16),
            pltpu.VMEM((2, OWN, 256), F32),
            pltpu.VMEM((OWN, D), F32),
            pltpu.SemaphoreType.DMA((24,)),
            pltpu.SemaphoreType.DMA((24,)),
            pltpu.SemaphoreType.DMA((24,)),
            pltpu.SemaphoreType.DMA((24,)),
            pltpu.SemaphoreType.DMA((4,)),
            pltpu.SemaphoreType.DMA((4,)),
            pltpu.SemaphoreType.DMA((15,)),
            pltpu.SemaphoreType.DMA((15,)),
            pltpu.SemaphoreType.DMA((4,)),
            pltpu.SemaphoreType.DMA((8,)),
            pltpu.SemaphoreType.DMA((2,)),
        ],
        compiler_params=pltpu.CompilerParams(
            collective_id=0, has_side_effects=True, vmem_limit_bytes=VMEM_LIMIT
        ),
        name="forward_all",
    )(att, ff, bias, count, embedding, inputs, targets, valid, memory, norms, table)


SHAPES = {ATT: (HD, D), FFN: (D, 256), SMALL: (64, D)}


def reduce_kernel(
    att_ref,
    ff_ref,
    small_ref,
    ce_ref,
    att_out,
    ff_out,
    small_out,
    ce_out,
    *scratch,
):
    here = Place()
    here.greet()
    groups = (GROUPS[2], GROUPS[3], GROUPS[1], GROUPS[0], SMALL_GROUP)
    count = len(groups)
    pair_buffers = scratch[:count]
    position = count
    one_buffers, two_buffers, three_buffers = [], [], []
    for _, _, parts, _ in groups:
        for buffers in (one_buffers, two_buffers, three_buffers):
            buffers.append(scratch[position : position + len(parts)])
            position += len(parts)
    ce_pair, ce_z, ce_y, ce_x, small_own = scratch[position : position + 5]
    sems = [
        (scratch[position + 5 + 2 * i], scratch[position + 6 + 2 * i]) for i in range(5)
    ]
    pair_sems, one_sems, two_sems, three_sems, four_sems = sems
    arrays = (att_ref, ff_ref, small_ref)
    outs = (att_out, ff_out, small_own)
    started = []

    def slice_at(index, rows):
        return pl.ds(pl.multiple_of(index * rows, rows), rows)

    def other(axis):
        return "x" if axis == "z" else "z"

    pair_copies = []
    for g, (kind, layer, parts, rows) in enumerate(groups):
        pair_copies.append(
            send(arrays[kind].at[layer, :, 1], pair_buffers[g], pair_sems, g, here.sibling())
        )
    ce_pair[here.core] = ce_ref[...]
    ce_copy = send(ce_ref, ce_pair.at[here.core], pair_sems, count, here.sibling())
    one_copies = []
    for g, (kind, layer, parts, rows) in enumerate(groups):
        pair_copies[g].wait_recv()
        mats = SHAPES[kind]
        pair = pair_buffers[g]
        for m in range(pair.shape[0]):
            for r in range(4):
                pair[m, r] = (
                    pair[m, r].astype(F32) + arrays[kind][layer, m, 0, r].astype(F32)
                ).astype(BF16)
        copies = []
        for p, (axis, low, high) in enumerate(parts):
            for s in (1, 2, 3):
                goal = (getattr(here, axis) + s) % 4
                copies.append(
                    send(
                        pair.at[low:high, :, slice_at(goal, rows)],
                        one_buffers[g][p].at[s - 1],
                        one_sems,
                        g * 6 + p * 3 + s - 1,
                        here.along(axis, s),
                    )
                )
        one_copies.append(copies)
    ce_copy.wait_recv()
    ce_z[here.z] = ce_pair[0] + ce_pair[1]
    ce_copies = [ce_copy] + [
        send(ce_z.at[here.z], ce_z.at[here.z], one_sems, 6 * count + s - 1, here.along("z", s))
        for s in (1, 2, 3)
    ]
    two_copies = []
    for g, (kind, layer, parts, rows) in enumerate(groups):
        for copy in one_copies[g]:
            copy.wait_recv()
        copies = []
        for p, (axis, low, high) in enumerate(parts):
            got = one_buffers[g][p]
            own = pair_buffers[g].at[low:high, :, slice_at(getattr(here, axis), rows)]
            for m in range(high - low):
                for r in range(4):
                    got[0, m, r] = (
                        (own[m, r].astype(F32) + got[0, m, r].astype(F32))
                        + (got[1, m, r].astype(F32) + got[2, m, r].astype(F32))
                    ).astype(BF16)
            for r in (1, 2, 3):
                copies.append(
                    send(
                        got.at[0, :, r],
                        two_buffers[g][p].at[r - 1],
                        two_sems,
                        g * 6 + p * 3 + r - 1,
                        here.along("y", r),
                    )
                )
        two_copies.append(copies)
    for copy in ce_copies[1:]:
        copy.wait_recv()
    ce_y[here.y] = (ce_z[0] + ce_z[1]) + (ce_z[2] + ce_z[3])
    ce_copies += [
        send(ce_y.at[here.y], ce_y.at[here.y], two_sems, 6 * count + s - 1, here.along("y", s))
        for s in (1, 2, 3)
    ]
    three_copies = []
    for g, (kind, layer, parts, rows) in enumerate(groups):
        for copy in two_copies[g]:
            copy.wait_recv()
        copies = []
        for p, (axis, low, high) in enumerate(parts):
            got, all_four = two_buffers[g][p], three_buffers[g][p]
            index = getattr(here, other(axis))
            for m in range(high - low):
                all_four[index, m] = (
                    (one_buffers[g][p][0, m, 0].astype(F32) + got[0, m].astype(F32))
                    + (got[1, m].astype(F32) + got[2, m].astype(F32))
                ).astype(BF16)
            for s in (1, 2, 3):
                copies.append(
                    send(
                        all_four.at[index],
                        all_four.at[index],
                        three_sems,
                        g * 6 + p * 3 + s - 1,
                        here.along(other(axis), s),
                    )
                )
        three_copies.append(copies)
    for copy in ce_copies[4:]:
        copy.wait_recv()
    ce_x[here.x] = (ce_y[0] + ce_y[1]) + (ce_y[2] + ce_y[3])
    ce_copies += [
        send(ce_x.at[here.x], ce_x.at[here.x], three_sems, 6 * count + s - 1, here.along("x", s))
        for s in (1, 2, 3)
    ]
    four_copies = []
    for g, (kind, layer, parts, rows) in enumerate(groups):
        for copy in three_copies[g]:
            copy.wait_recv()
        copies = []
        for p, (axis, low, high) in enumerate(parts):
            all_four = three_buffers[g][p]
            part = slice_at(getattr(here, axis), rows)
            for m in range(high - low):
                outs[kind][layer, low + m, part] = (
                    (all_four[0, m].astype(F32) + all_four[1, m].astype(F32))
                    + (all_four[2, m].astype(F32) + all_four[3, m].astype(F32))
                ).astype(BF16)
            target = outs[kind].at[layer, low:high, part]
            for s in (1, 2, 3):
                copies.append(
                    send(target, target, four_sems, g * 6 + p * 3 + s - 1, here.along(axis, s))
                )
        four_copies.append(copies)
    for copy in ce_copies[7:]:
        copy.wait_recv()
    ce_out[...] = (ce_x[0] + ce_x[1]) + (ce_x[2] + ce_x[3])
    for copy in four_copies[count - 1]:
        copy.wait_recv()
    small_out[here.y, here.core] = small_own[0, 0]
    piece = small_out.at[here.y, here.core]
    small_copies = [
        send(piece, piece, four_sems, 6 * count + r - 1, here.along("y", r)) for r in (1, 2, 3)
    ]
    for copy in small_copies:
        copy.wait_recv()
    piece = small_out.at[:, here.core]
    last = send(piece, piece, four_sems, 6 * count + 3, here.sibling())
    for copies in four_copies[: count - 1]:
        for copy in copies:
            copy.wait_recv()
    last.wait()
    for copies in [pair_copies, ce_copies, small_copies] + (
        one_copies + two_copies + three_copies + four_copies
    ):
        for copy in copies:
            copy.wait_send()


def reduce_gradients(att, ff, small, ce):
    groups = (GROUPS[2], GROUPS[3], GROUPS[1], GROUPS[0], SMALL_GROUP)
    mats = {ATT: 5, FFN: 2, SMALL: 1}
    scratch = [pltpu.VMEM((mats[k], 4) + SHAPES[k], BF16) for k, _, _, _ in groups]
    for kind, _, parts, rows in groups:
        width = SHAPES[kind][1]
        scratch += [pltpu.VMEM((3, hi - lo, 4, rows, width), BF16) for _, lo, hi in parts]
        scratch += [pltpu.VMEM((3, hi - lo, rows, width), BF16) for _, lo, hi in parts]
        scratch += [pltpu.VMEM((4, hi - lo, rows, width), BF16) for _, lo, hi in parts]
    scratch += [pltpu.VMEM((n, 8, 128), F32) for n in (2, 4, 4, 4)]
    scratch += [pltpu.VMEM((1, 1, 64, D), BF16)]
    for n in (6, 33, 33, 33, 34):
        scratch += [pltpu.SemaphoreType.DMA((n,)), pltpu.SemaphoreType.DMA((n,))]
    return pl.pallas_call(
        reduce_kernel,
        out_shape=[
            jax.ShapeDtypeStruct((2, 5, HD, D), BF16),
            jax.ShapeDtypeStruct((2, 2, D, 256), BF16),
            jax.ShapeDtypeStruct((4, 2, 64, D), BF16),
            jax.ShapeDtypeStruct((8, 128), F32),
        ],
        in_specs=[VMEM_SPEC] * 4,
        out_specs=[VMEM_SPEC] * 4,
        scratch_shapes=scratch,
        compiler_params=pltpu.CompilerParams(
            collective_id=1, has_side_effects=True, vmem_limit_bytes=VMEM_LIMIT
        ),
        name="reduce_gradients",
    )(att, ff, small, ce)


def by_partner(value, place, core):
    turned = lax.dynamic_slice_in_dim(jnp.concatenate([value, value[:3]]), place, 4, 0)
    own = lax.dynamic_index_in_dim(turned, core, 1, False)
    far = lax.dynamic_index_in_dim(turned, 1 - core, 1, False)
    return jnp.stack([own, far])


def body(
    inputs,
    targets,
    valid_mask,
    memory,
    attention_rank,
    feedforward_rank,
    attention_weight,
    attention_moment,
    attention_average,
    feedforward_weight,
    feedforward_moment,
    feedforward_average,
    embedding_weight,
    embedding_moment,
    embedding_average,
    head_bias_weight,
    head_bias_moment,
    head_bias_average,
    inner_bias_weight,
    inner_bias_moment,
    inner_bias_average,
    norm_weight,
    norm_moment,
    norm_average,
):
    layers = attention_weight.shape[0]
    device = lax.axis_index("mp")
    place, core = device // 2, device % 2
    start = core * OWN
    attention_a = expand(attention_rank < 2, D // attention_rank.shape[2])
    attention_b = expand(attention_rank < 3, D // attention_rank.shape[2])
    feedforward_a = expand(feedforward_rank < 2, D // feedforward_rank.shape[2])
    feedforward_b = expand(feedforward_rank < 3, D // feedforward_rank.shape[2])
    attention_eff = (attention_weight * attention_a).astype(BF16).transpose(0, 1, 3, 2)
    feedforward_eff = (feedforward_weight * feedforward_a).astype(BF16)

    bias_pack = jnp.concatenate(
        [
            jnp.concatenate(
                [head_bias_weight.reshape(layers, 1, 128), inner_bias_weight.reshape(layers, 2, 128)],
                axis=1,
            ).reshape(3 * layers, 128),
            jnp.zeros((8 - 3 * layers, 128), F32),
        ]
    )
    local_count = jnp.broadcast_to(jnp.sum(valid_mask.astype(F32)), (8, 128))
    table = tables()
    (
        att_got,
        ff_got,
        new_memory,
        probs,
        bias_got,
        count_got,
        hiddens,
        lows,
        *saved,
        grad_hidden,
        grad_embedding,
        ce_local,
    ) = forward_all(
        attention_eff,
        feedforward_eff,
        bias_pack,
        local_count,
        embedding_weight,
        inputs,
        targets,
        valid_mask,
        memory,
        norm_weight,
        table,
    )
    valid_count = count_got[0, 0]
    att_all = att_got.reshape(layers, 5, D, D)
    ff_all = ff_got.reshape(layers, 2, MP, D, 256)
    bias_got = bias_got.reshape(MP, 8, 128)
    inner_bias_all = [
        bias_got[:, 3 * l + 1 : 3 * l + 3].reshape(MP, 1, 256) for l in range(layers)
    ]
    table = lax.dynamic_index_in_dim(table, core, 0, False)
    vocab_ids = jnp.arange(VOCAB)
    tokens = lax.dynamic_index_in_dim(inputs, place, 0, False)
    own_tokens = lax.dynamic_slice_in_dim(tokens, start, OWN, 0)
    onehot_own = (own_tokens[:, None] == vocab_ids[None, :]).astype(F32)
    own_memory = lax.dynamic_index_in_dim(memory, place, 1, False)
    offset = start.reshape(1)
    states = [
        (hiddens[l], lows[l], [probs[l]] + [value[l] for value in saved]) for l in range(layers)
    ]

    grads = [None] * layers
    for l in reversed(range(layers)):
        layer_hidden, layer_low, saved = states[l]
        grad_own, kept, sent, grad_att, grad_kv, *rest = layer_backward(
            offset,
            grad_hidden,
            layer_hidden,
            layer_low,
            own_memory[l],
            att_all[l],
            ff_all[l],
            inner_bias_all[l],
            norm_weight[l],
            table,
            saved,
        )
        got = lax.ppermute(sent, "mp", PAIR)
        grad_hidden, grad_kv = layer_finish(
            grad_own, kept, got, layer_hidden, att_all[l], grad_kv
        )
        grad_att = jnp.concatenate([grad_att[0:1], grad_kv, grad_att[3:5]])
        grads[l] = (grad_att, *rest)
    grad_embedding = grad_embedding + lax.dot_general(
        onehot_own, grad_hidden, (((0,), (0,)), ((), ())), precision=lax.Precision.HIGHEST
    )

    grad_norm = jnp.concatenate([g[4] for g in grads], axis=0)
    ranked = jnp.concatenate(
        [grad_embedding.reshape(4, 2, 32, D), grad_norm.reshape(4, 2, 2, D)], axis=2
    ).astype(BF16)
    biases = [
        jnp.stack([g[2].reshape(2, MP, HD).transpose(1, 0, 2) for g in grads], axis=1).reshape(
            MP, 1, 256
        ),
        jnp.stack([g[3].reshape(MP, 256) for g in grads], axis=1).reshape(MP, 1, 512),
    ]
    biases = jnp.concatenate([jnp.pad(biases[0], ((0, 0), (0, 0), (0, 256))), biases[1]], axis=1)
    small = jnp.concatenate(
        [
            by_partner(ranked, place, core),
            biases.astype(BF16).reshape(2, 4, 2, D),
            jnp.zeros((2, 4, 28, D), BF16),
        ],
        axis=2,
    )
    grad_attention, grad_feedforward, grad_small, ce_got = reduce_gradients(
        jnp.stack([g[0] for g in grads]).reshape(layers, 5, 2, 4, HD, D),
        jnp.stack([g[1] for g in grads]).reshape(layers, 2, 2, 4, D, 256),
        small.reshape(1, 1, 2, 4, 64, D),
        ce_local,
    )
    ce_total = ce_got[0, 0]
    small_all = grad_small.reshape(MP, 64, D).astype(F32)
    grad_embedding = small_all[:, 0:32].reshape(VOCAB, D)
    grad_norm = small_all[:, 32:34].reshape(2, 8, D)[:, 0:5]
    own_small = lax.dynamic_index_in_dim(small_all, device, 0, False)
    grad_head_bias = own_small[34, 0:256].reshape(layers, 2, HD)
    grad_inner_bias = own_small[35].reshape(layers, 256)
    grad_attention = grad_attention.astype(F32).transpose(0, 1, 3, 2)
    grad_feedforward = grad_feedforward.astype(F32)

    attention_coef = attention_a + WIDEN * (attention_b - attention_a)
    feedforward_coef = feedforward_a + WIDEN * (feedforward_b - feedforward_a)
    grad_attention = (
        attention_b * grad_attention + 2.0 * PENALTY * attention_weight * attention_coef
    )
    grad_feedforward = (
        feedforward_b * grad_feedforward + 2.0 * PENALTY * feedforward_weight * feedforward_coef
    )
    groups = [
        (attention_weight, attention_moment, attention_average, grad_attention),
        (feedforward_weight, feedforward_moment, feedforward_average, grad_feedforward),
        (head_bias_weight, head_bias_moment, head_bias_average, grad_head_bias),
        (inner_bias_weight, inner_bias_moment, inner_bias_average, grad_inner_bias),
        (embedding_weight, embedding_moment, embedding_average, grad_embedding),
        (norm_weight, norm_moment, norm_average, grad_norm),
    ]
    moments_next = [MOMENTUM * entry[1] + entry[3] for entry in groups]
    directions = [entry[3] + MOMENTUM * moment for entry, moment in zip(groups, moments_next)]
    local_sums = jnp.stack(
        [jnp.sum(entry[0] * entry[0]) for entry in groups[:4]]
        + [jnp.sum(direction * direction) for direction in directions[:4]]
    )
    totals = lax.psum(local_sums, "mp")
    weight_squares = [totals[i] for i in range(4)] + [
        jnp.sum(entry[0] * entry[0]) for entry in groups[4:]
    ]
    direction_squares = [totals[4 + i] for i in range(4)] + [
        jnp.sum(direction * direction) for direction in directions[4:]
    ]
    results = []
    for i in range(6):
        weight, moment, average, grad = groups[i]
        trust_ratio = jnp.sqrt(weight_squares[i]) / jnp.sqrt(direction_squares[i])
        weight_next = weight - RATE * trust_ratio * directions[i]
        results.append(
            (weight_next, moments_next[i], AVERAGE * average + (1.0 - AVERAGE) * weight_next)
        )
    return (
        ce_total,
        valid_count,
        new_memory,
        grad_attention,
        *results[0],
        grad_feedforward,
        *results[1],
        *results[4],
        *results[2],
        *results[3],
        grad_norm,
        *results[5],
    )


def solution(mesh):
    rows = P("dp", None)
    matrix = P(None, None, None, "mp")
    split_two = P(None, None, "mp")
    split_one = P(None, "mp")
    whole = P()
    return jax.shard_map(
        body,
        mesh=mesh,
        in_specs=(
            (rows,) * 3
            + (P(None, "dp", None, None),)
            + (matrix,) * 8
            + (whole,) * 3
            + (split_two,) * 3
            + (split_one,) * 3
            + (whole,) * 3
        ),
        out_specs=(
            (whole,) * 2
            + (P(None, "dp", None, None),)
            + (matrix,) * 8
            + (whole,) * 3
            + (split_two,) * 3
            + (split_one,) * 3
            + (whole,) * 4
        ),
        check_vma=False,
    )
```

```python
import functools

import jax
import jax.numpy as jnp
import numpy as np
from jax import lax
from jax.experimental import pallas as pl
from jax.experimental.pallas import tpu as pltpu
from jax.sharding import PartitionSpec as P

HD = 64
D = 512
FF = 2048
SEG = 512
KLEN = 1024
OWN = 256
HEADS = 8
VOCAB = 256
MP = 8

EPSILON = 1e-05
MOMENTUM = 0.9
AVERAGE = 0.9
RATE = 0.3
PENALTY = 0.0001
WIDEN = 5.0
F32 = jnp.float32
BF16 = jnp.bfloat16
SCALE = HD ** (-0.5)


def dot_nn(a, b):
    return lax.dot_general(a, b, (((1,), (0,)), ((), ())), preferred_element_type=F32)


def dot_nt(a, b):
    return lax.dot_general(a, b, (((1,), (1,)), ((), ())), preferred_element_type=F32)


def smooth_unit(v):
    return 0.5 * v * (1.0 + jnp.tanh(0.7978845608028654 * (v + 0.044715 * v * v * v)))


def smooth_both(v):
    squared = v * v
    t = jnp.tanh(0.7978845608028654 * (v + 0.044715 * squared * v))
    half = 0.5 * (1.0 + t)
    slope = half + 0.5 * v * (1.0 - t * t) * (
        0.7978845608028654 * (1.0 + 3.0 * 0.044715 * squared)
    )
    return v * half, slope


def tables():
    freq = (1.0 / 10000.0 ** (np.arange(0, D, 2).astype(np.float32) / np.float32(D))).astype(
        np.float32
    )
    turned = []
    for half in range(2):
        distance = (SEG + half * OWN - np.arange(KLEN)) % KLEN
        angle = (distance.astype(np.float32)[:, None] * freq[None, :]).astype(np.float64)
        turned.append(np.concatenate([np.sin(angle), np.cos(angle)], axis=1).astype(np.float32))
    return jnp.asarray(np.stack(turned), BF16)


def norm_forward(values):
    centred = values - jnp.mean(values, axis=-1, keepdims=True)
    inverse = lax.rsqrt(jnp.mean(centred * centred, axis=-1, keepdims=True) + EPSILON)
    return centred * inverse, inverse


def norm_backward(grad, normed, inverse, gain):
    scaled = grad * gain
    grad_in = inverse * (
        scaled
        - jnp.mean(scaled, axis=-1, keepdims=True)
        - normed * jnp.mean(scaled * normed, axis=-1, keepdims=True)
    )
    return (
        grad_in,
        jnp.sum(grad * normed, axis=0, keepdims=True),
        jnp.sum(grad, axis=0, keepdims=True),
    )


def transposed(value):
    return value.astype(F32).T


ROWS = 64
VMEM_SPEC = pl.BlockSpec(memory_space=pltpu.VMEM)
VMEM_LIMIT = 60 * 1024 * 1024


def expand(block_rank, block_size):
    return jnp.repeat(jnp.repeat(block_rank, block_size, axis=-2), block_size, axis=-1).astype(F32)


ANY_SPEC = pl.BlockSpec(memory_space=pl.ANY)
MESH = pl.DeviceIdType.MESH

ATT, FFN, SMALL = 0, 1, 2
GROUPS = (
    (ATT, 0, (("z", 0, 3), ("x", 3, 5)), 16),
    (FFN, 0, (("z", 0, 1), ("x", 1, 2)), 128),
    (ATT, 1, (("z", 0, 2), ("x", 2, 5)), 16),
    (FFN, 1, (("z", 0, 1), ("x", 1, 2)), 128),
)
SMALL_GROUP = (SMALL, 0, (("z", 0, 1),), 16)


class Place:
    def __init__(self):
        dp, mp = lax.axis_index("dp"), lax.axis_index("mp")
        self.x, self.z = dp // 4, dp % 4
        self.y, self.core = mp // 2, mp % 2

    def device(self, x=None, z=None, y=None, core=None):
        x = self.x if x is None else x
        z = self.z if z is None else z
        y = self.y if y is None else y
        core = self.core if core is None else core
        return {"dp": x * 4 + z, "mp": y * 2 + core}

    def along(self, axis, shift):
        return self.device(**{axis: (getattr(self, axis) + shift + 4) % 4})

    def sibling(self):
        return self.device(core=1 - self.core)

    def greet(self):
        partners = [self.along(axis, s) for axis in "xzy" for s in (1, 2, 3)] + [self.sibling()]
        barrier = pltpu.get_barrier_semaphore()
        for partner in partners:
            pl.semaphore_signal(barrier, inc=1, device_id=partner, device_id_type=MESH)
        pl.semaphore_wait(barrier, len(partners))


def send(source, target, sems, index, device):
    copy = pltpu.make_async_remote_copy(
        src_ref=source,
        dst_ref=target,
        send_sem=sems[0].at[index],
        recv_sem=sems[1].at[index],
        device_id=device,
        device_id_type=MESH,
    )
    copy.start()
    return copy


class Weights:
    def __init__(self, here, sources, targets, sems, local_sem):
        self.here, self.sources, self.targets = here, sources, targets
        self.sems, self.local_sem = sems, local_sem
        self.copies = [[None] * len(GROUPS) for _ in range(3)]
        self.local = [None] * len(GROUPS)

    def slice_at(self, axis, rows):
        return pl.ds(pl.multiple_of(getattr(self.here, axis) * rows, rows), rows)

    def one(self, g):
        kind, layer, parts, rows = GROUPS[g]
        source, target = self.sources[kind].at[layer], self.targets[kind].at[layer]
        self.local[g] = pltpu.make_async_copy(source, target.at[:, 0, 0], self.local_sem.at[g])
        self.local[g].start()
        self.copies[0][g] = [
            send(
                source.at[low:high, self.slice_at(axis, rows)],
                target.at[low:high, 0, r, self.slice_at(axis, rows)],
                self.sems[0],
                g * 6 + p * 3 + r - 1,
                self.here.along("y", -r),
            )
            for p, (axis, low, high) in enumerate(parts)
            for r in (1, 2, 3)
        ]

    def two(self, g):
        kind, layer, parts, rows = GROUPS[g]
        target = self.targets[kind].at[layer]
        for copy in self.copies[0][g]:
            copy.wait_recv()
        self.copies[1][g] = []
        for p, (axis, low, high) in enumerate(parts):
            part = target.at[low:high, 0, 1:4, self.slice_at(axis, rows)]
            for s in (1, 2, 3):
                self.copies[1][g].append(
                    send(part, part, self.sems[1], g * 6 + p * 3 + s - 1, self.here.along(axis, s))
                )

    def three(self, g):
        kind, layer, _, _ = GROUPS[g]
        target = self.targets[kind].at[layer]
        for copy in self.copies[1][g]:
            copy.wait_recv()
        self.local[g].wait()
        self.copies[2][g] = [
            send(target.at[:, 0], target.at[:, 1], self.sems[2], g, self.here.sibling())
        ]

    def load(self, g, buffer, sem):
        kind, layer, _, _ = GROUPS[g]
        self.copies[2][g][0].wait_recv()
        copy = pltpu.make_async_copy(self.targets[kind].at[layer], buffer, sem)
        copy.start()
        return copy

    def end(self):
        for stage in self.copies:
            for copies in stage:
                for copy in copies:
                    copy.wait_send()


def forward_step(
    att_ref,
    ff_ref,
    bias_ref,
    count_ref,
    embedding_ref,
    inputs_ref,
    targets_ref,
    valid_ref,
    memory_ref,
    norm_ref,
    table_hbm,
    att_out,
    ff_out,
    new_memory_ref,
    prob_out,
    bias_out,
    count_out,
    low_out,
    query_u_out,
    query_w_out,
    mixed_out,
    normed_one_out,
    inverse_one_out,
    normed_two_out,
    inverse_two_out,
    grad_ref,
    grad_embedding_ref,
    ce_ref,
    count_z,
    count_x,
    att_w,
    ff_w,
    memory_w,
    table_ref,
    turned_ref,
    embed_ref,
    keys_ref,
    values_ref,
    rel_ref,
    score_ref,
    prob_ref,
    low_prob_ref,
    part_ref,
    hidden_ref,
    first_send,
    first_recv,
    second_send,
    second_recv,
    third_send,
    third_recv,
    extra_send,
    extra_recv,
    local_sem,
    load_sem,
    prob_sem,
):
    here = Place()
    here.greet()
    extra = (extra_send, extra_recv)
    weights = Weights(
        here,
        (att_ref, ff_ref),
        (att_out, ff_out),
        ((first_send, first_recv), (second_send, second_recv), (third_send, third_recv)),
        local_sem,
    )
    weights.one(0)
    count_z[here.z] = count_ref[...]
    count_copies = [
        send(count_ref, count_z.at[here.z], extra, s - 1, here.along("z", s)) for s in (1, 2, 3)
    ]
    bias_copies = [
        send(bias_ref, bias_out.at[0, r], extra, 2 + r, here.along("y", -r)) for r in (1, 2, 3)
    ]
    bias_out[0, 0] = bias_ref[...]
    for g in (1, 2, 3):
        weights.one(g)
    loads = [
        pltpu.make_async_copy(table_hbm.at[here.core], table_ref, load_sem.at[0]),
        pltpu.make_async_copy(memory_ref.at[0, here.y], memory_w.at[0], load_sem.at[1]),
        pltpu.make_async_copy(memory_ref.at[1, here.y], memory_w.at[1], load_sem.at[2]),
    ]
    for copy in loads:
        copy.start()

    own_rows = pl.ds(pl.multiple_of(here.core * OWN, OWN), OWN)
    turned_ref[...] = jnp.zeros_like(turned_ref)
    turned_ref[0:4, :] = inputs_ref[...].astype(F32)
    turned_ref[8:12, :] = targets_ref[...].astype(F32)
    turned_ref[16:20, :] = valid_ref[...].astype(F32)
    columns = turned_ref[...].T
    turned_ref[:, 0:128] = columns[0:128]
    turned_ref[:, 128:256] = columns[128:256]
    turned_ref[:, 256:384] = columns[256:384]
    turned_ref[:, 384:512] = columns[384:512]
    embedding = embedding_ref[...]
    embedding_low = embedding.astype(BF16)
    vocab_id = lax.broadcasted_iota(jnp.int32, (128, VOCAB), 1).astype(F32)

    def onehot(column):
        return jnp.where(column == vocab_id, 1.0, 0.0)

    for segment in range(4):
        for b in range(4):
            tokens = turned_ref[:, b * 128 + segment : b * 128 + segment + 1]
            embed_ref[segment, b * 128 : (b + 1) * 128, :] = dot_nn(
                onehot(tokens).astype(BF16), embedding_low
            ).astype(BF16)
    memory_zero = pltpu.make_async_copy(embed_ref, new_memory_ref.at[0], load_sem.at[3])
    memory_zero.start()
    weights.two(0)
    low_out[0] = embed_ref[here.y]
    rest_one = embedding - embedding_low.astype(F32)
    middle_part = rest_one.astype(BF16)
    rest_two = (rest_one - middle_part.astype(F32)).astype(BF16)
    lane = lax.broadcasted_iota(jnp.int32, (128, 128), 1)
    own_targets, own_valid = [], []
    for b in range(2):
        block = turned_ref[:, pl.ds(pl.multiple_of(here.core * 256 + b * 128, 128), 128)]

        def column(at):
            return jnp.sum(jnp.where(lane == here.y + at, block, 0.0), axis=1, keepdims=True)

        mine = onehot(column(0)).astype(BF16)
        hidden_ref[b * 128 : (b + 1) * 128, :] = (
            dot_nn(mine, embedding_low) + dot_nn(mine, middle_part)
        ) + dot_nn(mine, rest_two)
        own_targets.append(onehot(column(8)))
        own_valid.append(column(16))
    weights.three(0)
    for copy in bias_copies:
        copy.wait_recv()
    bias_last = send(bias_out.at[0], bias_out.at[1], extra, 6, here.sibling())
    for copy in count_copies:
        copy.wait_recv()
    count_x[here.x] = (count_z[0] + count_z[1]) + (count_z[2] + count_z[3])
    count_last = [
        send(count_x.at[here.x], count_x.at[here.x], extra, 6 + s, here.along("x", s))
        for s in (1, 2, 3)
    ]
    weights.two(1)
    for copy in loads:
        copy.wait()
    bias_last.wait_recv()
    pending = []
    offset = here.core * OWN
    lane_head = lax.broadcasted_iota(jnp.int32, (OWN, 256), 1) // HD

    def project(layer):
        own_low = hidden_ref[...].astype(BF16)
        query = dot_nt(own_low, att_w[layer, 0].reshape(D, D))
        for which, target in ((0, query_u_out), (1, query_w_out)):
            bias = jnp.concatenate(
                [
                    bias_out[cc, r, 3 * layer : 3 * layer + 1, which * HD : (which + 1) * HD]
                    for cc in range(2)
                    for r in range(4)
                ],
                axis=1,
            )
            target[layer] = (query + bias).astype(BF16)
        key_w, value_w = att_w[layer, 1].reshape(D, D), att_w[layer, 2].reshape(D, D)
        for half in range(2):
            rows = memory_w[layer] if half == 0 else low_out[layer]
            cols = slice(half * SEG, (half + 1) * SEG)
            keys_ref[:, cols] = dot_nt(key_w, rows).astype(BF16)
            values = dot_nt(rows, value_w).astype(BF16)
            values_ref[0, cols, :] = values[:, 0:256]
            values_ref[1, cols, :] = values[:, 256:512]
        rel_ref[...] = dot_nt(att_w[layer, 3].reshape(D, D), table_ref[...]).astype(BF16)
        part_ref[...] = jnp.zeros_like(part_ref)

    def head(layer):
        def run(h, carry):
            group = h // 4
            slot = h % 2
            mine = lane_head == h % 4
            lanes = pl.ds(pl.multiple_of(group * 256, 256), 256)
            query_u = jnp.where(mine, query_u_out[layer, :, lanes].astype(F32), 0.0).astype(BF16)
            query_w = jnp.where(mine, query_w_out[layer, :, lanes].astype(F32), 0.0).astype(BF16)
            score_ref[...] = dot_nn(query_w, rel_ref[lanes, :])

            @pl.when(h >= 2)
            def _():
                pltpu.make_async_copy(
                    prob_ref.at[slot], prob_out.at[layer, h], prob_sem.at[slot]
                ).wait()

            prob_ref[slot] = dot_nn(query_u, keys_ref[lanes, :])
            for b in range(0, OWN, ROWS):
                rows = slice(b, b + ROWS)
                moved = pltpu.roll(score_ref[rows, :], b, 1, stride=1, stride_axis=0)
                score = (prob_ref[slot, rows, :] + moved) * SCALE
                key_id = lax.broadcasted_iota(jnp.int32, (ROWS, KLEN), 1)
                query_id = lax.broadcasted_iota(jnp.int32, (ROWS, KLEN), 0) + (offset + b + SEG)
                score = jnp.where(key_id <= query_id, score, -1e30)
                expo = jnp.exp(score - jnp.max(score, axis=-1, keepdims=True))
                prob = expo * (1.0 / jnp.sum(expo, axis=-1, keepdims=True))
                prob_ref[slot, rows, :] = prob
                low_prob_ref[rows, :] = prob.astype(BF16)
            pltpu.make_async_copy(
                prob_ref.at[slot], prob_out.at[layer, h], prob_sem.at[slot]
            ).start()
            mixed = dot_nn(low_prob_ref[...], values_ref[group])
            part_ref[group] = part_ref[group] + jnp.where(mine, mixed, 0.0)
            return carry

        return run

    def attend(layer):
        for slot in range(2):
            pltpu.make_async_copy(
                prob_ref.at[slot], prob_out.at[layer, 6 + slot], prob_sem.at[slot]
            ).wait()
        mixed_out[layer, :, 0:256] = part_ref[0].astype(BF16)
        mixed_out[layer, :, 256:512] = part_ref[1].astype(BF16)
        attended = dot_nn(mixed_out[layer], att_w[layer, 4].reshape(D, D))
        normed_one, inverse_one = norm_forward(hidden_ref[...] + attended)
        normed_one_out[layer] = normed_one
        inverse_one_out[layer] = inverse_one
        return normed_one * norm_ref[layer, 0:1, :] + norm_ref[layer, 1:2, :]

    def feed(layer, middle):
        middle_low = middle.astype(BF16)
        branch = jnp.zeros((OWN, D), F32)
        for cc in range(2):
            for r in range(4):
                bias = jnp.concatenate(
                    [bias_out[cc, r, 3 * layer + 1 + i : 3 * layer + 2 + i, :] for i in range(2)],
                    axis=1,
                )
                inner = dot_nn(middle_low, ff_w[layer, 0, cc, r]) + bias
                branch = branch + dot_nt(smooth_unit(inner).astype(BF16), ff_w[layer, 1, cc, r])
        normed_two, inverse_two = norm_forward(middle + (branch + norm_ref[layer, 4:5, :]))
        normed_two_out[layer] = normed_two
        inverse_two_out[layer] = inverse_two
        hidden_ref[...] = normed_two * norm_ref[layer, 2:3, :] + norm_ref[layer, 3:4, :]

    weights.load(0, att_w.at[0], load_sem.at[4]).wait()
    project(0)
    lax.fori_loop(0, 4, head(0), 0)
    weights.three(1)
    weights.two(2)
    lax.fori_loop(4, 8, head(0), 0)
    middle = attend(0)
    weights.three(2)
    weights.two(3)
    weights.load(1, ff_w.at[0], load_sem.at[5]).wait()
    feed(0, middle)
    low_out[1, own_rows, :] = hidden_ref[...].astype(BF16)
    own_low = low_out.at[1, own_rows]
    swap = send(own_low, own_low, extra, 10, here.sibling())
    spread_at = new_memory_ref.at[1, here.y, own_rows]
    spread = [send(own_low, spread_at, extra, 10 + s, here.along("y", s)) for s in (1, 2, 3)]
    spread_own = pltpu.make_async_copy(own_low, spread_at, load_sem.at[6])
    spread_own.start()
    attention_one = weights.load(2, att_w.at[1], load_sem.at[7])
    swap.wait_recv()
    attention_one.wait()
    project(1)
    lax.fori_loop(0, 4, head(1), 0)
    weights.three(3)
    for copy in spread:
        copy.wait_recv()
    spread_own.wait()
    spread_all = new_memory_ref.at[1, :, own_rows]
    spread_last = send(spread_all, spread_all, extra, 14, here.sibling())
    lax.fori_loop(4, 8, head(1), 0)
    middle = attend(1)
    weights.load(3, ff_w.at[1], load_sem.at[5]).wait()
    feed(1, middle)
    for copy in count_last:
        copy.wait_recv()
    count_all = (count_x[0] + count_x[1]) + (count_x[2] + count_x[3])
    count_out[...] = count_all

    final_low = hidden_ref[...].astype(BF16)
    logit_scale = D ** (-0.5)
    logits = dot_nt(final_low, embedding_low) * logit_scale
    picked = jnp.concatenate(own_targets, axis=0)
    valid = jnp.concatenate(own_valid, axis=0)
    peak = jnp.max(logits, axis=-1, keepdims=True)
    log_total = peak + jnp.log(jnp.sum(jnp.exp(logits - peak), axis=-1, keepdims=True))
    losses = valid * (log_total - jnp.sum(logits * picked, axis=-1, keepdims=True))
    ce_ref[...] = jnp.broadcast_to(jnp.sum(losses, axis=0, keepdims=True), (8, 128))
    grad_logits = (valid * (jnp.exp(logits - log_total) - picked) / count_all[0:1, 0:1]).astype(
        BF16
    )
    grad_ref[...] = dot_nn(grad_logits, embedding_low) * logit_scale
    grad_embedding_ref[...] = (
        dot_nn(transposed(grad_logits).astype(BF16), final_low) * logit_scale
    ).reshape(MP, 32, D)
    memory_zero.wait()
    spread_last.wait()
    for copy in count_copies + bias_copies + [bias_last] + count_last + [swap] + spread:
        copy.wait_send()
    weights.end()


def forward_all(
    att, ff, bias, count, embedding, inputs, targets, valid, memory, norms, table
):
    vmem, hbm = VMEM_SPEC, ANY_SPEC
    outs = [
        (hbm, (2, 5, 2, 4, HD, D), BF16),
        (hbm, (2, 2, 2, 4, D, 256), BF16),
        (hbm, (2, 4, SEG, D), BF16),
        (hbm, (2, HEADS, OWN, KLEN), F32),
        (vmem, (2, 4, 8, 128), F32),
        (vmem, (8, 128), F32),
        (vmem, (2, SEG, D), BF16),
        (vmem, (2, OWN, D), BF16),
        (vmem, (2, OWN, D), BF16),
        (vmem, (2, OWN, D), BF16),
        (vmem, (2, OWN, D), F32),
        (vmem, (2, OWN, 1), F32),
        (vmem, (2, OWN, D), F32),
        (vmem, (2, OWN, 1), F32),
        (vmem, (OWN, D), F32),
        (vmem, (MP, 32, D), F32),
        (vmem, (8, 128), F32),
    ]
    return pl.pallas_call(
        forward_step,
        out_shape=[jax.ShapeDtypeStruct(s, t) for _, s, t in outs],
        in_specs=[hbm, hbm, vmem, vmem, vmem, vmem, vmem, vmem, hbm, vmem, hbm],
        out_specs=[m for m, _, _ in outs],
        scratch_shapes=[
            pltpu.VMEM((4, 8, 128), F32),
            pltpu.VMEM((4, 8, 128), F32),
            pltpu.VMEM((2, 5, 2, 4, HD, D), BF16),
            pltpu.VMEM((2, 2, 2, 4, D, 256), BF16),
            pltpu.VMEM((2, SEG, D), BF16),
            pltpu.VMEM((KLEN, D), BF16),
            pltpu.VMEM((128, SEG), F32),
            pltpu.VMEM((4, SEG, D), BF16),
            pltpu.VMEM((D, KLEN), BF16),
            pltpu.VMEM((2, KLEN, 256), BF16),
            pltpu.VMEM((D, KLEN), BF16),
            pltpu.VMEM((OWN, KLEN), F32),
            pltpu.VMEM((2, OWN, KLEN), F32),
            pltpu.VMEM((OWN, KLEN), BF16),
            pltpu.VMEM((2, OWN, 256), F32),
            pltpu.VMEM((OWN, D), F32),
            pltpu.SemaphoreType.DMA((24,)),
            pltpu.SemaphoreType.DMA((24,)),
            pltpu.SemaphoreType.DMA((24,)),
            pltpu.SemaphoreType.DMA((24,)),
            pltpu.SemaphoreType.DMA((4,)),
            pltpu.SemaphoreType.DMA((4,)),
            pltpu.SemaphoreType.DMA((15,)),
            pltpu.SemaphoreType.DMA((15,)),
            pltpu.SemaphoreType.DMA((4,)),
            pltpu.SemaphoreType.DMA((8,)),
            pltpu.SemaphoreType.DMA((2,)),
        ],
        compiler_params=pltpu.CompilerParams(
            collective_id=0, has_side_effects=True, vmem_limit_bytes=VMEM_LIMIT
        ),
        name="forward_all",
    )(att, ff, bias, count, embedding, inputs, targets, valid, memory, norms, table)


SHAPES = {ATT: (HD, D), FFN: (D, 256), SMALL: (64, D)}


ORDER = (3, 2, 1, 0)


class Sums:
    def __init__(self, here, arrays, outs, buffers, sems):
        self.here, self.arrays, self.outs = here, arrays, outs
        self.pairs, self.ones, self.twos, self.threes = buffers
        self.sems = sems
        self.copies = [[[] for _ in range(5)] for _ in range(5)]

    def group(self, g):
        return SMALL_GROUP if g == 4 else GROUPS[g]

    def slice_at(self, index, rows):
        return pl.ds(pl.multiple_of(index * rows, rows), rows)

    def arrived(self, stage, g):
        for copy in self.copies[stage][g]:
            copy.wait_recv()

    def pair(self, g):
        kind, layer, _, _ = self.group(g)
        self.copies[0][g].append(
            send(
                self.arrays[kind].at[layer, :, 1],
                self.pairs[g],
                self.sems[0],
                g,
                self.here.sibling(),
            )
        )

    def one(self, g):
        kind, layer, parts, rows = self.group(g)
        self.arrived(0, g)
        pair = self.pairs[g]
        for m in range(pair.shape[0]):
            for r in range(4):
                pair[m, r] = (
                    pair[m, r].astype(F32) + self.arrays[kind][layer, m, 0, r].astype(F32)
                ).astype(BF16)
        for p, (axis, low, high) in enumerate(parts):
            for s in (1, 2, 3):
                goal = (getattr(self.here, axis) + s) % 4
                self.copies[1][g].append(
                    send(
                        pair.at[low:high, :, self.slice_at(goal, rows)],
                        self.ones[g][p].at[s - 1],
                        self.sems[1],
                        g * 6 + p * 3 + s - 1,
                        self.here.along(axis, s),
                    )
                )

    def two(self, g):
        kind, layer, parts, rows = self.group(g)
        self.arrived(1, g)
        for p, (axis, low, high) in enumerate(parts):
            got = self.ones[g][p]
            own = self.pairs[g].at[low:high, :, self.slice_at(getattr(self.here, axis), rows)]
            for m in range(high - low):
                for r in range(4):
                    got[0, m, r] = (
                        (own[m, r].astype(F32) + got[0, m, r].astype(F32))
                        + (got[1, m, r].astype(F32) + got[2, m, r].astype(F32))
                    ).astype(BF16)
            for r in (1, 2, 3):
                self.copies[2][g].append(
                    send(
                        got.at[0, :, r],
                        self.twos[g][p].at[r - 1],
                        self.sems[2],
                        g * 6 + p * 3 + r - 1,
                        self.here.along("y", r),
                    )
                )

    def three(self, g):
        kind, layer, parts, rows = self.group(g)
        self.arrived(2, g)
        for p, (axis, low, high) in enumerate(parts):
            other = "x" if axis == "z" else "z"
            got, every = self.twos[g][p], self.threes[g][p]
            index = getattr(self.here, other)
            for m in range(high - low):
                every[index, m] = (
                    (self.ones[g][p][0, m, 0].astype(F32) + got[0, m].astype(F32))
                    + (got[1, m].astype(F32) + got[2, m].astype(F32))
                ).astype(BF16)
            for s in (1, 2, 3):
                self.copies[3][g].append(
                    send(
                        every.at[index],
                        every.at[index],
                        self.sems[3],
                        g * 6 + p * 3 + s - 1,
                        self.here.along(other, s),
                    )
                )

    def four(self, g):
        kind, layer, parts, rows = self.group(g)
        self.arrived(3, g)
        for p, (axis, low, high) in enumerate(parts):
            every = self.threes[g][p]
            part = self.slice_at(getattr(self.here, axis), rows)
            for m in range(high - low):
                self.outs[kind][layer, low + m, part] = (
                    (every[0, m].astype(F32) + every[1, m].astype(F32))
                    + (every[2, m].astype(F32) + every[3, m].astype(F32))
                ).astype(BF16)
            target = self.outs[kind].at[layer, low:high, part]
            for s in (1, 2, 3):
                self.copies[4][g].append(
                    send(
                        target,
                        target,
                        self.sems[4],
                        g * 6 + p * 3 + s - 1,
                        self.here.along(axis, s),
                    )
                )

    def end(self):
        for stage in self.copies:
            for copies in stage:
                for copy in copies:
                    copy.wait_send()


def backward_step(
    att_hbm,
    ff_hbm,
    prob_hbm,
    memory_hbm,
    table_hbm,
    grad_hbm,
    grad_embedding_hbm,
    bias_ref,
    norm_ref,
    inputs_ref,
    ce_ref,
    low_ref,
    query_u_ref,
    query_w_ref,
    mixed_ref,
    normed_one_ref,
    inverse_one_ref,
    normed_two_ref,
    inverse_two_ref,
    att_out,
    ff_out,
    small_out,
    ce_out,
    att_w,
    ff_w,
    memory_w,
    table_ref,
    prob_ref,
    grad_att_ref,
    grad_ff_ref,
    grad_small_ref,
    grad_ref,
    keys_ref,
    values_ref,
    rel_ref,
    gmix_ref,
    gmix_t_ref,
    query_t_ref,
    flip_t_ref,
    prob_grad_ref,
    score_grad_ref,
    low_prob_ref,
    flipped_ref,
    gquery_ref,
    gmemory_ref,
    ghidden_ref,
    got_ref,
    grel_ref,
    grad_bias_ref,
    grad_inner_ref,
    grad_norm_ref,
    ranked_ref,
    block_ref,
    ce_pair,
    ce_z,
    ce_y,
    ce_x,
    small_own,
    *scratch,
):
    here = Place()
    scratch = list(scratch)
    pairs = [scratch.pop(0) for _ in range(5)]
    ones, twos, threes = [], [], []
    for g in range(5):
        parts = (SMALL_GROUP if g == 4 else GROUPS[g])[2]
        for buffers in (ones, twos, threes):
            buffers.append([scratch.pop(0) for _ in parts])
    sems = [(scratch.pop(0), scratch.pop(0)) for _ in range(6)]
    load_sem, prob_sem = scratch
    extra = sems[5]
    sums = Sums(
        here,
        (grad_att_ref, grad_ff_ref, grad_small_ref),
        (att_out, ff_out, small_own),
        (pairs, ones, twos, threes),
        sems,
    )
    load_ff = pltpu.make_async_copy(ff_hbm.at[1], ff_w, load_sem.at[0])
    load_att = pltpu.make_async_copy(att_hbm.at[1], att_w, load_sem.at[1])
    loads = [
        pltpu.make_async_copy(memory_hbm.at[0, here.y], memory_w.at[0], load_sem.at[2]),
        pltpu.make_async_copy(memory_hbm.at[1, here.y], memory_w.at[1], load_sem.at[3]),
        pltpu.make_async_copy(table_hbm.at[here.core], table_ref, load_sem.at[4]),
        pltpu.make_async_copy(grad_embedding_hbm, ranked_ref, load_sem.at[5]),
    ]
    load_grad = pltpu.make_async_copy(grad_hbm, grad_ref, load_sem.at[6])
    load_grad.start()
    load_ff.start()
    load_att.start()
    for copy in loads:
        copy.start()
    here.greet()
    own_rows = pl.ds(pl.multiple_of(here.core * OWN, OWN), OWN)
    their_rows = pl.ds(pl.multiple_of(OWN - here.core * OWN, OWN), OWN)
    ce_pair[here.core] = ce_ref[...]
    ce_copies = [send(ce_ref, ce_pair.at[here.core], extra, 0, here.sibling())]
    flip = (
        lax.broadcasted_iota(jnp.int32, (OWN, OWN), 0)
        + lax.broadcasted_iota(jnp.int32, (OWN, OWN), 1)
        == OWN - 1
    )
    flip = jnp.where(flip, 1.0, 0.0).astype(BF16)
    lane_head = lax.broadcasted_iota(jnp.int32, (OWN, 256), 1) // HD
    load_grad.wait()

    def spread_ce(step):
        source, target, axis, base = (
            (ce_pair, ce_z, "z", 1),
            (ce_z, ce_y, "y", 4),
            (ce_y, ce_x, "x", 7),
        )[step]
        for copy in ce_copies[-1:] if step == 0 else ce_copies[-3:]:
            copy.wait_recv()
        total = source[0] + source[1]
        if step:
            total = total + (source[2] + source[3])
        index = getattr(here, axis)
        target[index] = total
        for s in (1, 2, 3):
            ce_copies.append(
                send(target.at[index], target.at[index], extra, base + s - 1, here.along(axis, s))
            )

    def feed(layer):
        gsum, ggain, goffset = norm_backward(
            grad_ref[...], normed_two_ref[layer], inverse_two_ref[layer], norm_ref[layer, 2:3, :]
        )
        middle = normed_one_ref[layer] * norm_ref[layer, 0:1, :] + norm_ref[layer, 1:2, :]
        middle_low = middle.astype(BF16)
        middle_t = transposed(middle_low).astype(BF16)
        gbranch = gsum.astype(BF16)
        gbranch_t = transposed(gbranch).astype(BF16)
        gmiddle = gsum
        load_ff.wait()
        for cc in range(2):
            for r in range(4):
                bias = jnp.concatenate(
                    [bias_ref[cc, r, 3 * layer + 1 + i : 3 * layer + 2 + i, :] for i in range(2)],
                    axis=1,
                )
                inner = dot_nn(middle_low, ff_w[0, cc, r]) + bias
                active, slope = smooth_both(inner)
                ginner = (dot_nn(gbranch, ff_w[1, cc, r]) * slope).astype(BF16)
                grad_ff_ref[layer, 0, cc, r] = dot_nn(middle_t, ginner).astype(BF16)
                grad_ff_ref[layer, 1, cc, r] = dot_nn(gbranch_t, active.astype(BF16)).astype(BF16)
                grad_inner_ref[layer, cc, r] = jnp.sum(
                    ginner.astype(F32), axis=0, keepdims=True
                )
                gmiddle = gmiddle + dot_nt(ginner, ff_w[0, cc, r])
        rows = [jnp.sum(gsum, axis=0, keepdims=True)]
        gsum, ggain_one, goffset_one = norm_backward(
            gmiddle, normed_one_ref[layer], inverse_one_ref[layer], norm_ref[layer, 0:1, :]
        )
        rows = [ggain_one, goffset_one, ggain, goffset] + rows
        for i, row in enumerate(rows):
            at = 8 * layer + i
            grad_norm_ref[at // 2, at % 2 : at % 2 + 1, :] = row
        grad_ref[...] = gsum

    def prepare(layer):
        gattended = grad_ref[...].astype(BF16)
        wide = dot_nn(transposed(mixed_ref[layer]).astype(BF16), gattended).astype(BF16)
        grad_att_ref[layer, 4] = wide.reshape(2, 4, HD, D)
        load_att.wait()
        gmix = dot_nt(gattended, att_w[4].reshape(D, D))
        gmix_ref[...] = gmix.astype(BF16)
        gmix_t_ref[...] = gmix.T.astype(BF16)
        query_t_ref[...] = transposed(query_u_ref[layer]).astype(BF16)
        flip_t_ref[...] = dot_nn(transposed(query_w_ref[layer]).astype(BF16), flip).astype(BF16)
        key_w, value_w = att_w[1].reshape(D, D), att_w[2].reshape(D, D)
        for half in range(2):
            rows = memory_w[layer] if half == 0 else low_ref[layer]
            cols = slice(half * SEG, (half + 1) * SEG)
            values_ref[:, cols] = dot_nt(value_w, rows).astype(BF16)
            keys = dot_nt(rows, key_w).astype(BF16)
            keys_ref[0, cols, :] = keys[:, 0:256]
            keys_ref[1, cols, :] = keys[:, 256:512]
        rel = dot_nt(table_ref[...], att_w[3].reshape(D, D)).astype(BF16)
        rel_ref[0] = rel[:, 0:256]
        rel_ref[1] = rel[:, 256:512]
        gquery_ref[...] = jnp.zeros_like(gquery_ref)

    def fetch(layer, h, slot):
        return pltpu.make_async_copy(prob_hbm.at[layer, h], prob_ref.at[slot], prob_sem.at[slot])

    def head(layer):
        def run(h, carry):
            group = h // 4
            slot = h % 2
            mine = lane_head == h % 4
            lanes = pl.ds(pl.multiple_of(group * 256, 256), 256)
            row = pl.ds(pl.multiple_of(h * HD, HD), HD)
            gmix_h = jnp.where(mine, gmix_ref[:, lanes].astype(F32), 0.0).astype(BF16)
            prob_grad_ref[...] = dot_nn(gmix_h, values_ref[lanes, :])
            fetch(layer, h, slot).wait()
            for b in range(0, OWN, ROWS):
                rows = slice(b, b + ROWS)
                prob = prob_ref[slot, rows, :]
                gprob = prob_grad_ref[rows, :]
                inner = jnp.sum(prob * gprob, axis=-1, keepdims=True)
                score_grad_ref[rows, :] = (prob * (gprob - inner)).astype(BF16)
                low_prob_ref[rows, :] = prob.astype(BF16)

            if layer == 1:
                @pl.when(h < HEADS - 2)
                def _():
                    fetch(1, h + 2, slot).start()

                @pl.when(h >= HEADS - 2)
                def _():
                    fetch(0, h + 2 - HEADS, slot).start()
            else:
                @pl.when(h < HEADS - 2)
                def _():
                    fetch(0, h + 2, slot).start()

            sgrad = score_grad_ref[...]
            gquery_ref[0, group] = gquery_ref[0, group] + jnp.where(
                mine, dot_nn(sgrad, keys_ref[group]), 0.0
            )
            gkey = dot_nn(query_t_ref[row, :], sgrad) * SCALE
            gvalue = dot_nn(gmix_t_ref[row, :], low_prob_ref[...])
            gmemory_ref[0, row, :] = gkey[:, 0:SEG].astype(BF16)
            gmemory_ref[1, row, :] = gvalue[:, 0:SEG].astype(BF16)
            ghidden_ref[0, row, :] = gkey[:, SEG:]
            ghidden_ref[1, row, :] = gvalue[:, SEG:]
            flipped = dot_nn(flip, sgrad).astype(BF16)
            flipped_ref[...] = pltpu.roll(flipped, KLEN - OWN + 1, 1, stride=1, stride_axis=0)
            gquery_ref[1, group] = gquery_ref[1, group] + jnp.where(
                mine, dot_nn(flipped_ref[...], rel_ref[group]), 0.0
            )
            grel_ref[row, :] = (dot_nn(flip_t_ref[row, :], flipped_ref[...]) * SCALE).astype(BF16)
            return carry

        return run

    def swap(layer):
        return [
            send(
                ghidden_ref.at[:, 256 * i : 256 * i + 256, their_rows],
                got_ref.at[:, 256 - 256 * i : 512 - 256 * i],
                extra,
                10 + 2 * layer + i,
                here.sibling(),
            )
            for i in range(2)
        ]

    def finish(layer, swaps):
        own_low = low_ref[layer, own_rows, :]
        for group in range(2):
            lanes = slice(group * 256, (group + 1) * 256)
            gquery_u = (gquery_ref[0, group] * SCALE).astype(BF16)
            gquery_w = dot_nn(flip, (gquery_ref[1, group] * SCALE).astype(BF16))
            grad_bias_ref[layer, 0:1, lanes] = jnp.sum(
                gquery_u.astype(F32), axis=0, keepdims=True
            )
            grad_bias_ref[layer, 1:2, lanes] = jnp.sum(gquery_w, axis=0, keepdims=True)
            gquery = gquery_u.astype(F32) + gquery_w
            grad_att_ref[layer, 0, group] = (
                dot_nn(gquery.T.astype(BF16), own_low).astype(BF16).reshape(4, HD, D)
            )
            grad_ref[...] += dot_nn(gquery.astype(BF16), att_w[0, group].reshape(256, D))
        grad_att_ref[layer, 3] = (
            dot_nn(grel_ref[...], table_ref[...]).astype(BF16).reshape(2, 4, HD, D)
        )
        parts = [dot_nn(gmemory_ref[i], memory_w[layer]) for i in range(2)]
        for copy in swaps:
            copy.wait_recv()
        for i in range(2):
            total = (ghidden_ref[i, :, own_rows] + got_ref[i]).astype(BF16)
            grad_att_ref[layer, 1 + i] = (
                (parts[i] + dot_nn(total, own_low)).astype(BF16).reshape(2, 4, HD, D)
            )
            grad_ref[...] += dot_nn(transposed(total).astype(BF16), att_w[1 + i].reshape(D, D))

    fetch(1, 0, 0).start()
    fetch(1, 1, 1).start()
    feed(1)
    sums.pair(3)
    load_ff = pltpu.make_async_copy(ff_hbm.at[0], ff_w, load_sem.at[0])
    load_ff.start()
    spread_ce(0)
    for copy in loads:
        copy.wait()
    prepare(1)
    sums.one(3)
    lax.fori_loop(0, HEADS, head(1), 0)
    swaps_one = swap(1)
    spread_ce(1)
    finish(1, swaps_one)
    sums.pair(2)
    load_att = pltpu.make_async_copy(att_hbm.at[0], att_w, load_sem.at[1])
    load_att.start()
    sums.two(3)
    feed(0)
    sums.pair(1)
    sums.one(2)
    spread_ce(2)
    for copy in swaps_one:
        copy.wait_send()
    prepare(0)
    sums.one(1)
    sums.three(3)
    lax.fori_loop(0, 4, head(0), 0)
    sums.two(2)
    sums.four(3)
    lax.fori_loop(4, HEADS, head(0), 0)
    swaps_zero = swap(0)
    sums.three(2)
    sums.two(1)
    finish(0, swaps_zero)
    sums.pair(0)

    tokens = inputs_ref[pl.ds(here.y, 1), own_rows]
    onehot = jnp.where(
        tokens == lax.broadcasted_iota(jnp.int32, (VOCAB, OWN), 0), 1.0, 0.0
    ).astype(BF16)
    grad = grad_ref[...]
    high = grad.astype(BF16)
    rest = (grad - high.astype(F32)).astype(BF16)
    ranked_ref[...] += (dot_nn(onehot, high) + dot_nn(onehot, rest)).reshape(MP, 32, D)
    block_ref[...] = jnp.zeros_like(block_ref)
    for cc in range(2):
        for r in range(4):
            device = ((here.y + r) % 4) * 2 + (here.core + cc) % 2
            first = (cc * 4 + r) * HD
            block_ref[0:32, :] = ranked_ref[device]
            block_ref[32:34, :] = grad_norm_ref[device]
            block_ref[34:35, 0:256] = jnp.concatenate(
                [
                    grad_bias_ref[l, k : k + 1, first : first + HD]
                    for l in range(2)
                    for k in range(2)
                ],
                axis=1,
            )
            block_ref[35:36, :] = jnp.concatenate(
                [grad_inner_ref[l, cc, r] for l in range(2)], axis=1
            )
            grad_small_ref[0, 0, cc, r] = block_ref[...].astype(BF16)
    sums.pair(4)
    sums.one(0)
    sums.one(4)
    sums.three(1)
    sums.four(2)
    sums.two(0)
    sums.two(4)
    sums.four(1)
    sums.three(0)
    sums.three(4)
    for copy in ce_copies[-3:]:
        copy.wait_recv()
    ce_out[...] = (ce_x[0] + ce_x[1]) + (ce_x[2] + ce_x[3])
    sums.four(4)
    sums.four(0)
    sums.arrived(4, 4)
    small_out[here.y, here.core] = small_own[0, 0]
    piece = small_out.at[here.y, here.core]
    small_copies = [send(piece, piece, extra, 13 + r, here.along("y", r)) for r in (1, 2, 3)]
    for copy in small_copies:
        copy.wait_recv()
    piece = small_out.at[:, here.core]
    last = send(piece, piece, extra, 17, here.sibling())
    for g in ORDER:
        sums.arrived(4, g)
    last.wait()
    for copy in ce_copies + swaps_zero + small_copies:
        copy.wait_send()
    sums.end()


def backward_all(*operands):
    vmem, hbm = VMEM_SPEC, ANY_SPEC
    outs = [
        ((2, 5, HD, D), BF16),
        ((2, 2, D, 256), BF16),
        ((4, 2, 64, D), BF16),
        ((8, 128), F32),
    ]
    mats = {ATT: 5, FFN: 2, SMALL: 1}
    groups = GROUPS + (SMALL_GROUP,)
    scratch = [
        pltpu.VMEM((5, 2, 4, HD, D), BF16),
        pltpu.VMEM((2, 2, 4, D, 256), BF16),
        pltpu.VMEM((2, SEG, D), BF16),
        pltpu.VMEM((KLEN, D), BF16),
        pltpu.VMEM((2, OWN, KLEN), F32),
        pltpu.VMEM((2, 5, 2, 4, HD, D), BF16),
        pltpu.VMEM((2, 2, 2, 4, D, 256), BF16),
        pltpu.VMEM((1, 1, 2, 4, 64, D), BF16),
        pltpu.VMEM((OWN, D), F32),
        pltpu.VMEM((2, KLEN, 256), BF16),
        pltpu.VMEM((D, KLEN), BF16),
        pltpu.VMEM((2, KLEN, 256), BF16),
        pltpu.VMEM((OWN, D), BF16),
        pltpu.VMEM((D, OWN), BF16),
        pltpu.VMEM((D, OWN), BF16),
        pltpu.VMEM((D, OWN), BF16),
        pltpu.VMEM((OWN, KLEN), F32),
        pltpu.VMEM((OWN, KLEN), BF16),
        pltpu.VMEM((OWN, KLEN), BF16),
        pltpu.VMEM((OWN, KLEN), BF16),
        pltpu.VMEM((2, 2, OWN, 256), F32),
        pltpu.VMEM((2, D, SEG), BF16),
        pltpu.VMEM((2, D, SEG), F32),
        pltpu.VMEM((2, D, OWN), F32),
        pltpu.VMEM((D, KLEN), BF16),
        pltpu.VMEM((2, 2, D), F32),
        pltpu.VMEM((2, 2, 4, 1, 256), F32),
        pltpu.VMEM((MP, 2, D), F32),
        pltpu.VMEM((MP, 32, D), F32),
        pltpu.VMEM((64, D), F32),
        pltpu.VMEM((2, 8, 128), F32),
        pltpu.VMEM((4, 8, 128), F32),
        pltpu.VMEM((4, 8, 128), F32),
        pltpu.VMEM((4, 8, 128), F32),
        pltpu.VMEM((1, 1, 64, D), BF16),
    ]
    scratch += [pltpu.VMEM((mats[k], 4) + SHAPES[k], BF16) for k, _, _, _ in groups]
    for kind, _, parts, rows in groups:
        width = SHAPES[kind][1]
        scratch += [pltpu.VMEM((3, hi - lo, 4, rows, width), BF16) for _, lo, hi in parts]
        scratch += [pltpu.VMEM((3, hi - lo, rows, width), BF16) for _, lo, hi in parts]
        scratch += [pltpu.VMEM((4, hi - lo, rows, width), BF16) for _, lo, hi in parts]
    for n in (5, 30, 30, 30, 30, 18):
        scratch += [pltpu.SemaphoreType.DMA((n,)), pltpu.SemaphoreType.DMA((n,))]
    scratch += [pltpu.SemaphoreType.DMA((7,)), pltpu.SemaphoreType.DMA((2,))]
    return pl.pallas_call(
        backward_step,
        out_shape=[jax.ShapeDtypeStruct(s, t) for s, t in outs],
        in_specs=[hbm] * 7 + [vmem] * 12,
        out_specs=[vmem] * 4,
        scratch_shapes=scratch,
        compiler_params=pltpu.CompilerParams(
            collective_id=1, has_side_effects=True, vmem_limit_bytes=63 * 1024 * 1024
        ),
        name="backward_all",
    )(*operands)


def body(
    inputs,
    targets,
    valid_mask,
    memory,
    attention_rank,
    feedforward_rank,
    attention_weight,
    attention_moment,
    attention_average,
    feedforward_weight,
    feedforward_moment,
    feedforward_average,
    embedding_weight,
    embedding_moment,
    embedding_average,
    head_bias_weight,
    head_bias_moment,
    head_bias_average,
    inner_bias_weight,
    inner_bias_moment,
    inner_bias_average,
    norm_weight,
    norm_moment,
    norm_average,
):
    layers = attention_weight.shape[0]
    device = lax.axis_index("mp")
    attention_a = expand(attention_rank < 2, D // attention_rank.shape[2])
    attention_b = expand(attention_rank < 3, D // attention_rank.shape[2])
    feedforward_a = expand(feedforward_rank < 2, D // feedforward_rank.shape[2])
    feedforward_b = expand(feedforward_rank < 3, D // feedforward_rank.shape[2])
    attention_eff = (attention_weight * attention_a).astype(BF16).transpose(0, 1, 3, 2)
    feedforward_eff = (feedforward_weight * feedforward_a).astype(BF16)

    bias_pack = jnp.concatenate(
        [
            jnp.concatenate(
                [head_bias_weight.reshape(layers, 1, 128), inner_bias_weight.reshape(layers, 2, 128)],
                axis=1,
            ).reshape(3 * layers, 128),
            jnp.zeros((8 - 3 * layers, 128), F32),
        ]
    )
    local_count = jnp.broadcast_to(jnp.sum(valid_mask.astype(F32)), (8, 128))
    table = tables()
    (
        att_got,
        ff_got,
        new_memory,
        probs,
        bias_got,
        count_got,
        lows,
        *saved,
        grad_hidden,
        grad_embedding,
        ce_local,
    ) = forward_all(
        attention_eff,
        feedforward_eff,
        bias_pack,
        local_count,
        embedding_weight,
        inputs,
        targets,
        valid_mask,
        memory,
        norm_weight,
        table,
    )
    valid_count = count_got[0, 0]
    grad_attention, grad_feedforward, grad_small, ce_got = backward_all(
        att_got,
        ff_got,
        probs,
        memory,
        table,
        grad_hidden,
        grad_embedding,
        bias_got,
        norm_weight,
        inputs,
        ce_local,
        lows,
        *saved,
    )
    ce_total = ce_got[0, 0]
    small_all = grad_small.reshape(MP, 64, D).astype(F32)
    grad_embedding = small_all[:, 0:32].reshape(VOCAB, D)
    grad_norm = small_all[:, 32:34].reshape(2, 8, D)[:, 0:5]
    own_small = lax.dynamic_index_in_dim(small_all, device, 0, False)
    grad_head_bias = own_small[34, 0:256].reshape(layers, 2, HD)
    grad_inner_bias = own_small[35].reshape(layers, 256)
    grad_attention = grad_attention.astype(F32).transpose(0, 1, 3, 2)
    grad_feedforward = grad_feedforward.astype(F32)

    attention_coef = attention_a + WIDEN * (attention_b - attention_a)
    feedforward_coef = feedforward_a + WIDEN * (feedforward_b - feedforward_a)
    grad_attention = (
        attention_b * grad_attention + 2.0 * PENALTY * attention_weight * attention_coef
    )
    grad_feedforward = (
        feedforward_b * grad_feedforward + 2.0 * PENALTY * feedforward_weight * feedforward_coef
    )
    groups = [
        (attention_weight, attention_moment, attention_average, grad_attention),
        (feedforward_weight, feedforward_moment, feedforward_average, grad_feedforward),
        (head_bias_weight, head_bias_moment, head_bias_average, grad_head_bias),
        (inner_bias_weight, inner_bias_moment, inner_bias_average, grad_inner_bias),
        (embedding_weight, embedding_moment, embedding_average, grad_embedding),
        (norm_weight, norm_moment, norm_average, grad_norm),
    ]
    moments_next = [MOMENTUM * entry[1] + entry[3] for entry in groups]
    directions = [entry[3] + MOMENTUM * moment for entry, moment in zip(groups, moments_next)]
    local_sums = jnp.stack(
        [jnp.sum(entry[0] * entry[0]) for entry in groups[:4]]
        + [jnp.sum(direction * direction) for direction in directions[:4]]
    )
    totals = lax.psum(local_sums, "mp")
    weight_squares = [totals[i] for i in range(4)] + [
        jnp.sum(entry[0] * entry[0]) for entry in groups[4:]
    ]
    direction_squares = [totals[4 + i] for i in range(4)] + [
        jnp.sum(direction * direction) for direction in directions[4:]
    ]
    results = []
    for i in range(6):
        weight, moment, average, grad = groups[i]
        trust_ratio = jnp.sqrt(weight_squares[i]) / jnp.sqrt(direction_squares[i])
        weight_next = weight - RATE * trust_ratio * directions[i]
        results.append(
            (weight_next, moments_next[i], AVERAGE * average + (1.0 - AVERAGE) * weight_next)
        )
    return (
        ce_total,
        valid_count,
        new_memory,
        grad_attention,
        *results[0],
        grad_feedforward,
        *results[1],
        *results[4],
        *results[2],
        *results[3],
        grad_norm,
        *results[5],
    )


def solution(mesh):
    rows = P("dp", None)
    matrix = P(None, None, None, "mp")
    split_two = P(None, None, "mp")
    split_one = P(None, "mp")
    whole = P()
    return jax.shard_map(
        body,
        mesh=mesh,
        in_specs=(
            (rows,) * 3
            + (P(None, "dp", None, None),)
            + (matrix,) * 8
            + (whole,) * 3
            + (split_two,) * 3
            + (split_one,) * 3
            + (whole,) * 3
        ),
        out_specs=(
            (whole,) * 2
            + (P(None, "dp", None, None),)
            + (matrix,) * 8
            + (whole,) * 3
            + (split_two,) * 3
            + (split_one,) * 3
            + (whole,) * 4
        ),
        check_vma=False,
    )
```

```python
import functools

import jax
import jax.numpy as jnp
import numpy as np
from jax import lax
from jax.experimental import pallas as pl
from jax.experimental.pallas import tpu as pltpu
from jax.sharding import PartitionSpec as P

HD = 64
D = 512
FF = 2048
SEG = 512
KLEN = 1024
OWN = 256
HEADS = 8
VOCAB = 256
MP = 8

EPSILON = 1e-05
MOMENTUM = 0.9
AVERAGE = 0.9
RATE = 0.3
PENALTY = 0.0001
WIDEN = 5.0
F32 = jnp.float32
BF16 = jnp.bfloat16
SCALE = HD ** (-0.5)


def dot_nn(a, b):
    return lax.dot_general(a, b, (((1,), (0,)), ((), ())), preferred_element_type=F32)


def dot_nt(a, b):
    return lax.dot_general(a, b, (((1,), (1,)), ((), ())), preferred_element_type=F32)


def smooth_unit(v):
    return 0.5 * v * (1.0 + jnp.tanh(0.7978845608028654 * (v + 0.044715 * v * v * v)))


def smooth_both(v):
    squared = v * v
    t = jnp.tanh(0.7978845608028654 * (v + 0.044715 * squared * v))
    half = 0.5 * (1.0 + t)
    slope = half + 0.5 * v * (1.0 - t * t) * (
        0.7978845608028654 * (1.0 + 3.0 * 0.044715 * squared)
    )
    return v * half, slope


def tables():
    freq = (1.0 / 10000.0 ** (np.arange(0, D, 2).astype(np.float32) / np.float32(D))).astype(
        np.float32
    )
    turned = []
    for half in range(2):
        distance = (SEG + half * OWN - np.arange(KLEN)) % KLEN
        angle = (distance.astype(np.float32)[:, None] * freq[None, :]).astype(np.float64)
        turned.append(np.concatenate([np.sin(angle), np.cos(angle)], axis=1).astype(np.float32))
    return jnp.asarray(np.stack(turned), BF16)


def norm_forward(values):
    centred = values - jnp.mean(values, axis=-1, keepdims=True)
    inverse = lax.rsqrt(jnp.mean(centred * centred, axis=-1, keepdims=True) + EPSILON)
    return centred * inverse, inverse


def norm_backward(grad, normed, inverse, gain):
    scaled = grad * gain
    grad_in = inverse * (
        scaled
        - jnp.mean(scaled, axis=-1, keepdims=True)
        - normed * jnp.mean(scaled * normed, axis=-1, keepdims=True)
    )
    return (
        grad_in,
        jnp.sum(grad * normed, axis=0, keepdims=True),
        jnp.sum(grad, axis=0, keepdims=True),
    )


def transposed(value):
    return value.astype(F32).T


ROWS = 64
VMEM_SPEC = pl.BlockSpec(memory_space=pltpu.VMEM)
VMEM_LIMIT = 60 * 1024 * 1024


ANY_SPEC = pl.BlockSpec(memory_space=pl.ANY)
MESH = pl.DeviceIdType.MESH

ATT, FFN, SMALL = 0, 1, 2
GROUPS = (
    (ATT, 0, (("z", 0, 3), ("x", 3, 5)), 16),
    (FFN, 0, (("z", 0, 1), ("x", 1, 2)), 128),
    (ATT, 1, (("z", 0, 2), ("x", 2, 5)), 16),
    (FFN, 1, (("z", 0, 1), ("x", 1, 2)), 128),
)
SUM_GROUPS = (
    (ATT, 0, (0, 4), (("z", 0, 2), ("x", 2, 4)), 16),
    (FFN, 0, (0, 2), (("z", 0, 1), ("x", 1, 2)), 128),
    (ATT, 1, (0, 4), (("z", 0, 2), ("x", 2, 4)), 16),
    (FFN, 1, (0, 2), (("z", 0, 1), ("x", 1, 2)), 128),
    (SMALL, 0, (0, 1), (("z", 0, 1),), 16),
    (ATT, 0, (4, 5), (("z", 0, 1),), 16),
    (ATT, 1, (4, 5), (("x", 0, 1),), 16),
)


class Place:
    def __init__(self):
        dp, mp = lax.axis_index("dp"), lax.axis_index("mp")
        self.x, self.z = dp // 4, dp % 4
        self.y, self.core = mp // 2, mp % 2

    def device(self, x=None, z=None, y=None, core=None):
        x = self.x if x is None else x
        z = self.z if z is None else z
        y = self.y if y is None else y
        core = self.core if core is None else core
        return {"dp": x * 4 + z, "mp": y * 2 + core}

    def along(self, axis, shift):
        return self.device(**{axis: (getattr(self, axis) + shift + 4) % 4})

    def sibling(self):
        return self.device(core=1 - self.core)

    def greet(self):
        partners = [self.along(axis, s) for axis in "xzy" for s in (1, 2, 3)] + [self.sibling()]
        barrier = pltpu.get_barrier_semaphore()
        for partner in partners:
            pl.semaphore_signal(barrier, inc=1, device_id=partner, device_id_type=MESH)

    def greeted(self):
        pl.semaphore_wait(pltpu.get_barrier_semaphore(), 10)


def send(source, target, sems, index, device):
    copy = pltpu.make_async_remote_copy(
        src_ref=source,
        dst_ref=target,
        send_sem=sems[0].at[index],
        recv_sem=sems[1].at[index],
        device_id=device,
        device_id_type=MESH,
    )
    copy.start()
    return copy


def spread_rank(rank, width):
    blocks = rank.shape[1]
    lane = lax.broadcasted_iota(jnp.int32, (blocks, width), 1) // (width // blocks)
    row = lax.broadcasted_iota(jnp.int32, (blocks, width), 0)
    return dot_nn(rank, jnp.where(lane == row, 1.0, 0.0))


class Weights:
    def __init__(self, here, sources, targets, sems, local_sem):
        self.here, self.sources, self.targets = here, sources, targets
        self.sems, self.local_sem = sems, local_sem
        self.copies = [[None] * len(GROUPS) for _ in range(3)]
        self.local = [None] * len(GROUPS)

    def slice_at(self, axis, rows):
        return pl.ds(pl.multiple_of(getattr(self.here, axis) * rows, rows), rows)

    def one(self, g):
        kind, layer, parts, rows = GROUPS[g]
        source, target = self.sources[kind].at[layer], self.targets[kind].at[layer]
        self.local[g] = pltpu.make_async_copy(source, target.at[:, 0, 0], self.local_sem.at[g])
        self.local[g].start()
        self.copies[0][g] = [
            send(
                source.at[low:high, self.slice_at(axis, rows)],
                target.at[low:high, 0, r, self.slice_at(axis, rows)],
                self.sems[0],
                g * 6 + p * 3 + r - 1,
                self.here.along("y", -r),
            )
            for p, (axis, low, high) in enumerate(parts)
            for r in (1, 2, 3)
        ]

    def two(self, g):
        kind, layer, parts, rows = GROUPS[g]
        target = self.targets[kind].at[layer]
        for copy in self.copies[0][g]:
            copy.wait_recv()
        self.copies[1][g] = []
        for p, (axis, low, high) in enumerate(parts):
            part = target.at[low:high, 0, 1:4, self.slice_at(axis, rows)]
            for s in (1, 2, 3):
                self.copies[1][g].append(
                    send(part, part, self.sems[1], g * 6 + p * 3 + s - 1, self.here.along(axis, s))
                )

    def three(self, g):
        kind, layer, _, _ = GROUPS[g]
        target = self.targets[kind].at[layer]
        for copy in self.copies[1][g]:
            copy.wait_recv()
        self.local[g].wait()
        self.copies[2][g] = [
            send(target.at[:, 0], target.at[:, 1], self.sems[2], g, self.here.sibling())
        ]

    def load(self, g, buffer, sem):
        kind, layer, _, _ = GROUPS[g]
        self.copies[2][g][0].wait_recv()
        copy = pltpu.make_async_copy(self.targets[kind].at[layer], buffer, sem)
        copy.start()
        return copy

    def end(self):
        for stage in self.copies:
            for copies in stage:
                for copy in copies:
                    copy.wait_send()


def forward_step(
    att_weight_ref,
    ff_weight_ref,
    att_rank_ref,
    ff_rank_ref,
    head_bias_ref,
    inner_bias_ref,
    embedding_ref,
    inputs_ref,
    targets_ref,
    valid_ref,
    memory_ref,
    norm_ref,
    table_hbm,
    att_out,
    ff_out,
    new_memory_ref,
    prob_out,
    bias_out,
    count_out,
    low_out,
    query_u_out,
    query_w_out,
    mixed_out,
    normed_one_out,
    inverse_one_out,
    normed_two_out,
    inverse_two_out,
    grad_ref,
    grad_embedding_ref,
    ce_ref,
    att_ref,
    ff_ref,
    bias_ref,
    count_ref,
    rank_ref,
    block_rank_ref,
    count_z,
    count_x,
    att_w,
    ff_w,
    memory_w,
    table_ref,
    turned_ref,
    embed_ref,
    keys_ref,
    values_ref,
    rel_ref,
    score_ref,
    prob_ref,
    low_prob_ref,
    part_ref,
    hidden_ref,
    first_send,
    first_recv,
    second_send,
    second_recv,
    third_send,
    third_recv,
    extra_send,
    extra_recv,
    local_sem,
    load_sem,
    prob_sem,
):
    here = Place()
    here.greet()
    extra = (extra_send, extra_recv)
    rank_ref[...] = spread_rank(att_rank_ref[...], D)
    block_rank_ref[...] = spread_rank(ff_rank_ref[...], 256)

    def mask_attention(layer):
        for i in range(5):
            kept = rank_ref[layer * 5 + i : layer * 5 + i + 1, :] < 1.5
            att_ref[layer, i] = jnp.where(kept, att_weight_ref[layer, i], 0.0).astype(BF16)

    def mask_feedforward(layer):
        for i in range(16):
            kept = block_rank_ref[layer * 16 + i : layer * 16 + i + 1, :] < 1.5
            rows = slice(i % 8 * 64, i % 8 * 64 + 64)
            ff_ref[layer, i // 8, rows, :] = jnp.where(
                kept, ff_weight_ref[layer, i // 8, rows, :], 0.0
            ).astype(BF16)

    mask_attention(0)
    here.greeted()
    weights = Weights(
        here,
        (att_ref, ff_ref),
        (att_out, ff_out),
        ((first_send, first_recv), (second_send, second_recv), (third_send, third_recv)),
        local_sem,
    )
    weights.one(0)
    mask_feedforward(0)
    weights.one(1)
    counted = jnp.sum(valid_ref[...].astype(F32), axis=1, keepdims=True)
    count_ref[...] = jnp.broadcast_to(jnp.sum(counted, axis=0, keepdims=True), (8, 128))
    bias_ref[6:8, :] = jnp.zeros((2, 128), F32)
    for l in range(2):
        bias_ref[3 * l : 3 * l + 1, :] = jnp.concatenate(
            [head_bias_ref[l, k : k + 1, :] for k in range(2)], axis=1
        )
        for k in range(2):
            bias_ref[3 * l + 1 + k : 3 * l + 2 + k, :] = inner_bias_ref[
                l : l + 1, k * 128 : (k + 1) * 128
            ]
    count_z[here.z] = count_ref[...]
    count_copies = [
        send(count_ref, count_z.at[here.z], extra, s - 1, here.along("z", s)) for s in (1, 2, 3)
    ]
    bias_copies = [
        send(bias_ref, bias_out.at[0, r], extra, 2 + r, here.along("y", -r)) for r in (1, 2, 3)
    ]
    bias_out[0, 0] = bias_ref[...]
    mask_attention(1)
    weights.one(2)
    mask_feedforward(1)
    weights.one(3)
    loads = [
        pltpu.make_async_copy(table_hbm.at[here.core], table_ref, load_sem.at[0]),
        pltpu.make_async_copy(memory_ref.at[0, here.y], memory_w.at[0], load_sem.at[1]),
        pltpu.make_async_copy(memory_ref.at[1, here.y], memory_w.at[1], load_sem.at[2]),
    ]
    for copy in loads:
        copy.start()

    own_rows = pl.ds(pl.multiple_of(here.core * OWN, OWN), OWN)
    turned_ref[...] = jnp.zeros_like(turned_ref)
    turned_ref[0:4, :] = inputs_ref[...].astype(F32)
    turned_ref[8:12, :] = targets_ref[...].astype(F32)
    turned_ref[16:20, :] = valid_ref[...].astype(F32)
    columns = turned_ref[...].T
    turned_ref[:, 0:128] = columns[0:128]
    turned_ref[:, 128:256] = columns[128:256]
    turned_ref[:, 256:384] = columns[256:384]
    turned_ref[:, 384:512] = columns[384:512]
    embedding = embedding_ref[...]
    embedding_low = embedding.astype(BF16)
    vocab_id = lax.broadcasted_iota(jnp.int32, (128, VOCAB), 1).astype(F32)

    def onehot(column):
        return jnp.where(column == vocab_id, 1.0, 0.0)

    for segment in range(4):
        for b in range(4):
            tokens = turned_ref[:, b * 128 + segment : b * 128 + segment + 1]
            embed_ref[segment, b * 128 : (b + 1) * 128, :] = dot_nn(
                onehot(tokens).astype(BF16), embedding_low
            ).astype(BF16)
    memory_zero = pltpu.make_async_copy(embed_ref, new_memory_ref.at[0], load_sem.at[3])
    memory_zero.start()
    weights.two(0)
    low_out[0] = embed_ref[here.y]
    rest_one = embedding - embedding_low.astype(F32)
    middle_part = rest_one.astype(BF16)
    rest_two = (rest_one - middle_part.astype(F32)).astype(BF16)
    lane = lax.broadcasted_iota(jnp.int32, (128, 128), 1)
    own_targets, own_valid = [], []
    for b in range(2):
        block = turned_ref[:, pl.ds(pl.multiple_of(here.core * 256 + b * 128, 128), 128)]

        def column(at):
            return jnp.sum(jnp.where(lane == here.y + at, block, 0.0), axis=1, keepdims=True)

        mine = onehot(column(0)).astype(BF16)
        hidden_ref[b * 128 : (b + 1) * 128, :] = (
            dot_nn(mine, embedding_low) + dot_nn(mine, middle_part)
        ) + dot_nn(mine, rest_two)
        own_targets.append(onehot(column(8)))
        own_valid.append(column(16))
    weights.three(0)
    for copy in bias_copies:
        copy.wait_recv()
    bias_last = send(bias_out.at[0], bias_out.at[1], extra, 6, here.sibling())
    for copy in count_copies:
        copy.wait_recv()
    count_x[here.x] = (count_z[0] + count_z[1]) + (count_z[2] + count_z[3])
    count_last = [
        send(count_x.at[here.x], count_x.at[here.x], extra, 6 + s, here.along("x", s))
        for s in (1, 2, 3)
    ]
    weights.two(1)
    for copy in loads:
        copy.wait()
    bias_last.wait_recv()
    pending = []
    offset = here.core * OWN
    lane_head = lax.broadcasted_iota(jnp.int32, (OWN, 256), 1) // HD

    def project(layer):
        own_low = hidden_ref[...].astype(BF16)
        query = dot_nt(own_low, att_w[layer, 0].reshape(D, D))
        for which, target in ((0, query_u_out), (1, query_w_out)):
            bias = jnp.concatenate(
                [
                    bias_out[cc, r, 3 * layer : 3 * layer + 1, which * HD : (which + 1) * HD]
                    for cc in range(2)
                    for r in range(4)
                ],
                axis=1,
            )
            target[layer] = (query + bias).astype(BF16)
        key_w, value_w = att_w[layer, 1].reshape(D, D), att_w[layer, 2].reshape(D, D)
        for half in range(2):
            rows = memory_w[layer] if half == 0 else low_out[layer]
            cols = slice(half * SEG, (half + 1) * SEG)
            keys_ref[:, cols] = dot_nt(key_w, rows).astype(BF16)
            values = dot_nt(rows, value_w).astype(BF16)
            values_ref[0, cols, :] = values[:, 0:256]
            values_ref[1, cols, :] = values[:, 256:512]
        rel_ref[...] = dot_nt(att_w[layer, 3].reshape(D, D), table_ref[...]).astype(BF16)
        part_ref[...] = jnp.zeros_like(part_ref)

    def head(layer):
        def run(h, carry):
            group = h // 4
            slot = h % 2
            mine = lane_head == h % 4
            lanes = pl.ds(pl.multiple_of(group * 256, 256), 256)
            query_u = jnp.where(mine, query_u_out[layer, :, lanes].astype(F32), 0.0).astype(BF16)
            query_w = jnp.where(mine, query_w_out[layer, :, lanes].astype(F32), 0.0).astype(BF16)
            score_ref[...] = dot_nn(query_w, rel_ref[lanes, :])

            @pl.when(h >= 2)
            def _():
                pltpu.make_async_copy(
                    prob_ref.at[slot], prob_out.at[layer, h], prob_sem.at[slot]
                ).wait()

            prob_ref[slot] = dot_nn(query_u, keys_ref[lanes, :])
            for b in range(0, OWN, ROWS):
                rows = slice(b, b + ROWS)
                moved = pltpu.roll(score_ref[rows, :], b, 1, stride=1, stride_axis=0)
                score = (prob_ref[slot, rows, :] + moved) * SCALE
                key_id = lax.broadcasted_iota(jnp.int32, (ROWS, KLEN), 1)
                query_id = lax.broadcasted_iota(jnp.int32, (ROWS, KLEN), 0) + (offset + b + SEG)
                score = jnp.where(key_id <= query_id, score, -1e30)
                expo = jnp.exp(score - jnp.max(score, axis=-1, keepdims=True))
                prob = expo * (1.0 / jnp.sum(expo, axis=-1, keepdims=True))
                prob_ref[slot, rows, :] = prob
                low_prob_ref[rows, :] = prob.astype(BF16)
            pltpu.make_async_copy(
                prob_ref.at[slot], prob_out.at[layer, h], prob_sem.at[slot]
            ).start()
            mixed = dot_nn(low_prob_ref[...], values_ref[group])
            part_ref[group] = part_ref[group] + jnp.where(mine, mixed, 0.0)
            return carry

        return run

    def attend(layer):
        for slot in range(2):
            pltpu.make_async_copy(
                prob_ref.at[slot], prob_out.at[layer, 6 + slot], prob_sem.at[slot]
            ).wait()
        mixed_out[layer, :, 0:256] = part_ref[0].astype(BF16)
        mixed_out[layer, :, 256:512] = part_ref[1].astype(BF16)
        attended = dot_nn(mixed_out[layer], att_w[layer, 4].reshape(D, D))
        normed_one, inverse_one = norm_forward(hidden_ref[...] + attended)
        normed_one_out[layer] = normed_one
        inverse_one_out[layer] = inverse_one
        return normed_one * norm_ref[0, layer : layer + 1, :] + norm_ref[1, layer : layer + 1, :]

    def feed(layer, middle):
        middle_low = middle.astype(BF16)
        branch = jnp.zeros((OWN, D), F32)
        for cc in range(2):
            for r in range(4):
                bias = jnp.concatenate(
                    [bias_out[cc, r, 3 * layer + 1 + i : 3 * layer + 2 + i, :] for i in range(2)],
                    axis=1,
                )
                inner = dot_nn(middle_low, ff_w[layer, 0, cc, r]) + bias
                branch = branch + dot_nt(smooth_unit(inner).astype(BF16), ff_w[layer, 1, cc, r])
        normed_two, inverse_two = norm_forward(middle + (branch + norm_ref[4, layer : layer + 1, :]))
        normed_two_out[layer] = normed_two
        inverse_two_out[layer] = inverse_two
        hidden_ref[...] = normed_two * norm_ref[2, layer : layer + 1, :] + norm_ref[3, layer : layer + 1, :]

    weights.load(0, att_w.at[0], load_sem.at[4]).wait()
    project(0)
    weights.two(2)
    lax.fori_loop(0, 4, head(0), 0)
    weights.three(1)
    weights.two(3)
    lax.fori_loop(4, 8, head(0), 0)
    weights.three(2)
    feed_load = weights.load(1, ff_w.at[0], load_sem.at[5])
    middle = attend(0)
    feed_load.wait()
    feed(0, middle)
    low_out[1, own_rows, :] = hidden_ref[...].astype(BF16)
    own_low = low_out.at[1, own_rows]
    swap = send(own_low, own_low, extra, 10, here.sibling())
    spread_at = new_memory_ref.at[1, here.y, own_rows]
    spread = [send(own_low, spread_at, extra, 10 + s, here.along("y", s)) for s in (1, 2, 3)]
    spread_own = pltpu.make_async_copy(own_low, spread_at, load_sem.at[6])
    spread_own.start()
    attention_one = weights.load(2, att_w.at[1], load_sem.at[7])
    swap.wait_recv()
    attention_one.wait()
    project(1)
    lax.fori_loop(0, 4, head(1), 0)
    weights.three(3)
    for copy in spread:
        copy.wait_recv()
    spread_own.wait()
    spread_all = new_memory_ref.at[1, :, own_rows]
    spread_last = send(spread_all, spread_all, extra, 14, here.sibling())
    lax.fori_loop(4, 8, head(1), 0)
    feed_load = weights.load(3, ff_w.at[1], load_sem.at[5])
    middle = attend(1)
    feed_load.wait()
    feed(1, middle)
    for copy in count_last:
        copy.wait_recv()
    count_all = (count_x[0] + count_x[1]) + (count_x[2] + count_x[3])
    count_out[...] = count_all

    final_low = hidden_ref[...].astype(BF16)
    logit_scale = D ** (-0.5)
    logits = dot_nt(final_low, embedding_low) * logit_scale
    picked = jnp.concatenate(own_targets, axis=0)
    valid = jnp.concatenate(own_valid, axis=0)
    peak = jnp.max(logits, axis=-1, keepdims=True)
    log_total = peak + jnp.log(jnp.sum(jnp.exp(logits - peak), axis=-1, keepdims=True))
    losses = valid * (log_total - jnp.sum(logits * picked, axis=-1, keepdims=True))
    ce_ref[...] = jnp.broadcast_to(jnp.sum(losses, axis=0, keepdims=True), (8, 128))
    grad_logits = (valid * (jnp.exp(logits - log_total) - picked) / count_all[0:1, 0:1]).astype(
        BF16
    )
    grad_ref[...] = dot_nn(grad_logits, embedding_low) * logit_scale
    grad_embedding_ref[...] = (
        dot_nn(transposed(grad_logits).astype(BF16), final_low) * logit_scale
    ).reshape(MP, 32, D)
    memory_zero.wait()
    spread_last.wait()
    for copy in count_copies + bias_copies + [bias_last] + count_last + [swap] + spread:
        copy.wait_send()
    weights.end()


def forward_all(*operands):
    vmem, hbm = VMEM_SPEC, ANY_SPEC
    outs = [
        (hbm, (2, 5, 2, 4, HD, D), BF16),
        (hbm, (2, 2, 2, 4, D, 256), BF16),
        (hbm, (2, 4, SEG, D), BF16),
        (hbm, (2, HEADS, OWN, KLEN), F32),
        (vmem, (2, 4, 8, 128), F32),
        (vmem, (8, 128), F32),
        (vmem, (2, SEG, D), BF16),
        (vmem, (2, OWN, D), BF16),
        (vmem, (2, OWN, D), BF16),
        (vmem, (2, OWN, D), BF16),
        (vmem, (2, OWN, D), F32),
        (vmem, (2, OWN, 1), F32),
        (vmem, (2, OWN, D), F32),
        (vmem, (2, OWN, 1), F32),
        (vmem, (OWN, D), F32),
        (vmem, (MP, 32, D), F32),
        (vmem, (8, 128), F32),
    ]
    return pl.pallas_call(
        forward_step,
        out_shape=[jax.ShapeDtypeStruct(s, t) for _, s, t in outs],
        in_specs=[vmem] * 10 + [hbm, vmem, hbm],
        out_specs=[m for m, _, _ in outs],
        scratch_shapes=[
            pltpu.VMEM((2, 5, HD, D), BF16),
            pltpu.VMEM((2, 2, D, 256), BF16),
            pltpu.VMEM((8, 128), F32),
            pltpu.VMEM((8, 128), F32),
            pltpu.VMEM((10, D), F32),
            pltpu.VMEM((32, 256), F32),
            pltpu.VMEM((4, 8, 128), F32),
            pltpu.VMEM((4, 8, 128), F32),
            pltpu.VMEM((2, 5, 2, 4, HD, D), BF16),
            pltpu.VMEM((2, 2, 2, 4, D, 256), BF16),
            pltpu.VMEM((2, SEG, D), BF16),
            pltpu.VMEM((KLEN, D), BF16),
            pltpu.VMEM((128, SEG), F32),
            pltpu.VMEM((4, SEG, D), BF16),
            pltpu.VMEM((D, KLEN), BF16),
            pltpu.VMEM((2, KLEN, 256), BF16),
            pltpu.VMEM((D, KLEN), BF16),
            pltpu.VMEM((OWN, KLEN), F32),
            pltpu.VMEM((2, OWN, KLEN), F32),
            pltpu.VMEM((OWN, KLEN), BF16),
            pltpu.VMEM((2, OWN, 256), F32),
            pltpu.VMEM((OWN, D), F32),
            pltpu.SemaphoreType.DMA((24,)),
            pltpu.SemaphoreType.DMA((24,)),
            pltpu.SemaphoreType.DMA((24,)),
            pltpu.SemaphoreType.DMA((24,)),
            pltpu.SemaphoreType.DMA((4,)),
            pltpu.SemaphoreType.DMA((4,)),
            pltpu.SemaphoreType.DMA((15,)),
            pltpu.SemaphoreType.DMA((15,)),
            pltpu.SemaphoreType.DMA((4,)),
            pltpu.SemaphoreType.DMA((8,)),
            pltpu.SemaphoreType.DMA((2,)),
        ],
        compiler_params=pltpu.CompilerParams(
            collective_id=0, has_side_effects=True, vmem_limit_bytes=VMEM_LIMIT
        ),
        name="forward_all",
    )(*operands)


SHAPES = {ATT: (HD, D), FFN: (D, 256), SMALL: (64, D)}


class Sums:
    def __init__(self, here, arrays, outs, buffers, sems):
        self.here, self.arrays, self.outs = here, arrays, outs
        self.pairs, self.ones, self.twos, self.threes = buffers
        self.sems = sems
        self.copies = [[[] for _ in SUM_GROUPS] for _ in range(5)]

    def slice_at(self, index, rows):
        return pl.ds(pl.multiple_of(index * rows, rows), rows)

    def arrived(self, stage, g):
        for copy in self.copies[stage][g]:
            copy.wait_recv()

    def pair(self, g):
        kind, layer, (base, end), _, _ = SUM_GROUPS[g]
        self.copies[0][g].append(
            send(
                self.arrays[kind].at[layer, base:end, 1],
                self.pairs[g],
                self.sems[0],
                g,
                self.here.sibling(),
            )
        )

    def one(self, g):
        kind, layer, (base, _), parts, rows = SUM_GROUPS[g]
        self.arrived(0, g)
        pair = self.pairs[g]
        for m in range(pair.shape[0]):
            for r in range(4):
                pair[m, r] = (
                    pair[m, r].astype(F32) + self.arrays[kind][layer, base + m, 0, r].astype(F32)
                ).astype(BF16)
        for p, (axis, low, high) in enumerate(parts):
            for s in (1, 2, 3):
                goal = (getattr(self.here, axis) + s) % 4
                self.copies[1][g].append(
                    send(
                        pair.at[low:high, :, self.slice_at(goal, rows)],
                        self.ones[g][p].at[s - 1],
                        self.sems[1],
                        g * 6 + p * 3 + s - 1,
                        self.here.along(axis, s),
                    )
                )

    def two(self, g):
        kind, layer, (base, _), parts, rows = SUM_GROUPS[g]
        self.arrived(1, g)
        for p, (axis, low, high) in enumerate(parts):
            got = self.ones[g][p]
            own = self.pairs[g].at[low:high, :, self.slice_at(getattr(self.here, axis), rows)]
            for m in range(high - low):
                for r in range(4):
                    got[0, m, r] = (
                        (own[m, r].astype(F32) + got[0, m, r].astype(F32))
                        + (got[1, m, r].astype(F32) + got[2, m, r].astype(F32))
                    ).astype(BF16)
            for r in (1, 2, 3):
                self.copies[2][g].append(
                    send(
                        got.at[0, :, r],
                        self.twos[g][p].at[r - 1],
                        self.sems[2],
                        g * 6 + p * 3 + r - 1,
                        self.here.along("y", r),
                    )
                )

    def three(self, g):
        kind, layer, (base, _), parts, rows = SUM_GROUPS[g]
        self.arrived(2, g)
        for p, (axis, low, high) in enumerate(parts):
            other = "x" if axis == "z" else "z"
            got, every = self.twos[g][p], self.threes[g][p]
            index = getattr(self.here, other)
            for m in range(high - low):
                every[index, m] = (
                    (self.ones[g][p][0, m, 0].astype(F32) + got[0, m].astype(F32))
                    + (got[1, m].astype(F32) + got[2, m].astype(F32))
                ).astype(BF16)
            for s in (1, 2, 3):
                self.copies[3][g].append(
                    send(
                        every.at[index],
                        every.at[index],
                        self.sems[3],
                        g * 6 + p * 3 + s - 1,
                        self.here.along(other, s),
                    )
                )

    def four(self, g):
        kind, layer, (base, _), parts, rows = SUM_GROUPS[g]
        self.arrived(3, g)
        for p, (axis, low, high) in enumerate(parts):
            every = self.threes[g][p]
            part = self.slice_at(getattr(self.here, axis), rows)
            for m in range(high - low):
                self.outs[kind][layer, base + low + m, part] = (
                    (every[0, m].astype(F32) + every[1, m].astype(F32))
                    + (every[2, m].astype(F32) + every[3, m].astype(F32))
                ).astype(BF16)
            target = self.outs[kind].at[layer, base + low : base + high, part]
            for s in (1, 2, 3):
                self.copies[4][g].append(
                    send(
                        target,
                        target,
                        self.sems[4],
                        g * 6 + p * 3 + s - 1,
                        self.here.along(axis, s),
                    )
                )

    def end(self):
        for stage in self.copies:
            for copies in stage:
                for copy in copies:
                    copy.wait_send()


def backward_step(
    att_hbm,
    ff_hbm,
    prob_hbm,
    memory_hbm,
    table_hbm,
    grad_hbm,
    grad_embedding_hbm,
    normed_two_hbm,
    bias_ref,
    norm_ref,
    inputs_ref,
    ce_ref,
    low_ref,
    query_u_ref,
    query_w_ref,
    mixed_ref,
    normed_one_ref,
    inverse_one_ref,
    inverse_two_ref,
    att_out,
    ff_out,
    small_out,
    ce_out,
    att_w,
    ff_w,
    memory_w,
    table_ref,
    prob_ref,
    grad_att_ref,
    grad_ff_ref,
    grad_small_ref,
    grad_ref,
    keys_ref,
    values_ref,
    rel_ref,
    gmix_ref,
    gmix_t_ref,
    query_t_ref,
    flip_t_ref,
    prob_grad_ref,
    score_grad_ref,
    low_prob_ref,
    flipped_ref,
    gquery_ref,
    gmemory_ref,
    ghidden_ref,
    got_ref,
    grel_ref,
    grad_bias_ref,
    grad_inner_ref,
    grad_norm_ref,
    ranked_ref,
    block_ref,
    ce_pair,
    ce_z,
    ce_y,
    ce_x,
    small_own,
    *scratch,
):
    here = Place()
    scratch = list(scratch)
    pairs = [scratch.pop(0) for _ in SUM_GROUPS]
    ones, twos, threes = [], [], []
    for group in SUM_GROUPS:
        for buffers in (ones, twos, threes):
            buffers.append([scratch.pop(0) for _ in group[3]])
    sems = [(scratch.pop(0), scratch.pop(0)) for _ in range(6)]
    load_sem, prob_sem = scratch
    extra = sems[5]
    sums = Sums(
        here,
        (grad_att_ref, grad_ff_ref, grad_small_ref),
        (att_out, ff_out, small_own),
        (pairs, ones, twos, threes),
        sems,
    )
    load_ff = pltpu.make_async_copy(ff_hbm.at[1], ff_w, load_sem.at[0])
    load_att = pltpu.make_async_copy(att_hbm.at[1], att_w, load_sem.at[1])
    loads = [
        pltpu.make_async_copy(memory_hbm.at[0, here.y], memory_w.at[0], load_sem.at[2]),
        pltpu.make_async_copy(memory_hbm.at[1, here.y], memory_w.at[1], load_sem.at[3]),
        pltpu.make_async_copy(table_hbm.at[here.core], table_ref, load_sem.at[4]),
        pltpu.make_async_copy(grad_embedding_hbm, ranked_ref, load_sem.at[5]),
    ]
    load_grad = pltpu.make_async_copy(grad_hbm, grad_ref, load_sem.at[6])
    load_grad.start()
    load_normed = pltpu.make_async_copy(
        normed_two_hbm.at[1], prob_grad_ref.at[:, 0:D], load_sem.at[7]
    )
    load_normed.start()
    load_ff.start()
    load_att.start()
    for copy in loads:
        copy.start()
    here.greet()
    here.greeted()
    own_rows = pl.ds(pl.multiple_of(here.core * OWN, OWN), OWN)
    their_rows = pl.ds(pl.multiple_of(OWN - here.core * OWN, OWN), OWN)
    ce_pair[here.core] = ce_ref[...]
    ce_copies = [send(ce_ref, ce_pair.at[here.core], extra, 0, here.sibling())]
    flip = (
        lax.broadcasted_iota(jnp.int32, (OWN, OWN), 0)
        + lax.broadcasted_iota(jnp.int32, (OWN, OWN), 1)
        == OWN - 1
    )
    flip = jnp.where(flip, 1.0, 0.0).astype(BF16)
    lane_head = lax.broadcasted_iota(jnp.int32, (OWN, 256), 1) // HD
    load_grad.wait()

    def spread_ce(step):
        source, target, axis, base = (
            (ce_pair, ce_z, "z", 1),
            (ce_z, ce_y, "y", 4),
            (ce_y, ce_x, "x", 7),
        )[step]
        for copy in ce_copies[-1:] if step == 0 else ce_copies[-3:]:
            copy.wait_recv()
        total = source[0] + source[1]
        if step:
            total = total + (source[2] + source[3])
        index = getattr(here, axis)
        target[index] = total
        for s in (1, 2, 3):
            ce_copies.append(
                send(target.at[index], target.at[index], extra, base + s - 1, here.along(axis, s))
            )

    def feed(layer):
        load_normed.wait()
        gsum, ggain, goffset = norm_backward(
            grad_ref[...], prob_grad_ref[:, 0:D], inverse_two_ref[layer], norm_ref[2, layer : layer + 1, :]
        )
        middle = normed_one_ref[layer] * norm_ref[0, layer : layer + 1, :] + norm_ref[1, layer : layer + 1, :]
        middle_low = middle.astype(BF16)
        middle_t = transposed(middle_low).astype(BF16)
        gbranch = gsum.astype(BF16)
        gbranch_t = transposed(gbranch).astype(BF16)
        gmiddle = gsum
        load_ff.wait()
        for cc in (1, 0):
            if cc == 0:
                sums.pair(1 if layer == 0 else 3)
            for r in range(4):
                bias = jnp.concatenate(
                    [bias_ref[cc, r, 3 * layer + 1 + i : 3 * layer + 2 + i, :] for i in range(2)],
                    axis=1,
                )
                inner = dot_nn(middle_low, ff_w[0, cc, r]) + bias
                active, slope = smooth_both(inner)
                ginner = (dot_nn(gbranch, ff_w[1, cc, r]) * slope).astype(BF16)
                grad_ff_ref[layer, 0, cc, r] = dot_nn(middle_t, ginner).astype(BF16)
                grad_ff_ref[layer, 1, cc, r] = dot_nn(gbranch_t, active.astype(BF16)).astype(BF16)
                grad_inner_ref[layer, cc, r] = jnp.sum(
                    ginner.astype(F32), axis=0, keepdims=True
                )
                gmiddle = gmiddle + dot_nt(ginner, ff_w[0, cc, r])
        rows = [jnp.sum(gsum, axis=0, keepdims=True)]
        gsum, ggain_one, goffset_one = norm_backward(
            gmiddle, normed_one_ref[layer], inverse_one_ref[layer], norm_ref[0, layer : layer + 1, :]
        )
        rows = [ggain_one, goffset_one, ggain, goffset] + rows
        for i, row in enumerate(rows):
            at = 8 * layer + i
            grad_norm_ref[at // 2, at % 2 : at % 2 + 1, :] = row
        grad_ref[...] = gsum

    def prepare(layer):
        gattended = grad_ref[...].astype(BF16)
        wide = dot_nn(transposed(mixed_ref[layer]).astype(BF16), gattended).astype(BF16)
        grad_att_ref[layer, 4] = wide.reshape(2, 4, HD, D)
        sums.pair(5 + layer)
        load_att.wait()
        gmix = dot_nt(gattended, att_w[4].reshape(D, D))
        gmix_ref[...] = gmix.astype(BF16)
        gmix_t_ref[...] = gmix.T.astype(BF16)
        query_t_ref[...] = transposed(query_u_ref[layer]).astype(BF16)
        flip_t_ref[...] = dot_nn(transposed(query_w_ref[layer]).astype(BF16), flip).astype(BF16)
        key_w, value_w = att_w[1].reshape(D, D), att_w[2].reshape(D, D)
        for half in range(2):
            rows = memory_w[layer] if half == 0 else low_ref[layer]
            cols = slice(half * SEG, (half + 1) * SEG)
            values_ref[:, cols] = dot_nt(value_w, rows).astype(BF16)
            keys = dot_nt(rows, key_w).astype(BF16)
            keys_ref[0, cols, :] = keys[:, 0:256]
            keys_ref[1, cols, :] = keys[:, 256:512]
        rel = dot_nt(table_ref[...], att_w[3].reshape(D, D)).astype(BF16)
        rel_ref[0] = rel[:, 0:256]
        rel_ref[1] = rel[:, 256:512]
        gquery_ref[...] = jnp.zeros_like(gquery_ref)

    def fetch(layer, n, slot):
        h = (n + 4) % HEADS
        return pltpu.make_async_copy(prob_hbm.at[layer, h], prob_ref.at[slot], prob_sem.at[slot])

    def head(layer):
        def run(n, carry):
            h = (n + 4) % HEADS
            group = h // 4
            slot = n % 2
            mine = lane_head == h % 4
            lanes = pl.ds(pl.multiple_of(group * 256, 256), 256)
            row = pl.ds(pl.multiple_of(h * HD, HD), HD)
            gmix_h = jnp.where(mine, gmix_ref[:, lanes].astype(F32), 0.0).astype(BF16)
            prob_grad_ref[...] = dot_nn(gmix_h, values_ref[lanes, :])
            fetch(layer, n, slot).wait()
            for b in range(0, OWN, ROWS):
                rows = slice(b, b + ROWS)
                prob = prob_ref[slot, rows, :]
                gprob = prob_grad_ref[rows, :]
                inner = jnp.sum(prob * gprob, axis=-1, keepdims=True)
                score_grad_ref[rows, :] = (prob * (gprob - inner)).astype(BF16)
                low_prob_ref[rows, :] = prob.astype(BF16)

            @pl.when(n < HEADS - 2)
            def _():
                fetch(layer, n + 2, slot).start()

            if layer == 1:
                @pl.when(n >= HEADS - 2)
                def _():
                    fetch(0, n + 2 - HEADS, slot).start()

            sgrad = score_grad_ref[...]
            gquery_ref[0, group] = gquery_ref[0, group] + jnp.where(
                mine, dot_nn(sgrad, keys_ref[group]), 0.0
            )
            gkey = dot_nn(query_t_ref[row, :], sgrad) * SCALE
            gvalue = dot_nn(gmix_t_ref[row, :], low_prob_ref[...])
            gmemory_ref[0, row, :] = gkey[:, 0:SEG].astype(BF16)
            gmemory_ref[1, row, :] = gvalue[:, 0:SEG].astype(BF16)
            ghidden_ref[0, row, :] = gkey[:, SEG:]
            ghidden_ref[1, row, :] = gvalue[:, SEG:]
            flipped = dot_nn(flip, sgrad).astype(BF16)
            flipped_ref[...] = pltpu.roll(flipped, KLEN - OWN + 1, 1, stride=1, stride_axis=0)
            gquery_ref[1, group] = gquery_ref[1, group] + jnp.where(
                mine, dot_nn(flipped_ref[...], rel_ref[group]), 0.0
            )
            grel_ref[row, :] = (dot_nn(flip_t_ref[row, :], flipped_ref[...]) * SCALE).astype(BF16)
            return carry

        return run

    def swap(layer, i):
        return send(
            ghidden_ref.at[:, 256 * i : 256 * i + 256, their_rows],
            got_ref.at[:, 256 - 256 * i : 512 - 256 * i],
            extra,
            10 + 2 * layer + i,
            here.sibling(),
        )

    def half(layer, group):
        own_low = low_ref[layer, own_rows, :]
        lanes = slice(group * 256, (group + 1) * 256)
        gquery_u = (gquery_ref[0, group] * SCALE).astype(BF16)
        gquery_w = dot_nn(flip, (gquery_ref[1, group] * SCALE).astype(BF16))
        grad_bias_ref[layer, 0:1, lanes] = jnp.sum(gquery_u.astype(F32), axis=0, keepdims=True)
        grad_bias_ref[layer, 1:2, lanes] = jnp.sum(gquery_w, axis=0, keepdims=True)
        gquery = gquery_u.astype(F32) + gquery_w
        grad_att_ref[layer, 0, group] = (
            dot_nn(gquery.T.astype(BF16), own_low).astype(BF16).reshape(4, HD, D)
        )
        grad_att_ref[layer, 3, group] = (
            dot_nn(grel_ref[lanes, :], table_ref[...]).astype(BF16).reshape(4, HD, D)
        )
        for i in range(2):
            part = dot_nn(gmemory_ref[i, lanes, :], memory_w[layer]) + dot_nn(
                ghidden_ref[i, lanes, :].astype(BF16), low_ref[layer]
            )
            grad_att_ref[layer, 1 + i, group] = part.astype(BF16).reshape(4, HD, D)
        return dot_nn(gquery.astype(BF16), att_w[0, group].reshape(256, D))

    def finish(swaps):
        for copy in swaps:
            copy.wait_recv()
        for i in range(2):
            total = (ghidden_ref[i, :, own_rows] + got_ref[i]).astype(BF16)
            grad_ref[...] += dot_nn(transposed(total).astype(BF16), att_w[1 + i].reshape(D, D))

    fetch(1, 0, 0).start()
    fetch(1, 1, 1).start()
    feed(1)
    load_ff = pltpu.make_async_copy(ff_hbm.at[0], ff_w, load_sem.at[0])
    load_ff.start()
    spread_ce(0)
    for copy in loads:
        copy.wait()
    prepare(1)
    sums.one(3)
    sums.one(6)
    lax.fori_loop(0, 4, head(1), 0)
    swaps_one = [swap(1, 1)]
    grad_ref[...] += half(1, 1)
    sums.pair(2)
    lax.fori_loop(4, HEADS, head(1), 0)
    swaps_one.append(swap(1, 0))
    load_normed = pltpu.make_async_copy(
        normed_two_hbm.at[0], prob_grad_ref.at[:, 0:D], load_sem.at[7]
    )
    load_normed.start()
    spread_ce(1)
    grad_ref[...] += half(1, 0)
    sums.one(2)
    sums.two(3)
    sums.two(6)
    finish(swaps_one)
    load_att = pltpu.make_async_copy(att_hbm.at[0], att_w, load_sem.at[1])
    load_att.start()
    feed(0)
    spread_ce(2)
    for copy in swaps_one:
        copy.wait_send()
    prepare(0)
    sums.one(1)
    sums.one(5)
    sums.two(2)
    lax.fori_loop(0, 4, head(0), 0)
    swaps_zero = [swap(0, 1)]
    grad_ref[...] += half(0, 1)
    sums.pair(0)
    sums.three(3)
    sums.three(6)
    lax.fori_loop(4, HEADS, head(0), 0)
    swaps_zero.append(swap(0, 0))
    grad_ref[...] += half(0, 0)
    sums.one(0)
    sums.two(1)
    sums.two(5)
    sums.three(2)
    finish(swaps_zero)

    tokens = inputs_ref[pl.ds(here.y, 1), own_rows]
    onehot = jnp.where(
        tokens == lax.broadcasted_iota(jnp.int32, (VOCAB, OWN), 0), 1.0, 0.0
    ).astype(BF16)
    grad = grad_ref[...]
    high = grad.astype(BF16)
    rest = (grad - high.astype(F32)).astype(BF16)
    ranked_ref[...] += (dot_nn(onehot, high) + dot_nn(onehot, rest)).reshape(MP, 32, D)
    block_ref[...] = jnp.zeros_like(block_ref)
    for cc in range(2):
        for r in range(4):
            device = ((here.y + r) % 4) * 2 + (here.core + cc) % 2
            first = (cc * 4 + r) * HD
            block_ref[0:32, :] = ranked_ref[device]
            block_ref[32:34, :] = grad_norm_ref[device]
            block_ref[34:35, 0:256] = jnp.concatenate(
                [
                    grad_bias_ref[l, k : k + 1, first : first + HD]
                    for l in range(2)
                    for k in range(2)
                ],
                axis=1,
            )
            block_ref[35:36, :] = jnp.concatenate(
                [grad_inner_ref[l, cc, r] for l in range(2)], axis=1
            )
            grad_small_ref[0, 0, cc, r] = block_ref[...].astype(BF16)
    sums.pair(4)
    sums.four(3)
    sums.four(6)
    sums.one(4)
    sums.two(0)
    sums.three(1)
    sums.three(5)
    sums.two(4)
    sums.four(2)
    sums.three(0)
    sums.three(4)
    sums.four(1)
    sums.four(5)
    for copy in ce_copies[-3:]:
        copy.wait_recv()
    ce_out[...] = (ce_x[0] + ce_x[1]) + (ce_x[2] + ce_x[3])
    sums.four(4)
    sums.four(0)
    sums.arrived(4, 4)
    small_out[here.y, here.core] = small_own[0, 0]
    piece = small_out.at[here.y, here.core]
    small_copies = [send(piece, piece, extra, 13 + r, here.along("y", r)) for r in (1, 2, 3)]
    for copy in small_copies:
        copy.wait_recv()
    piece = small_out.at[:, here.core]
    last = send(piece, piece, extra, 17, here.sibling())
    for g in (3, 6, 2, 1, 5, 0):
        sums.arrived(4, g)
    last.wait()
    for copy in ce_copies + swaps_zero + small_copies:
        copy.wait_send()
    sums.end()


def backward_all(*operands):
    vmem, hbm = VMEM_SPEC, ANY_SPEC
    outs = [
        ((2, 5, HD, D), BF16),
        ((2, 2, D, 256), BF16),
        ((4, 2, 64, D), BF16),
        ((8, 128), F32),
    ]
    scratch = [
        pltpu.VMEM((5, 2, 4, HD, D), BF16),
        pltpu.VMEM((2, 2, 4, D, 256), BF16),
        pltpu.VMEM((2, SEG, D), BF16),
        pltpu.VMEM((KLEN, D), BF16),
        pltpu.VMEM((2, OWN, KLEN), F32),
        pltpu.VMEM((2, 5, 2, 4, HD, D), BF16),
        pltpu.VMEM((2, 2, 2, 4, D, 256), BF16),
        pltpu.VMEM((1, 1, 2, 4, 64, D), BF16),
        pltpu.VMEM((OWN, D), F32),
        pltpu.VMEM((2, KLEN, 256), BF16),
        pltpu.VMEM((D, KLEN), BF16),
        pltpu.VMEM((2, KLEN, 256), BF16),
        pltpu.VMEM((OWN, D), BF16),
        pltpu.VMEM((D, OWN), BF16),
        pltpu.VMEM((D, OWN), BF16),
        pltpu.VMEM((D, OWN), BF16),
        pltpu.VMEM((OWN, KLEN), F32),
        pltpu.VMEM((OWN, KLEN), BF16),
        pltpu.VMEM((OWN, KLEN), BF16),
        pltpu.VMEM((OWN, KLEN), BF16),
        pltpu.VMEM((2, 2, OWN, 256), F32),
        pltpu.VMEM((2, D, SEG), BF16),
        pltpu.VMEM((2, D, SEG), F32),
        pltpu.VMEM((2, D, OWN), F32),
        pltpu.VMEM((D, KLEN), BF16),
        pltpu.VMEM((2, 2, D), F32),
        pltpu.VMEM((2, 2, 4, 1, 256), F32),
        pltpu.VMEM((MP, 2, D), F32),
        pltpu.VMEM((MP, 32, D), F32),
        pltpu.VMEM((64, D), F32),
        pltpu.VMEM((2, 8, 128), F32),
        pltpu.VMEM((4, 8, 128), F32),
        pltpu.VMEM((4, 8, 128), F32),
        pltpu.VMEM((4, 8, 128), F32),
        pltpu.VMEM((1, 1, 64, D), BF16),
    ]
    scratch += [pltpu.VMEM((hi - lo, 4) + SHAPES[k], BF16) for k, _, (lo, hi), _, _ in SUM_GROUPS]
    for kind, _, _, parts, rows in SUM_GROUPS:
        width = SHAPES[kind][1]
        scratch += [pltpu.VMEM((3, hi - lo, 4, rows, width), BF16) for _, lo, hi in parts]
        scratch += [pltpu.VMEM((3, hi - lo, rows, width), BF16) for _, lo, hi in parts]
        scratch += [pltpu.VMEM((4, hi - lo, rows, width), BF16) for _, lo, hi in parts]
    for n in (7, 42, 42, 42, 42, 18):
        scratch += [pltpu.SemaphoreType.DMA((n,)), pltpu.SemaphoreType.DMA((n,))]
    scratch += [pltpu.SemaphoreType.DMA((8,)), pltpu.SemaphoreType.DMA((2,))]
    return pl.pallas_call(
        backward_step,
        out_shape=[jax.ShapeDtypeStruct(s, t) for s, t in outs],
        in_specs=[hbm] * 8 + [vmem] * 11,
        out_specs=[vmem] * 4,
        scratch_shapes=scratch,
        compiler_params=pltpu.CompilerParams(
            collective_id=1, has_side_effects=True, vmem_limit_bytes=63 * 1024 * 1024
        ),
        name="backward_all",
    )(*operands)


def advance_one(grad, weight, moment):
    moment_next = MOMENTUM * moment + grad
    return moment_next, grad + MOMENTUM * moment_next


def masked(grad, weight, rank):
    coefficient = jnp.where(rank < 1.5, 1.0, jnp.where(rank < 2.5, WIDEN, 0.0))
    return jnp.where(rank < 2.5, grad, 0.0) + (2.0 * PENALTY) * weight * coefficient


def square_sum(value):
    return jnp.sum(value * value, axis=0, keepdims=True)


def moments_kernel(
    att_w_hbm,
    att_m_hbm,
    ff_w_hbm,
    ff_m_hbm,
    new_memory_hbm,
    att_sum_ref,
    ff_sum_ref,
    small_ref,
    att_rank_ref,
    ff_rank_ref,
    embedding_m_ref,
    head_w_ref,
    head_m_ref,
    inner_w_ref,
    inner_m_ref,
    norm_m_ref,
    att_g_hbm,
    att_m_out,
    ff_g_hbm,
    ff_m_out,
    new_memory_out,
    embedding_g_ref,
    embedding_m_out,
    head_g_ref,
    head_m_out,
    inner_g_ref,
    inner_m_out,
    norm_g_ref,
    norm_m_out,
    part_ref,
    att_w,
    att_m,
    att_g,
    ff_w,
    ff_m,
    ff_g,
    att_rank,
    ff_rank,
    memory_ref,
    load_sem,
    store_sem,
    memory_sem,
):
    loads, stores = [], []
    for l in range(2):
        for i, (source, target) in enumerate(
            ((ff_w_hbm, ff_w), (ff_m_hbm, ff_m), (att_w_hbm, att_w), (att_m_hbm, att_m))
        ):
            copy = pltpu.make_async_copy(source.at[l], target.at[l], load_sem.at[4 * l + i])
            copy.start()
            loads.append(copy)
    memory_in = pltpu.make_async_copy(new_memory_hbm, memory_ref, memory_sem.at[0])
    memory_in.start()
    att_rank[...] = spread_rank(att_rank_ref[...], D)
    ff_rank[...] = spread_rank(ff_rank_ref[...], 256)

    small = small_ref[lax.axis_index("mp") // 2, lax.axis_index("mp") % 2].astype(F32)
    head_sums = [jnp.zeros((1, HD), F32)] * 2
    inner_sums = [jnp.zeros((1, 256), F32)] * 2
    for l in range(2):
        for k in range(2):
            at = (l * 2 + k) * HD
            grad = small[34:35, at : at + HD]
            head_g_ref[l, k : k + 1, :] = grad
            weight = head_w_ref[l, k : k + 1, :]
            moment, direction = advance_one(grad, weight, head_m_ref[l, k : k + 1, :])
            head_m_out[l, k : k + 1, :] = moment
            head_sums[0] = head_sums[0] + weight * weight
            head_sums[1] = head_sums[1] + direction * direction
        grad = small[35:36, l * 256 : (l + 1) * 256]
        inner_g_ref[l : l + 1, :] = grad
        weight = inner_w_ref[l : l + 1, :]
        moment, direction = advance_one(grad, weight, inner_m_ref[l : l + 1, :])
        inner_m_out[l : l + 1, :] = moment
        inner_sums[0] = inner_sums[0] + weight * weight
        inner_sums[1] = inner_sums[1] + direction * direction
        for i in range(5):
            at = 8 * l + i
            grad = small_ref[at // 4, at // 2 % 2, 32:34, :].astype(F32)[at % 2 : at % 2 + 1]
            norm_g_ref[i, l : l + 1, :] = grad
            norm_m_out[i, l : l + 1, :] = MOMENTUM * norm_m_ref[i, l : l + 1, :] + grad
    for m in range(MP):
        rows = slice(m * 32, (m + 1) * 32)
        grad = small_ref[m // 2, m % 2, 0:32, :].astype(F32)
        embedding_g_ref[rows, :] = grad
        embedding_m_out[rows, :] = MOMENTUM * embedding_m_ref[rows, :] + grad

    ff_sums = (jnp.zeros((1, 256), F32), jnp.zeros((1, 256), F32))
    att_sums = (jnp.zeros((1, D), F32), jnp.zeros((1, D), F32))
    for l in range(2):
        loads[4 * l].wait()
        loads[4 * l + 1].wait()

        def ff_block(i, sums):
            mat = i // 8
            rows = pl.ds(pl.multiple_of(i % 8 * 64, 64), 64)
            weight = ff_w[l, mat, rows, :]
            rank = ff_rank[pl.ds(l * 16 + i, 1), :]
            grad = masked(ff_sum_ref[l, mat, rows, :].astype(F32), weight, rank)
            moment, direction = advance_one(grad, weight, ff_m[l, mat, rows, :])
            ff_g[l, mat, rows, :] = grad
            ff_m[l, mat, rows, :] = moment
            return sums[0] + square_sum(weight), sums[1] + square_sum(direction)

        ff_sums = lax.fori_loop(0, 16, ff_block, ff_sums)
        for i, (source, target) in enumerate(((ff_g, ff_g_hbm), (ff_m, ff_m_out))):
            copy = pltpu.make_async_copy(source.at[l], target.at[l], store_sem.at[4 * l + i])
            copy.start()
            stores.append(copy)
        loads[4 * l + 2].wait()
        loads[4 * l + 3].wait()

        def att_block(i, sums):
            weight = att_w[l, i]
            rank = att_rank[pl.ds(l * 5 + i, 1), :]
            grad = masked(att_sum_ref[l, i].astype(F32), weight, rank)
            moment, direction = advance_one(grad, weight, att_m[l, i])
            att_g[l, i] = grad
            att_m[l, i] = moment
            return sums[0] + square_sum(weight), sums[1] + square_sum(direction)

        att_sums = lax.fori_loop(0, 5, att_block, att_sums)
        for i, (source, target) in enumerate(((att_g, att_g_hbm), (att_m, att_m_out))):
            copy = pltpu.make_async_copy(source.at[l], target.at[l], store_sem.at[4 * l + 2 + i])
            copy.start()
            stores.append(copy)
    for k in range(2):
        for i, sums in enumerate((att_sums, ff_sums, head_sums, inner_sums)):
            part_ref[4 * k + i : 4 * k + i + 1, :] = jnp.broadcast_to(
                jnp.sum(sums[k], axis=1, keepdims=True), (1, 128)
            )
    memory_in.wait()
    memory_back = pltpu.make_async_copy(memory_ref, new_memory_out, memory_sem.at[1])
    memory_back.start()
    for copy in stores:
        copy.wait()
    memory_back.wait()


def moments(*operands):
    att, ff = (2, 5, HD, D), (2, 2, D, 256)
    outs = [
        (ANY_SPEC, att, F32),
        (ANY_SPEC, att, F32),
        (ANY_SPEC, ff, F32),
        (ANY_SPEC, ff, F32),
        (ANY_SPEC, (2, 4, SEG, D), BF16),
    ] + [
        (VMEM_SPEC, shape, F32)
        for shape in (
            (VOCAB, D),
            (VOCAB, D),
            (2, 2, HD),
            (2, 2, HD),
            (2, 256),
            (2, 256),
            (5, 2, D),
            (5, 2, D),
            (8, 128),
        )
    ]
    return pl.pallas_call(
        moments_kernel,
        out_shape=[jax.ShapeDtypeStruct(s, t) for _, s, t in outs],
        in_specs=[ANY_SPEC] * 5 + [VMEM_SPEC] * 11,
        out_specs=[m for m, _, _ in outs],
        scratch_shapes=[pltpu.VMEM(att, F32)] * 3
        + [pltpu.VMEM(ff, F32)] * 3
        + [
            pltpu.VMEM((10, D), F32),
            pltpu.VMEM((32, 256), F32),
            pltpu.VMEM((2, 4, SEG, D), BF16),
            pltpu.SemaphoreType.DMA((8,)),
            pltpu.SemaphoreType.DMA((8,)),
            pltpu.SemaphoreType.DMA((2,)),
        ],
        compiler_params=pltpu.CompilerParams(vmem_limit_bytes=62 * 1024 * 1024),
        name="moments",
    )(*operands)


def exchange_kernel(part_ref, out_ref, send_sem, recv_sem):
    here = Place()
    partners = [
        here.device(y=(here.y + s) % 4, core=(here.core + k) % 2)
        for s in range(4)
        for k in range(2)
        if s or k
    ]
    barrier = pltpu.get_barrier_semaphore()
    for partner in partners:
        pl.semaphore_signal(barrier, inc=1, device_id=partner, device_id_type=MESH)
    pl.semaphore_wait(barrier, len(partners))
    index = here.y * 2 + here.core
    out_ref[index] = part_ref[...]
    copies = [
        send(part_ref, out_ref.at[index], (send_sem, recv_sem), i, partner)
        for i, partner in enumerate(partners)
    ]
    for copy in copies:
        copy.wait()


def exchange(part):
    return pl.pallas_call(
        exchange_kernel,
        out_shape=jax.ShapeDtypeStruct((MP, 8, 128), F32),
        in_specs=[VMEM_SPEC],
        out_specs=VMEM_SPEC,
        scratch_shapes=[pltpu.SemaphoreType.DMA((7,)), pltpu.SemaphoreType.DMA((7,))],
        compiler_params=pltpu.CompilerParams(
            collective_id=2, has_side_effects=True, vmem_limit_bytes=62 * 1024 * 1024
        ),
        name="exchange",
    )(part)


def weights_kernel(*refs):
    inputs, outputs, scratch = refs[:25], refs[25:37], refs[37:]
    parts_ref = inputs[24]
    groups = [inputs[4 * i : 4 * i + 4] for i in range(6)]
    results = [outputs[2 * i : 2 * i + 2] for i in range(6)]
    buffers = [scratch[0:4], scratch[4:8]]
    load_sem, store_sem = scratch[8:10]
    loads = [
        [
            [
                pltpu.make_async_copy(
                    groups[g][i].at[l], buffers[g][i].at[l], load_sem.at[8 * g + 4 * l + i]
                )
                for i in range(4)
            ]
            for l in range(2)
        ]
        for g in range(2)
    ]
    for l in range(2):
        for g in (1, 0):
            for copy in loads[g][l]:
                copy.start()
    total = parts_ref[0]
    for m in range(1, MP):
        total = total + parts_ref[m]

    def rate(weight_square, direction_square):
        return RATE * (jnp.sqrt(weight_square) / jnp.sqrt(direction_square))

    def step(weight, grad, moment, average, ratio):
        weight_next = weight - ratio * (grad + MOMENTUM * moment)
        return weight_next, AVERAGE * average + (1.0 - AVERAGE) * weight_next

    ratios = [rate(total[i : i + 1, 0:1], total[4 + i : 5 + i, 0:1]) for i in range(4)]
    for l in range(2):
        for k in range(2):
            row = (l, slice(k, k + 1))
            new, mean = step(*[ref[row] for ref in groups[2]], ratios[2])
            results[2][0][row] = new
            results[2][1][row] = mean
    new, mean = step(*[ref[...] for ref in groups[3]], ratios[3])
    results[3][0][...] = new
    results[3][1][...] = mean
    squares = [jnp.zeros((1, D), F32), jnp.zeros((1, D), F32)]
    for b in range(4):
        rows = slice(b * 64, (b + 1) * 64)
        squares[0] = squares[0] + square_sum(groups[4][0][rows, :])
        squares[1] = squares[1] + square_sum(
            groups[4][1][rows, :] + MOMENTUM * groups[4][2][rows, :]
        )
    ratio = rate(*[jnp.sum(value, axis=1, keepdims=True) for value in squares])
    for b in range(4):
        rows = slice(b * 64, (b + 1) * 64)
        new, mean = step(*[ref[rows, :] for ref in groups[4]], ratio)
        results[4][0][rows, :] = new
        results[4][1][rows, :] = mean
    squares = [jnp.zeros((2, D), F32), jnp.zeros((2, D), F32)]
    for i in range(5):
        direction = groups[5][1][i] + MOMENTUM * groups[5][2][i]
        squares[0] = squares[0] + groups[5][0][i] * groups[5][0][i]
        squares[1] = squares[1] + direction * direction
    ratio = rate(
        *[jnp.sum(square_sum_rows(value), axis=1, keepdims=True) for value in squares]
    )
    for i in range(5):
        new, mean = step(*[ref[i] for ref in groups[5]], ratio)
        results[5][0][i] = new
        results[5][1][i] = mean

    stores = []
    for l in range(2):
        for g in (1, 0):
            for copy in loads[g][l]:
                copy.wait()
            weight, grad, moment, average = buffers[g]
            if g == 0:

                def block(i, carry):
                    new, mean = step(
                        weight[l, i], grad[l, i], moment[l, i], average[l, i], ratios[0]
                    )
                    weight[l, i] = new
                    average[l, i] = mean
                    return carry

                lax.fori_loop(0, 5, block, 0)
            else:

                def block(i, carry):
                    mat = i // 8
                    rows = pl.ds(pl.multiple_of(i % 8 * 64, 64), 64)
                    new, mean = step(
                        weight[l, mat, rows, :],
                        grad[l, mat, rows, :],
                        moment[l, mat, rows, :],
                        average[l, mat, rows, :],
                        ratios[1],
                    )
                    weight[l, mat, rows, :] = new
                    average[l, mat, rows, :] = mean
                    return carry

                lax.fori_loop(0, 16, block, 0)
            for k, source in enumerate((weight, average)):
                copy = pltpu.make_async_copy(
                    source.at[l], results[g][k].at[l], store_sem.at[4 * g + 2 * l + k]
                )
                copy.start()
                stores.append(copy)
    for copy in stores:
        copy.wait()


def square_sum_rows(value):
    return jnp.sum(value, axis=0, keepdims=True)


def new_weights(*operands):
    att, ff = (2, 5, HD, D), (2, 2, D, 256)
    shapes = [att, ff, (2, 2, HD), (2, 256), (VOCAB, D), (5, 2, D)]
    return pl.pallas_call(
        weights_kernel,
        out_shape=[jax.ShapeDtypeStruct(s, F32) for s in shapes for _ in range(2)],
        in_specs=[ANY_SPEC] * 8 + [VMEM_SPEC] * 17,
        out_specs=[ANY_SPEC] * 4 + [VMEM_SPEC] * 8,
        scratch_shapes=[pltpu.VMEM(att, F32)] * 4
        + [pltpu.VMEM(ff, F32)] * 4
        + [pltpu.SemaphoreType.DMA((16,)), pltpu.SemaphoreType.DMA((8,))],
        compiler_params=pltpu.CompilerParams(vmem_limit_bytes=62 * 1024 * 1024),
        name="new_weights",
    )(*operands)


def body(
    inputs,
    targets,
    valid_mask,
    memory,
    attention_rank,
    feedforward_rank,
    attention_weight,
    attention_moment,
    attention_average,
    feedforward_weight,
    feedforward_moment,
    feedforward_average,
    embedding_weight,
    embedding_moment,
    embedding_average,
    head_bias_weight,
    head_bias_moment,
    head_bias_average,
    inner_bias_weight,
    inner_bias_moment,
    inner_bias_average,
    norm_weight,
    norm_moment,
    norm_average,
):
    def turned(value):
        return value.transpose(0, 1, 3, 2)

    def swapped(value):
        return value.transpose(1, 0, 2)

    att_rank = attention_rank.reshape(10, 8).astype(F32)
    ff_rank = feedforward_rank.reshape(32, 4).astype(F32)
    table = tables()
    (
        att_got,
        ff_got,
        new_memory,
        probs,
        bias_got,
        count_got,
        lows,
        query_u,
        query_w,
        mixed,
        normed_one,
        inverse_one,
        normed_two,
        inverse_two,
        grad_hidden,
        grad_embedding,
        ce_local,
    ) = forward_all(
        turned(attention_weight),
        feedforward_weight,
        att_rank,
        ff_rank,
        head_bias_weight,
        inner_bias_weight,
        embedding_weight,
        inputs,
        targets,
        valid_mask,
        memory,
        swapped(norm_weight),
        table,
    )
    valid_count = count_got[0, 0]
    grad_attention, grad_feedforward, grad_small, ce_got = backward_all(
        att_got,
        ff_got,
        probs,
        memory,
        table,
        grad_hidden,
        grad_embedding,
        normed_two,
        bias_got,
        swapped(norm_weight),
        inputs,
        ce_local,
        lows,
        query_u,
        query_w,
        mixed,
        normed_one,
        inverse_one,
        inverse_two,
    )
    ce_total = ce_got[0, 0]
    (
        att_grad,
        att_moment,
        ff_grad,
        ff_moment,
        new_memory,
        embedding_grad,
        embedding_moment_next,
        head_grad,
        head_moment,
        inner_grad,
        inner_moment,
        norm_grad,
        norm_moment_next,
        part,
    ) = moments(
        turned(attention_weight),
        turned(attention_moment),
        feedforward_weight,
        feedforward_moment,
        new_memory,
        grad_attention,
        grad_feedforward,
        grad_small,
        att_rank,
        ff_rank,
        embedding_moment,
        head_bias_weight,
        head_bias_moment,
        inner_bias_weight,
        inner_bias_moment,
        swapped(norm_moment),
    )
    parts = exchange(part)
    (
        att_next,
        att_average,
        ff_next,
        ff_average,
        head_next,
        head_average,
        inner_next,
        inner_average,
        embedding_next,
        embedding_average_next,
        norm_next,
        norm_average_next,
    ) = new_weights(
        turned(attention_weight),
        att_grad,
        att_moment,
        turned(attention_average),
        feedforward_weight,
        ff_grad,
        ff_moment,
        feedforward_average,
        head_bias_weight,
        head_grad,
        head_moment,
        head_bias_average,
        inner_bias_weight,
        inner_grad,
        inner_moment,
        inner_bias_average,
        embedding_weight,
        embedding_grad,
        embedding_moment_next,
        embedding_average,
        swapped(norm_weight),
        norm_grad,
        norm_moment_next,
        swapped(norm_average),
        parts,
    )
    return (
        ce_total,
        valid_count,
        new_memory,
        turned(att_grad),
        turned(att_next),
        turned(att_moment),
        turned(att_average),
        ff_grad,
        ff_next,
        ff_moment,
        ff_average,
        embedding_next,
        embedding_moment_next,
        embedding_average_next,
        head_next,
        head_moment,
        head_average,
        inner_next,
        inner_moment,
        inner_average,
        swapped(norm_grad),
        swapped(norm_next),
        swapped(norm_moment_next),
        swapped(norm_average_next),
    )


def solution(mesh):
    rows = P("dp", None)
    matrix = P(None, None, None, "mp")
    split_two = P(None, None, "mp")
    split_one = P(None, "mp")
    whole = P()
    return jax.shard_map(
        body,
        mesh=mesh,
        in_specs=(
            (rows,) * 3
            + (P(None, "dp", None, None),)
            + (matrix,) * 8
            + (whole,) * 3
            + (split_two,) * 3
            + (split_one,) * 3
            + (whole,) * 3
        ),
        out_specs=(
            (whole,) * 2
            + (P(None, "dp", None, None),)
            + (matrix,) * 8
            + (whole,) * 3
            + (split_two,) * 3
            + (split_one,) * 3
            + (whole,) * 4
        ),
        check_vma=False,
    )
```

```python
import functools

import jax
import jax.numpy as jnp
import numpy as np
from jax import lax
from jax.experimental import pallas as pl
from jax.experimental.pallas import tpu as pltpu
from jax.sharding import PartitionSpec as P

HD = 64
D = 512
FF = 2048
SEG = 512
KLEN = 1024
OWN = 256
HEADS = 8
VOCAB = 256
MP = 8

EPSILON = 1e-05
MOMENTUM = 0.9
AVERAGE = 0.9
RATE = 0.3
PENALTY = 0.0001
WIDEN = 5.0
F32 = jnp.float32
BF16 = jnp.bfloat16
SCALE = HD ** (-0.5)


def dot_nn(a, b):
    return lax.dot_general(a, b, (((1,), (0,)), ((), ())), preferred_element_type=F32)


def dot_nt(a, b):
    return lax.dot_general(a, b, (((1,), (1,)), ((), ())), preferred_element_type=F32)


def smooth_unit(v):
    return 0.5 * v * (1.0 + jnp.tanh(0.7978845608028654 * (v + 0.044715 * v * v * v)))


def smooth_both(v):
    squared = v * v
    t = jnp.tanh(0.7978845608028654 * (v + 0.044715 * squared * v))
    half = 0.5 * (1.0 + t)
    slope = half + 0.5 * v * (1.0 - t * t) * (
        0.7978845608028654 * (1.0 + 3.0 * 0.044715 * squared)
    )
    return v * half, slope


def tables():
    freq = (1.0 / 10000.0 ** (np.arange(0, D, 2).astype(np.float32) / np.float32(D))).astype(
        np.float32
    )
    turned = []
    for half in range(2):
        distance = (SEG + half * OWN - np.arange(KLEN)) % KLEN
        angle = (distance.astype(np.float32)[:, None] * freq[None, :]).astype(np.float64)
        turned.append(np.concatenate([np.sin(angle), np.cos(angle)], axis=1).astype(np.float32))
    return jnp.asarray(np.stack(turned), BF16)


def norm_forward(values):
    centred = values - jnp.mean(values, axis=-1, keepdims=True)
    inverse = lax.rsqrt(jnp.mean(centred * centred, axis=-1, keepdims=True) + EPSILON)
    return centred * inverse, inverse


def norm_backward(grad, normed, inverse, gain):
    scaled = grad * gain
    grad_in = inverse * (
        scaled
        - jnp.mean(scaled, axis=-1, keepdims=True)
        - normed * jnp.mean(scaled * normed, axis=-1, keepdims=True)
    )
    return (
        grad_in,
        jnp.sum(grad * normed, axis=0, keepdims=True),
        jnp.sum(grad, axis=0, keepdims=True),
    )


def transposed(value):
    return value.astype(F32).T


ROWS = 64
VMEM_SPEC = pl.BlockSpec(memory_space=pltpu.VMEM)
VMEM_LIMIT = 60 * 1024 * 1024


ANY_SPEC = pl.BlockSpec(memory_space=pl.ANY)
MESH = pl.DeviceIdType.MESH

ATT, FFN, SMALL = 0, 1, 2
GROUPS = (
    (ATT, 0, (("z", 0, 3), ("x", 3, 5)), 16),
    (FFN, 0, (("z", 0, 1), ("x", 1, 2)), 128),
    (ATT, 1, (("z", 0, 2), ("x", 2, 5)), 16),
    (FFN, 1, (("z", 0, 1), ("x", 1, 2)), 128),
)
SUM_GROUPS = (
    (ATT, 0, (0, 4), (("z", 0, 2), ("x", 2, 4)), 16),
    (FFN, 0, (0, 2), (("z", 0, 1), ("x", 1, 2)), 128),
    (ATT, 1, (0, 4), (("z", 0, 2), ("x", 2, 4)), 16),
    (FFN, 1, (0, 2), (("z", 0, 1), ("x", 1, 2)), 128),
    (SMALL, 0, (0, 1), (("z", 0, 1),), 16),
    (ATT, 0, (4, 5), (("z", 0, 1),), 16),
    (ATT, 1, (4, 5), (("x", 0, 1),), 16),
)


class Place:
    def __init__(self):
        dp, mp = lax.axis_index("dp"), lax.axis_index("mp")
        self.x, self.z = dp // 4, dp % 4
        self.y, self.core = mp // 2, mp % 2

    def device(self, x=None, z=None, y=None, core=None):
        x = self.x if x is None else x
        z = self.z if z is None else z
        y = self.y if y is None else y
        core = self.core if core is None else core
        return {"dp": x * 4 + z, "mp": y * 2 + core}

    def along(self, axis, shift):
        return self.device(**{axis: (getattr(self, axis) + shift + 4) % 4})

    def sibling(self):
        return self.device(core=1 - self.core)

    def greet(self, more=()):
        partners = [self.along(axis, s) for axis in "xzy" for s in (1, 2, 3)]
        partners += [self.sibling(), *more]
        barrier = pltpu.get_barrier_semaphore()
        for partner in partners:
            pl.semaphore_signal(barrier, inc=1, device_id=partner, device_id_type=MESH)

    def greeted(self, count=10):
        pl.semaphore_wait(pltpu.get_barrier_semaphore(), count)


def send(source, target, sems, index, device):
    copy = pltpu.make_async_remote_copy(
        src_ref=source,
        dst_ref=target,
        send_sem=sems[0].at[index],
        recv_sem=sems[1].at[index],
        device_id=device,
        device_id_type=MESH,
    )
    copy.start()
    return copy


def spread_rank(rank, width):
    blocks = rank.shape[1]
    lane = lax.broadcasted_iota(jnp.int32, (blocks, width), 1) // (width // blocks)
    row = lax.broadcasted_iota(jnp.int32, (blocks, width), 0)
    return dot_nn(rank, jnp.where(lane == row, 1.0, 0.0))


def advance_one(grad, weight, moment):
    moment_next = MOMENTUM * moment + grad
    return moment_next, grad + MOMENTUM * moment_next


def masked(grad, weight, rank):
    coefficient = jnp.where(rank < 1.5, 1.0, jnp.where(rank < 2.5, WIDEN, 0.0))
    return jnp.where(rank < 2.5, grad, 0.0) + (2.0 * PENALTY) * weight * coefficient


def square_sum(value):
    return jnp.sum(value * value, axis=0, keepdims=True)


class Weights:
    def __init__(self, here, sources, targets, sems, local_sem):
        self.here, self.sources, self.targets = here, sources, targets
        self.sems, self.local_sem = sems, local_sem
        self.copies = [[None] * len(GROUPS) for _ in range(3)]
        self.local = [None] * len(GROUPS)

    def slice_at(self, axis, rows):
        return pl.ds(pl.multiple_of(getattr(self.here, axis) * rows, rows), rows)

    def one(self, g):
        kind, layer, parts, rows = GROUPS[g]
        source, target = self.sources[kind].at[layer], self.targets[kind].at[layer]
        self.local[g] = pltpu.make_async_copy(source, target.at[:, 0, 0], self.local_sem.at[g])
        self.local[g].start()
        self.copies[0][g] = [
            send(
                source.at[low:high, self.slice_at(axis, rows)],
                target.at[low:high, 0, r, self.slice_at(axis, rows)],
                self.sems[0],
                g * 6 + p * 3 + r - 1,
                self.here.along("y", -r),
            )
            for p, (axis, low, high) in enumerate(parts)
            for r in (1, 2, 3)
        ]

    def two(self, g):
        kind, layer, parts, rows = GROUPS[g]
        target = self.targets[kind].at[layer]
        for copy in self.copies[0][g]:
            copy.wait_recv()
        self.copies[1][g] = []
        for p, (axis, low, high) in enumerate(parts):
            part = target.at[low:high, 0, 1:4, self.slice_at(axis, rows)]
            for s in (1, 2, 3):
                self.copies[1][g].append(
                    send(part, part, self.sems[1], g * 6 + p * 3 + s - 1, self.here.along(axis, s))
                )

    def three(self, g):
        kind, layer, _, _ = GROUPS[g]
        target = self.targets[kind].at[layer]
        for copy in self.copies[1][g]:
            copy.wait_recv()
        self.local[g].wait()
        self.copies[2][g] = [
            send(target.at[:, 0], target.at[:, 1], self.sems[2], g, self.here.sibling())
        ]

    def load(self, g, buffer, sem):
        kind, layer, _, _ = GROUPS[g]
        self.copies[2][g][0].wait_recv()
        copy = pltpu.make_async_copy(self.targets[kind].at[layer], buffer, sem)
        copy.start()
        return copy

    def end(self):
        for stage in self.copies:
            for copies in stage:
                for copy in copies:
                    copy.wait_send()


def forward_step(
    att_weight_ref,
    ff_weight_ref,
    att_rank_ref,
    ff_rank_ref,
    head_bias_ref,
    inner_bias_ref,
    embedding_ref,
    inputs_ref,
    targets_ref,
    valid_ref,
    memory_ref,
    norm_ref,
    table_hbm,
    att_out,
    ff_out,
    new_memory_ref,
    prob_out,
    bias_out,
    count_out,
    low_out,
    query_u_out,
    query_w_out,
    mixed_out,
    normed_one_out,
    inverse_one_out,
    normed_two_out,
    inverse_two_out,
    grad_ref,
    grad_embedding_ref,
    ce_ref,
    att_ref,
    ff_ref,
    bias_ref,
    count_ref,
    rank_ref,
    block_rank_ref,
    count_z,
    count_x,
    att_w,
    ff_w,
    memory_w,
    table_ref,
    turned_ref,
    embed_ref,
    keys_ref,
    values_ref,
    rel_ref,
    score_ref,
    prob_ref,
    low_prob_ref,
    part_ref,
    hidden_ref,
    first_send,
    first_recv,
    second_send,
    second_recv,
    third_send,
    third_recv,
    extra_send,
    extra_recv,
    local_sem,
    load_sem,
    prob_sem,
):
    here = Place()
    here.greet()
    extra = (extra_send, extra_recv)
    rank_ref[...] = spread_rank(att_rank_ref[...], D)
    block_rank_ref[...] = spread_rank(ff_rank_ref[...], 256)

    def mask_attention(layer):
        for i in range(5):
            kept = rank_ref[layer * 5 + i : layer * 5 + i + 1, :] < 1.5
            att_ref[layer, i] = jnp.where(kept, att_weight_ref[layer, i], 0.0).astype(BF16)

    def mask_feedforward(layer):
        for i in range(16):
            kept = block_rank_ref[layer * 16 + i : layer * 16 + i + 1, :] < 1.5
            rows = slice(i % 8 * 64, i % 8 * 64 + 64)
            ff_ref[layer, i // 8, rows, :] = jnp.where(
                kept, ff_weight_ref[layer, i // 8, rows, :], 0.0
            ).astype(BF16)

    mask_attention(0)
    here.greeted()
    weights = Weights(
        here,
        (att_ref, ff_ref),
        (att_out, ff_out),
        ((first_send, first_recv), (second_send, second_recv), (third_send, third_recv)),
        local_sem,
    )
    weights.one(0)
    mask_feedforward(0)
    weights.one(1)
    counted = jnp.sum(valid_ref[...].astype(F32), axis=1, keepdims=True)
    count_ref[...] = jnp.broadcast_to(jnp.sum(counted, axis=0, keepdims=True), (8, 128))
    bias_ref[6:8, :] = jnp.zeros((2, 128), F32)
    for l in range(2):
        bias_ref[3 * l : 3 * l + 1, :] = jnp.concatenate(
            [head_bias_ref[l, k : k + 1, :] for k in range(2)], axis=1
        )
        for k in range(2):
            bias_ref[3 * l + 1 + k : 3 * l + 2 + k, :] = inner_bias_ref[
                l : l + 1, k * 128 : (k + 1) * 128
            ]
    count_z[here.z] = count_ref[...]
    count_copies = [
        send(count_ref, count_z.at[here.z], extra, s - 1, here.along("z", s)) for s in (1, 2, 3)
    ]
    bias_copies = [
        send(bias_ref, bias_out.at[0, r], extra, 2 + r, here.along("y", -r)) for r in (1, 2, 3)
    ]
    bias_out[0, 0] = bias_ref[...]
    mask_attention(1)
    weights.one(2)
    mask_feedforward(1)
    weights.one(3)
    loads = [
        pltpu.make_async_copy(table_hbm.at[here.core], table_ref, load_sem.at[0]),
        pltpu.make_async_copy(memory_ref.at[0, here.y], memory_w.at[0], load_sem.at[1]),
        pltpu.make_async_copy(memory_ref.at[1, here.y], memory_w.at[1], load_sem.at[2]),
    ]
    for copy in loads:
        copy.start()

    own_rows = pl.ds(pl.multiple_of(here.core * OWN, OWN), OWN)
    turned_ref[...] = jnp.zeros_like(turned_ref)
    turned_ref[0:4, :] = inputs_ref[...].astype(F32)
    turned_ref[8:12, :] = targets_ref[...].astype(F32)
    turned_ref[16:20, :] = valid_ref[...].astype(F32)
    columns = turned_ref[...].T
    turned_ref[:, 0:128] = columns[0:128]
    turned_ref[:, 128:256] = columns[128:256]
    turned_ref[:, 256:384] = columns[256:384]
    turned_ref[:, 384:512] = columns[384:512]
    embedding = embedding_ref[...]
    embedding_low = embedding.astype(BF16)
    vocab_id = lax.broadcasted_iota(jnp.int32, (128, VOCAB), 1).astype(F32)

    def onehot(column):
        return jnp.where(column == vocab_id, 1.0, 0.0)

    for segment in range(4):
        for b in range(4):
            tokens = turned_ref[:, b * 128 + segment : b * 128 + segment + 1]
            embed_ref[segment, b * 128 : (b + 1) * 128, :] = dot_nn(
                onehot(tokens).astype(BF16), embedding_low
            ).astype(BF16)
    memory_zero = pltpu.make_async_copy(embed_ref, new_memory_ref.at[0], load_sem.at[3])
    memory_zero.start()
    weights.two(0)
    low_out[0] = embed_ref[here.y]
    rest_one = embedding - embedding_low.astype(F32)
    middle_part = rest_one.astype(BF16)
    rest_two = (rest_one - middle_part.astype(F32)).astype(BF16)
    lane = lax.broadcasted_iota(jnp.int32, (128, 128), 1)
    own_targets, own_valid = [], []
    for b in range(2):
        block = turned_ref[:, pl.ds(pl.multiple_of(here.core * 256 + b * 128, 128), 128)]

        def column(at):
            return jnp.sum(jnp.where(lane == here.y + at, block, 0.0), axis=1, keepdims=True)

        mine = onehot(column(0)).astype(BF16)
        hidden_ref[b * 128 : (b + 1) * 128, :] = (
            dot_nn(mine, embedding_low) + dot_nn(mine, middle_part)
        ) + dot_nn(mine, rest_two)
        own_targets.append(onehot(column(8)))
        own_valid.append(column(16))
    weights.three(0)
    for copy in bias_copies:
        copy.wait_recv()
    bias_last = send(bias_out.at[0], bias_out.at[1], extra, 6, here.sibling())
    for copy in count_copies:
        copy.wait_recv()
    count_x[here.x] = (count_z[0] + count_z[1]) + (count_z[2] + count_z[3])
    count_last = [
        send(count_x.at[here.x], count_x.at[here.x], extra, 6 + s, here.along("x", s))
        for s in (1, 2, 3)
    ]
    weights.two(1)
    for copy in loads:
        copy.wait()
    bias_last.wait_recv()
    pending = []
    offset = here.core * OWN
    lane_head = lax.broadcasted_iota(jnp.int32, (OWN, 256), 1) // HD

    def project(layer):
        own_low = hidden_ref[...].astype(BF16)
        query = dot_nt(own_low, att_w[layer, 0].reshape(D, D))
        for which, target in ((0, query_u_out), (1, query_w_out)):
            bias = jnp.concatenate(
                [
                    bias_out[cc, r, 3 * layer : 3 * layer + 1, which * HD : (which + 1) * HD]
                    for cc in range(2)
                    for r in range(4)
                ],
                axis=1,
            )
            target[layer] = (query + bias).astype(BF16)
        key_w, value_w = att_w[layer, 1].reshape(D, D), att_w[layer, 2].reshape(D, D)
        for half in range(2):
            rows = memory_w[layer] if half == 0 else low_out[layer]
            cols = slice(half * SEG, (half + 1) * SEG)
            keys_ref[:, cols] = dot_nt(key_w, rows).astype(BF16)
            values = dot_nt(rows, value_w).astype(BF16)
            values_ref[0, cols, :] = values[:, 0:256]
            values_ref[1, cols, :] = values[:, 256:512]
        rel_ref[...] = dot_nt(att_w[layer, 3].reshape(D, D), table_ref[...]).astype(BF16)
        part_ref[...] = jnp.zeros_like(part_ref)

    def head(layer):
        def run(h, carry):
            group = h // 4
            slot = h % 2
            mine = lane_head == h % 4
            lanes = pl.ds(pl.multiple_of(group * 256, 256), 256)
            query_u = jnp.where(mine, query_u_out[layer, :, lanes].astype(F32), 0.0).astype(BF16)
            query_w = jnp.where(mine, query_w_out[layer, :, lanes].astype(F32), 0.0).astype(BF16)
            score_ref[...] = dot_nn(query_w, rel_ref[lanes, :])

            @pl.when(h >= 2)
            def _():
                pltpu.make_async_copy(
                    prob_ref.at[slot], prob_out.at[layer, h], prob_sem.at[slot]
                ).wait()

            prob_ref[slot] = dot_nn(query_u, keys_ref[lanes, :])
            for b in range(0, OWN, ROWS):
                rows = slice(b, b + ROWS)
                moved = pltpu.roll(score_ref[rows, :], b, 1, stride=1, stride_axis=0)
                score = (prob_ref[slot, rows, :] + moved) * SCALE
                key_id = lax.broadcasted_iota(jnp.int32, (ROWS, KLEN), 1)
                query_id = lax.broadcasted_iota(jnp.int32, (ROWS, KLEN), 0) + (offset + b + SEG)
                score = jnp.where(key_id <= query_id, score, -1e30)
                expo = jnp.exp(score - jnp.max(score, axis=-1, keepdims=True))
                prob = expo * (1.0 / jnp.sum(expo, axis=-1, keepdims=True))
                prob_ref[slot, rows, :] = prob
                low_prob_ref[rows, :] = prob.astype(BF16)
            pltpu.make_async_copy(
                prob_ref.at[slot], prob_out.at[layer, h], prob_sem.at[slot]
            ).start()
            mixed = dot_nn(low_prob_ref[...], values_ref[group])
            part_ref[group] = part_ref[group] + jnp.where(mine, mixed, 0.0)
            return carry

        return run

    def attend(layer):
        for slot in range(2):
            pltpu.make_async_copy(
                prob_ref.at[slot], prob_out.at[layer, 6 + slot], prob_sem.at[slot]
            ).wait()
        mixed_out[layer, :, 0:256] = part_ref[0].astype(BF16)
        mixed_out[layer, :, 256:512] = part_ref[1].astype(BF16)
        attended = dot_nn(mixed_out[layer], att_w[layer, 4].reshape(D, D))
        normed_one, inverse_one = norm_forward(hidden_ref[...] + attended)
        normed_one_out[layer] = normed_one
        inverse_one_out[layer] = inverse_one
        return normed_one * norm_ref[0, layer : layer + 1, :] + norm_ref[1, layer : layer + 1, :]

    def feed(layer, middle):
        middle_low = middle.astype(BF16)
        branch = jnp.zeros((OWN, D), F32)
        for cc in range(2):
            for r in range(4):
                bias = jnp.concatenate(
                    [bias_out[cc, r, 3 * layer + 1 + i : 3 * layer + 2 + i, :] for i in range(2)],
                    axis=1,
                )
                inner = dot_nn(middle_low, ff_w[layer, 0, cc, r]) + bias
                branch = branch + dot_nt(smooth_unit(inner).astype(BF16), ff_w[layer, 1, cc, r])
        normed_two, inverse_two = norm_forward(middle + (branch + norm_ref[4, layer : layer + 1, :]))
        normed_two_out[layer] = normed_two
        inverse_two_out[layer] = inverse_two
        hidden_ref[...] = normed_two * norm_ref[2, layer : layer + 1, :] + norm_ref[3, layer : layer + 1, :]

    weights.load(0, att_w.at[0], load_sem.at[4]).wait()
    project(0)
    weights.two(2)
    lax.fori_loop(0, 4, head(0), 0)
    weights.three(1)
    weights.two(3)
    lax.fori_loop(4, 8, head(0), 0)
    weights.three(2)
    feed_load = weights.load(1, ff_w.at[0], load_sem.at[5])
    middle = attend(0)
    feed_load.wait()
    feed(0, middle)
    low_out[1, own_rows, :] = hidden_ref[...].astype(BF16)
    own_low = low_out.at[1, own_rows]
    swap = send(own_low, own_low, extra, 10, here.sibling())
    spread_at = new_memory_ref.at[1, here.y, own_rows]
    spread = [send(own_low, spread_at, extra, 10 + s, here.along("y", s)) for s in (1, 2, 3)]
    spread_own = pltpu.make_async_copy(own_low, spread_at, load_sem.at[6])
    spread_own.start()
    attention_one = weights.load(2, att_w.at[1], load_sem.at[7])
    swap.wait_recv()
    attention_one.wait()
    project(1)
    lax.fori_loop(0, 4, head(1), 0)
    weights.three(3)
    for copy in spread:
        copy.wait_recv()
    spread_own.wait()
    spread_all = new_memory_ref.at[1, :, own_rows]
    spread_last = send(spread_all, spread_all, extra, 14, here.sibling())
    lax.fori_loop(4, 8, head(1), 0)
    feed_load = weights.load(3, ff_w.at[1], load_sem.at[5])
    middle = attend(1)
    feed_load.wait()
    feed(1, middle)
    for copy in count_last:
        copy.wait_recv()
    count_all = (count_x[0] + count_x[1]) + (count_x[2] + count_x[3])
    count_out[...] = count_all

    final_low = hidden_ref[...].astype(BF16)
    logit_scale = D ** (-0.5)
    logits = dot_nt(final_low, embedding_low) * logit_scale
    picked = jnp.concatenate(own_targets, axis=0)
    valid = jnp.concatenate(own_valid, axis=0)
    peak = jnp.max(logits, axis=-1, keepdims=True)
    log_total = peak + jnp.log(jnp.sum(jnp.exp(logits - peak), axis=-1, keepdims=True))
    losses = valid * (log_total - jnp.sum(logits * picked, axis=-1, keepdims=True))
    ce_ref[...] = jnp.broadcast_to(jnp.sum(losses, axis=0, keepdims=True), (8, 128))
    grad_logits = (valid * (jnp.exp(logits - log_total) - picked) / count_all[0:1, 0:1]).astype(
        BF16
    )
    grad_ref[...] = dot_nn(grad_logits, embedding_low) * logit_scale
    grad_embedding_ref[...] = (
        dot_nn(transposed(grad_logits).astype(BF16), final_low) * logit_scale
    ).reshape(MP, 32, D)
    memory_zero.wait()
    spread_last.wait()
    for copy in count_copies + bias_copies + [bias_last] + count_last + [swap] + spread:
        copy.wait_send()
    weights.end()


def forward_all(*operands):
    vmem, hbm = VMEM_SPEC, ANY_SPEC
    outs = [
        (hbm, (2, 5, 2, 4, HD, D), BF16),
        (hbm, (2, 2, 2, 4, D, 256), BF16),
        (hbm, (2, 4, SEG, D), BF16),
        (hbm, (2, HEADS, OWN, KLEN), F32),
        (vmem, (2, 4, 8, 128), F32),
        (vmem, (8, 128), F32),
        (vmem, (2, SEG, D), BF16),
        (vmem, (2, OWN, D), BF16),
        (vmem, (2, OWN, D), BF16),
        (vmem, (2, OWN, D), BF16),
        (vmem, (2, OWN, D), F32),
        (vmem, (2, OWN, 1), F32),
        (vmem, (2, OWN, D), F32),
        (vmem, (2, OWN, 1), F32),
        (vmem, (OWN, D), F32),
        (vmem, (MP, 32, D), F32),
        (vmem, (8, 128), F32),
    ]
    return pl.pallas_call(
        forward_step,
        out_shape=[jax.ShapeDtypeStruct(s, t) for _, s, t in outs],
        in_specs=[vmem] * 10 + [hbm, vmem, hbm],
        out_specs=[m for m, _, _ in outs],
        scratch_shapes=[
            pltpu.VMEM((2, 5, HD, D), BF16),
            pltpu.VMEM((2, 2, D, 256), BF16),
            pltpu.VMEM((8, 128), F32),
            pltpu.VMEM((8, 128), F32),
            pltpu.VMEM((10, D), F32),
            pltpu.VMEM((32, 256), F32),
            pltpu.VMEM((4, 8, 128), F32),
            pltpu.VMEM((4, 8, 128), F32),
            pltpu.VMEM((2, 5, 2, 4, HD, D), BF16),
            pltpu.VMEM((2, 2, 2, 4, D, 256), BF16),
            pltpu.VMEM((2, SEG, D), BF16),
            pltpu.VMEM((KLEN, D), BF16),
            pltpu.VMEM((128, SEG), F32),
            pltpu.VMEM((4, SEG, D), BF16),
            pltpu.VMEM((D, KLEN), BF16),
            pltpu.VMEM((2, KLEN, 256), BF16),
            pltpu.VMEM((D, KLEN), BF16),
            pltpu.VMEM((OWN, KLEN), F32),
            pltpu.VMEM((2, OWN, KLEN), F32),
            pltpu.VMEM((OWN, KLEN), BF16),
            pltpu.VMEM((2, OWN, 256), F32),
            pltpu.VMEM((OWN, D), F32),
            pltpu.SemaphoreType.DMA((24,)),
            pltpu.SemaphoreType.DMA((24,)),
            pltpu.SemaphoreType.DMA((24,)),
            pltpu.SemaphoreType.DMA((24,)),
            pltpu.SemaphoreType.DMA((4,)),
            pltpu.SemaphoreType.DMA((4,)),
            pltpu.SemaphoreType.DMA((15,)),
            pltpu.SemaphoreType.DMA((15,)),
            pltpu.SemaphoreType.DMA((4,)),
            pltpu.SemaphoreType.DMA((8,)),
            pltpu.SemaphoreType.DMA((2,)),
        ],
        compiler_params=pltpu.CompilerParams(
            collective_id=0, has_side_effects=True, vmem_limit_bytes=VMEM_LIMIT
        ),
        name="forward_all",
    )(*operands)


SHAPES = {ATT: (HD, D), FFN: (D, 256), SMALL: (64, D)}


class Sums:
    def __init__(self, here, arrays, outs, buffers, sems):
        self.here, self.arrays, self.outs = here, arrays, outs
        self.pairs, self.ones, self.twos, self.threes = buffers
        self.sems = sems
        self.copies = [[[] for _ in SUM_GROUPS] for _ in range(5)]

    def slice_at(self, index, rows):
        return pl.ds(pl.multiple_of(index * rows, rows), rows)

    def arrived(self, stage, g):
        for copy in self.copies[stage][g]:
            copy.wait_recv()

    def pair(self, g):
        kind, layer, (base, end), _, _ = SUM_GROUPS[g]
        self.copies[0][g].append(
            send(
                self.arrays[kind].at[layer, base:end, 1],
                self.pairs[g],
                self.sems[0],
                g,
                self.here.sibling(),
            )
        )

    def one(self, g):
        kind, layer, (base, _), parts, rows = SUM_GROUPS[g]
        self.arrived(0, g)
        pair = self.pairs[g]
        for m in range(pair.shape[0]):
            for r in range(4):
                pair[m, r] = (
                    pair[m, r].astype(F32) + self.arrays[kind][layer, base + m, 0, r].astype(F32)
                ).astype(BF16)
        for p, (axis, low, high) in enumerate(parts):
            for s in (1, 2, 3):
                goal = (getattr(self.here, axis) + s) % 4
                self.copies[1][g].append(
                    send(
                        pair.at[low:high, :, self.slice_at(goal, rows)],
                        self.ones[g][p].at[s - 1],
                        self.sems[1],
                        g * 6 + p * 3 + s - 1,
                        self.here.along(axis, s),
                    )
                )

    def two(self, g):
        kind, layer, (base, _), parts, rows = SUM_GROUPS[g]
        self.arrived(1, g)
        for p, (axis, low, high) in enumerate(parts):
            got = self.ones[g][p]
            own = self.pairs[g].at[low:high, :, self.slice_at(getattr(self.here, axis), rows)]
            for m in range(high - low):
                for r in range(4):
                    got[0, m, r] = (
                        (own[m, r].astype(F32) + got[0, m, r].astype(F32))
                        + (got[1, m, r].astype(F32) + got[2, m, r].astype(F32))
                    ).astype(BF16)
            for r in (1, 2, 3):
                self.copies[2][g].append(
                    send(
                        got.at[0, :, r],
                        self.twos[g][p].at[r - 1],
                        self.sems[2],
                        g * 6 + p * 3 + r - 1,
                        self.here.along("y", r),
                    )
                )

    def three(self, g):
        kind, layer, (base, _), parts, rows = SUM_GROUPS[g]
        self.arrived(2, g)
        for p, (axis, low, high) in enumerate(parts):
            other = "x" if axis == "z" else "z"
            got, every = self.twos[g][p], self.threes[g][p]
            index = getattr(self.here, other)
            for m in range(high - low):
                every[index, m] = (
                    (self.ones[g][p][0, m, 0].astype(F32) + got[0, m].astype(F32))
                    + (got[1, m].astype(F32) + got[2, m].astype(F32))
                ).astype(BF16)
            for s in (1, 2, 3):
                self.copies[3][g].append(
                    send(
                        every.at[index],
                        every.at[index],
                        self.sems[3],
                        g * 6 + p * 3 + s - 1,
                        self.here.along(other, s),
                    )
                )

    def four(self, g):
        kind, layer, (base, _), parts, rows = SUM_GROUPS[g]
        self.arrived(3, g)
        for p, (axis, low, high) in enumerate(parts):
            every = self.threes[g][p]
            part = self.slice_at(getattr(self.here, axis), rows)
            for m in range(high - low):
                self.outs[kind][layer, base + low + m, part] = (
                    (every[0, m].astype(F32) + every[1, m].astype(F32))
                    + (every[2, m].astype(F32) + every[3, m].astype(F32))
                ).astype(BF16)
            target = self.outs[kind].at[layer, base + low : base + high, part]
            for s in (1, 2, 3):
                self.copies[4][g].append(
                    send(
                        target,
                        target,
                        self.sems[4],
                        g * 6 + p * 3 + s - 1,
                        self.here.along(axis, s),
                    )
                )

    def end(self):
        for stage in self.copies:
            for copies in stage:
                for copy in copies:
                    copy.wait_send()


def backward_step(
    att_hbm,
    ff_hbm,
    prob_hbm,
    memory_hbm,
    table_hbm,
    grad_hbm,
    grad_embedding_hbm,
    normed_two_hbm,
    att_weight_hbm,
    att_moment_hbm,
    ff_weight_hbm,
    ff_moment_hbm,
    att_rank_ref,
    ff_rank_ref,
    head_weight_ref,
    head_moment_ref,
    inner_weight_ref,
    inner_moment_ref,
    bias_ref,
    norm_ref,
    inputs_ref,
    ce_ref,
    low_ref,
    query_u_ref,
    query_w_ref,
    mixed_ref,
    normed_one_ref,
    inverse_one_ref,
    inverse_two_ref,
    att_out,
    ff_out,
    small_out,
    ce_out,
    parts_out,
    att_w,
    ff_w,
    memory_w,
    table_ref,
    prob_ref,
    grad_att_ref,
    grad_ff_ref,
    grad_small_ref,
    grad_ref,
    keys_ref,
    values_ref,
    rel_ref,
    gmix_ref,
    gmix_t_ref,
    query_t_ref,
    flip_t_ref,
    prob_grad_ref,
    score_grad_ref,
    low_prob_ref,
    flipped_ref,
    gquery_ref,
    gmemory_ref,
    ghidden_ref,
    got_ref,
    grel_ref,
    grad_bias_ref,
    grad_inner_ref,
    grad_norm_ref,
    ranked_ref,
    block_ref,
    ce_pair,
    ce_z,
    ce_y,
    ce_x,
    small_own,
    rank_ref,
    block_rank_ref,
    part_ref,
    *scratch,
):
    here = Place()
    scratch = list(scratch)
    pairs = [scratch.pop(0) for _ in SUM_GROUPS]
    ones, twos, threes = [], [], []
    for group in SUM_GROUPS:
        for buffers in (ones, twos, threes):
            buffers.append([scratch.pop(0) for _ in group[3]])
    sems = [(scratch.pop(0), scratch.pop(0)) for _ in range(7)]
    load_sem, prob_sem, stage_sem = scratch
    extra = sems[5]
    sums = Sums(
        here,
        (grad_att_ref, grad_ff_ref, grad_small_ref),
        (att_out, ff_out, small_own),
        (pairs, ones, twos, threes),
        sems,
    )
    load_ff = pltpu.make_async_copy(ff_hbm.at[1], ff_w, load_sem.at[0])
    load_att = pltpu.make_async_copy(att_hbm.at[1], att_w, load_sem.at[1])
    loads = [
        pltpu.make_async_copy(memory_hbm.at[0, here.y], memory_w.at[0], load_sem.at[2]),
        pltpu.make_async_copy(memory_hbm.at[1, here.y], memory_w.at[1], load_sem.at[3]),
        pltpu.make_async_copy(table_hbm.at[here.core], table_ref, load_sem.at[4]),
        pltpu.make_async_copy(grad_embedding_hbm, ranked_ref, load_sem.at[5]),
    ]
    load_grad = pltpu.make_async_copy(grad_hbm, grad_ref, load_sem.at[6])
    load_grad.start()
    load_normed = pltpu.make_async_copy(
        normed_two_hbm.at[1], prob_grad_ref.at[:, 0:D], load_sem.at[7]
    )
    load_normed.start()
    load_ff.start()
    load_att.start()
    for copy in loads:
        copy.start()
    others = [
        here.device(y=(here.y + s) % 4, core=(here.core + k) % 2)
        for s in range(4)
        for k in range(2)
        if s or k
    ]
    here.greet(others[2::2])
    rank_ref[...] = spread_rank(att_rank_ref[...], D)
    block_rank_ref[...] = spread_rank(ff_rank_ref[...], 256)
    here.greeted(13)
    own_rows = pl.ds(pl.multiple_of(here.core * OWN, OWN), OWN)
    their_rows = pl.ds(pl.multiple_of(OWN - here.core * OWN, OWN), OWN)
    ce_pair[here.core] = ce_ref[...]
    ce_copies = [send(ce_ref, ce_pair.at[here.core], extra, 0, here.sibling())]
    flip = (
        lax.broadcasted_iota(jnp.int32, (OWN, OWN), 0)
        + lax.broadcasted_iota(jnp.int32, (OWN, OWN), 1)
        == OWN - 1
    )
    flip = jnp.where(flip, 1.0, 0.0).astype(BF16)
    lane_head = lax.broadcasted_iota(jnp.int32, (OWN, 256), 1) // HD
    load_grad.wait()

    def spread_ce(step):
        source, target, axis, base = (
            (ce_pair, ce_z, "z", 1),
            (ce_z, ce_y, "y", 4),
            (ce_y, ce_x, "x", 7),
        )[step]
        for copy in ce_copies[-1:] if step == 0 else ce_copies[-3:]:
            copy.wait_recv()
        total = source[0] + source[1]
        if step:
            total = total + (source[2] + source[3])
        index = getattr(here, axis)
        target[index] = total
        for s in (1, 2, 3):
            ce_copies.append(
                send(target.at[index], target.at[index], extra, base + s - 1, here.along(axis, s))
            )

    def feed(layer):
        load_normed.wait()
        gsum, ggain, goffset = norm_backward(
            grad_ref[...], prob_grad_ref[:, 0:D], inverse_two_ref[layer], norm_ref[2, layer : layer + 1, :]
        )
        middle = normed_one_ref[layer] * norm_ref[0, layer : layer + 1, :] + norm_ref[1, layer : layer + 1, :]
        middle_low = middle.astype(BF16)
        middle_t = transposed(middle_low).astype(BF16)
        gbranch = gsum.astype(BF16)
        gbranch_t = transposed(gbranch).astype(BF16)
        gmiddle = gsum
        load_ff.wait()
        for cc in (1, 0):
            if cc == 0:
                sums.pair(1 if layer == 0 else 3)
            for r in range(4):
                bias = jnp.concatenate(
                    [bias_ref[cc, r, 3 * layer + 1 + i : 3 * layer + 2 + i, :] for i in range(2)],
                    axis=1,
                )
                inner = dot_nn(middle_low, ff_w[0, cc, r]) + bias
                active, slope = smooth_both(inner)
                ginner = (dot_nn(gbranch, ff_w[1, cc, r]) * slope).astype(BF16)
                grad_ff_ref[layer, 0, cc, r] = dot_nn(middle_t, ginner).astype(BF16)
                grad_ff_ref[layer, 1, cc, r] = dot_nn(gbranch_t, active.astype(BF16)).astype(BF16)
                grad_inner_ref[layer, cc, r] = jnp.sum(
                    ginner.astype(F32), axis=0, keepdims=True
                )
                gmiddle = gmiddle + dot_nt(ginner, ff_w[0, cc, r])
        rows = [jnp.sum(gsum, axis=0, keepdims=True)]
        gsum, ggain_one, goffset_one = norm_backward(
            gmiddle, normed_one_ref[layer], inverse_one_ref[layer], norm_ref[0, layer : layer + 1, :]
        )
        rows = [ggain_one, goffset_one, ggain, goffset] + rows
        for i, row in enumerate(rows):
            at = 8 * layer + i
            grad_norm_ref[at // 2, at % 2 : at % 2 + 1, :] = row
        grad_ref[...] = gsum

    def prepare(layer):
        gattended = grad_ref[...].astype(BF16)
        wide = dot_nn(transposed(mixed_ref[layer]).astype(BF16), gattended).astype(BF16)
        grad_att_ref[layer, 4] = wide.reshape(2, 4, HD, D)
        sums.pair(5 + layer)
        load_att.wait()
        gmix = dot_nt(gattended, att_w[4].reshape(D, D))
        gmix_ref[...] = gmix.astype(BF16)
        gmix_t_ref[...] = gmix.T.astype(BF16)
        query_t_ref[...] = transposed(query_u_ref[layer]).astype(BF16)
        flip_t_ref[...] = dot_nn(transposed(query_w_ref[layer]).astype(BF16), flip).astype(BF16)
        key_w, value_w = att_w[1].reshape(D, D), att_w[2].reshape(D, D)
        for half in range(2):
            rows = memory_w[layer] if half == 0 else low_ref[layer]
            cols = slice(half * SEG, (half + 1) * SEG)
            values_ref[:, cols] = dot_nt(value_w, rows).astype(BF16)
            keys = dot_nt(rows, key_w).astype(BF16)
            keys_ref[0, cols, :] = keys[:, 0:256]
            keys_ref[1, cols, :] = keys[:, 256:512]
        rel = dot_nt(table_ref[...], att_w[3].reshape(D, D)).astype(BF16)
        rel_ref[0] = rel[:, 0:256]
        rel_ref[1] = rel[:, 256:512]
        gquery_ref[...] = jnp.zeros_like(gquery_ref)

    def fetch(layer, n, slot):
        h = (n + 4) % HEADS
        return pltpu.make_async_copy(prob_hbm.at[layer, h], prob_ref.at[slot], prob_sem.at[slot])

    def head(layer):
        def run(n, carry):
            h = (n + 4) % HEADS
            group = h // 4
            slot = n % 2
            mine = lane_head == h % 4
            lanes = pl.ds(pl.multiple_of(group * 256, 256), 256)
            row = pl.ds(pl.multiple_of(h * HD, HD), HD)
            gmix_h = jnp.where(mine, gmix_ref[:, lanes].astype(F32), 0.0).astype(BF16)
            prob_grad_ref[...] = dot_nn(gmix_h, values_ref[lanes, :])
            fetch(layer, n, slot).wait()
            for b in range(0, OWN, ROWS):
                rows = slice(b, b + ROWS)
                prob = prob_ref[slot, rows, :]
                gprob = prob_grad_ref[rows, :]
                inner = jnp.sum(prob * gprob, axis=-1, keepdims=True)
                score_grad_ref[rows, :] = (prob * (gprob - inner)).astype(BF16)
                low_prob_ref[rows, :] = prob.astype(BF16)

            @pl.when(n < HEADS - 2)
            def _():
                fetch(layer, n + 2, slot).start()

            if layer == 1:
                @pl.when(n >= HEADS - 2)
                def _():
                    fetch(0, n + 2 - HEADS, slot).start()

            sgrad = score_grad_ref[...]
            gquery_ref[0, group] = gquery_ref[0, group] + jnp.where(
                mine, dot_nn(sgrad, keys_ref[group]), 0.0
            )
            gkey = dot_nn(query_t_ref[row, :], sgrad) * SCALE
            gvalue = dot_nn(gmix_t_ref[row, :], low_prob_ref[...])
            gmemory_ref[0, row, :] = gkey[:, 0:SEG].astype(BF16)
            gmemory_ref[1, row, :] = gvalue[:, 0:SEG].astype(BF16)
            ghidden_ref[0, row, :] = gkey[:, SEG:]
            ghidden_ref[1, row, :] = gvalue[:, SEG:]
            flipped = dot_nn(flip, sgrad).astype(BF16)
            flipped_ref[...] = pltpu.roll(flipped, KLEN - OWN + 1, 1, stride=1, stride_axis=0)
            gquery_ref[1, group] = gquery_ref[1, group] + jnp.where(
                mine, dot_nn(flipped_ref[...], rel_ref[group]), 0.0
            )
            grel_ref[row, :] = (dot_nn(flip_t_ref[row, :], flipped_ref[...]) * SCALE).astype(BF16)
            return carry

        return run

    def swap(layer, i):
        return send(
            ghidden_ref.at[:, 256 * i : 256 * i + 256, their_rows],
            got_ref.at[:, 256 - 256 * i : 512 - 256 * i],
            extra,
            10 + 2 * layer + i,
            here.sibling(),
        )

    def half(layer, group):
        own_low = low_ref[layer, own_rows, :]
        lanes = slice(group * 256, (group + 1) * 256)
        gquery_u = (gquery_ref[0, group] * SCALE).astype(BF16)
        gquery_w = dot_nn(flip, (gquery_ref[1, group] * SCALE).astype(BF16))
        grad_bias_ref[layer, 0:1, lanes] = jnp.sum(gquery_u.astype(F32), axis=0, keepdims=True)
        grad_bias_ref[layer, 1:2, lanes] = jnp.sum(gquery_w, axis=0, keepdims=True)
        gquery = gquery_u.astype(F32) + gquery_w
        grad_att_ref[layer, 0, group] = (
            dot_nn(gquery.T.astype(BF16), own_low).astype(BF16).reshape(4, HD, D)
        )
        grad_att_ref[layer, 3, group] = (
            dot_nn(grel_ref[lanes, :], table_ref[...]).astype(BF16).reshape(4, HD, D)
        )
        for i in range(2):
            part = dot_nn(gmemory_ref[i, lanes, :], memory_w[layer]) + dot_nn(
                ghidden_ref[i, lanes, :].astype(BF16), low_ref[layer]
            )
            grad_att_ref[layer, 1 + i, group] = part.astype(BF16).reshape(4, HD, D)
        return dot_nn(gquery.astype(BF16), att_w[0, group].reshape(256, D))

    def finish(swaps):
        for copy in swaps:
            copy.wait_recv()
        for i in range(2):
            total = (ghidden_ref[i, :, own_rows] + got_ref[i]).astype(BF16)
            grad_ref[...] += dot_nn(transposed(total).astype(BF16), att_w[1 + i].reshape(D, D))

    fetch(1, 0, 0).start()
    fetch(1, 1, 1).start()
    feed(1)
    load_ff = pltpu.make_async_copy(ff_hbm.at[0], ff_w, load_sem.at[0])
    load_ff.start()
    spread_ce(0)
    for copy in loads:
        copy.wait()
    prepare(1)
    sums.one(3)
    sums.one(6)
    lax.fori_loop(0, 4, head(1), 0)
    swaps_one = [swap(1, 1)]
    grad_ref[...] += half(1, 1)
    sums.pair(2)
    lax.fori_loop(4, HEADS, head(1), 0)
    swaps_one.append(swap(1, 0))
    load_normed = pltpu.make_async_copy(
        normed_two_hbm.at[0], prob_grad_ref.at[:, 0:D], load_sem.at[7]
    )
    load_normed.start()
    spread_ce(1)
    grad_ref[...] += half(1, 0)
    sums.one(2)
    sums.two(3)
    sums.two(6)
    finish(swaps_one)
    load_att = pltpu.make_async_copy(att_hbm.at[0], att_w, load_sem.at[1])
    load_att.start()
    feed(0)
    spread_ce(2)
    for copy in swaps_one:
        copy.wait_send()
    prepare(0)
    sums.one(1)
    sums.one(5)
    sums.two(2)
    lax.fori_loop(0, 4, head(0), 0)
    swaps_zero = [swap(0, 1)]
    grad_ref[...] += half(0, 1)
    sums.pair(0)
    sums.three(3)
    sums.three(6)
    lax.fori_loop(4, HEADS, head(0), 0)
    swaps_zero.append(swap(0, 0))
    grad_ref[...] += half(0, 0)
    sums.one(0)
    sums.two(1)
    sums.two(5)
    sums.three(2)
    finish(swaps_zero)

    def stage(pairs, slot):
        copies = []
        for i, (source, target) in enumerate(pairs):
            copies.append(pltpu.make_async_copy(source, target, stage_sem.at[10 * slot + i]))
            copies[-1].start()
        return copies

    def stage_ff(layer, mat):
        return stage(
            [
                (
                    source.at[layer, mat, 256 * i : 256 * i + 256],
                    prob_ref.at[mat, :, 512 * k + 256 * i : 512 * k + 256 * i + 256],
                )
                for k, source in enumerate((ff_weight_hbm, ff_moment_hbm))
                for i in range(2)
            ],
            mat,
        )

    def stage_att(layer):
        pairs = []
        for k, source in enumerate((att_weight_hbm, att_moment_hbm)):
            cols = slice(512 * k, 512 * k + 512)
            for i in range(4):
                pairs.append(
                    (source.at[layer, i], prob_ref.at[layer, 64 * i : 64 * i + 64, cols])
                )
            rows = slice(64 * layer, 64 * layer + 64)
            pairs.append((source.at[layer, 4], prob_grad_ref.at[rows, cols]))
        return stage(pairs, layer)

    squares = {ATT: [jnp.zeros((1, D), F32)] * 2, FFN: [jnp.zeros((1, 256), F32)] * 2}

    def add_squares(kind, total, weight, moment, rank):
        grad = masked(total.astype(F32), weight, rank)
        _, direction = advance_one(grad, weight, moment)
        first, second = squares[kind]
        squares[kind] = [first + square_sum(weight), second + square_sum(direction)]

    def square_ff(layer, copies):
        for copy in copies:
            copy.wait()
        for mat in range(2):
            for i in range(8):
                rows = slice(i % 4 * 64, i % 4 * 64 + 64)
                col = i // 4 * 256
                rank_at = layer * 16 + mat * 8 + i
                add_squares(
                    FFN,
                    ff_out[layer, mat, i * 64 : i * 64 + 64, :],
                    prob_ref[mat, rows, col : col + 256],
                    prob_ref[mat, rows, 512 + col : 768 + col],
                    block_rank_ref[rank_at : rank_at + 1, :],
                )

    def square_att(layer, copies):
        for copy in copies:
            copy.wait()
        for i in range(5):
            rows = slice(64 * i, 64 * i + 64) if i < 4 else slice(64 * layer, 64 * layer + 64)
            block = prob_ref.at[layer, rows] if i < 4 else prob_grad_ref.at[rows]
            add_squares(
                ATT,
                att_out[layer, i],
                block[:, 0:512],
                block[:, 512:1024],
                rank_ref[layer * 5 + i : layer * 5 + i + 1, :],
            )

    staged = stage_ff(1, 0) + stage_ff(1, 1)

    tokens = inputs_ref[pl.ds(here.y, 1), own_rows]
    onehot = jnp.where(
        tokens == lax.broadcasted_iota(jnp.int32, (VOCAB, OWN), 0), 1.0, 0.0
    ).astype(BF16)
    grad = grad_ref[...]
    high = grad.astype(BF16)
    rest = (grad - high.astype(F32)).astype(BF16)
    ranked_ref[...] += (dot_nn(onehot, high) + dot_nn(onehot, rest)).reshape(MP, 32, D)
    block_ref[...] = jnp.zeros_like(block_ref)
    for cc in range(2):
        for r in range(4):
            device = ((here.y + r) % 4) * 2 + (here.core + cc) % 2
            first = (cc * 4 + r) * HD
            block_ref[0:32, :] = ranked_ref[device]
            block_ref[32:34, :] = grad_norm_ref[device]
            block_ref[34:35, 0:256] = jnp.concatenate(
                [
                    grad_bias_ref[l, k : k + 1, first : first + HD]
                    for l in range(2)
                    for k in range(2)
                ],
                axis=1,
            )
            block_ref[35:36, :] = jnp.concatenate(
                [grad_inner_ref[l, cc, r] for l in range(2)], axis=1
            )
            grad_small_ref[0, 0, cc, r] = block_ref[...].astype(BF16)
    sums.pair(4)
    sums.four(3)
    sums.four(6)
    sums.one(4)
    sums.two(0)
    sums.three(1)
    sums.three(5)
    sums.two(4)
    sums.four(2)
    sums.arrived(4, 3)
    square_ff(1, staged)
    staged = stage_ff(0, 0) + stage_ff(0, 1)
    sums.three(0)
    sums.three(4)
    sums.four(1)
    sums.four(5)
    for copy in ce_copies[-3:]:
        copy.wait_recv()
    ce_out[...] = (ce_x[0] + ce_x[1]) + (ce_x[2] + ce_x[3])
    sums.four(4)
    sums.four(0)
    sums.arrived(4, 1)
    square_ff(0, staged)
    staged_one, staged_zero = stage_att(1), stage_att(0)
    sums.arrived(4, 4)
    small_out[here.y, here.core] = small_own[0, 0]
    piece = small_out.at[here.y, here.core]
    small_copies = [send(piece, piece, extra, 13 + r, here.along("y", r)) for r in (1, 2, 3)]
    small = small_own[0, 0].astype(F32)
    head_sums = [jnp.zeros((1, HD), F32)] * 2
    inner_sums = [jnp.zeros((1, 256), F32)] * 2
    for l in range(2):
        for k in range(2):
            at = (l * 2 + k) * HD
            weight = head_weight_ref[l, k : k + 1, :]
            _, direction = advance_one(
                small[34:35, at : at + HD], weight, head_moment_ref[l, k : k + 1, :]
            )
            head_sums = [head_sums[0] + weight * weight, head_sums[1] + direction * direction]
        weight = inner_weight_ref[l : l + 1, :]
        _, direction = advance_one(
            small[35:36, l * 256 : (l + 1) * 256], weight, inner_moment_ref[l : l + 1, :]
        )
        inner_sums = [inner_sums[0] + weight * weight, inner_sums[1] + direction * direction]
    sums.arrived(4, 2)
    sums.arrived(4, 6)
    square_att(1, staged_one)
    for copy in small_copies:
        copy.wait_recv()
    piece = small_out.at[:, here.core]
    last = send(piece, piece, extra, 17, here.sibling())
    sums.arrived(4, 5)
    sums.arrived(4, 0)
    square_att(0, staged_zero)
    for k in range(2):
        for i, value in enumerate((squares[ATT], squares[FFN], head_sums, inner_sums)):
            part_ref[4 * k + i : 4 * k + i + 1, :] = jnp.broadcast_to(
                jnp.sum(value[k], axis=1, keepdims=True), (1, 128)
            )
    index = here.y * 2 + here.core
    parts_out[index] = part_ref[...]
    norm_copies = [
        send(part_ref, parts_out.at[index], sems[6], i, partner)
        for i, partner in enumerate(others)
    ]
    last.wait()
    for copy in norm_copies:
        copy.wait()
    for copy in ce_copies + swaps_zero + small_copies:
        copy.wait_send()
    sums.end()


def backward_all(*operands):
    vmem, hbm = VMEM_SPEC, ANY_SPEC
    outs = [
        ((2, 5, HD, D), BF16),
        ((2, 2, D, 256), BF16),
        ((4, 2, 64, D), BF16),
        ((8, 128), F32),
        ((MP, 8, 128), F32),
    ]
    scratch = [
        pltpu.VMEM((5, 2, 4, HD, D), BF16),
        pltpu.VMEM((2, 2, 4, D, 256), BF16),
        pltpu.VMEM((2, SEG, D), BF16),
        pltpu.VMEM((KLEN, D), BF16),
        pltpu.VMEM((2, OWN, KLEN), F32),
        pltpu.VMEM((2, 5, 2, 4, HD, D), BF16),
        pltpu.VMEM((2, 2, 2, 4, D, 256), BF16),
        pltpu.VMEM((1, 1, 2, 4, 64, D), BF16),
        pltpu.VMEM((OWN, D), F32),
        pltpu.VMEM((2, KLEN, 256), BF16),
        pltpu.VMEM((D, KLEN), BF16),
        pltpu.VMEM((2, KLEN, 256), BF16),
        pltpu.VMEM((OWN, D), BF16),
        pltpu.VMEM((D, OWN), BF16),
        pltpu.VMEM((D, OWN), BF16),
        pltpu.VMEM((D, OWN), BF16),
        pltpu.VMEM((OWN, KLEN), F32),
        pltpu.VMEM((OWN, KLEN), BF16),
        pltpu.VMEM((OWN, KLEN), BF16),
        pltpu.VMEM((OWN, KLEN), BF16),
        pltpu.VMEM((2, 2, OWN, 256), F32),
        pltpu.VMEM((2, D, SEG), BF16),
        pltpu.VMEM((2, D, SEG), F32),
        pltpu.VMEM((2, D, OWN), F32),
        pltpu.VMEM((D, KLEN), BF16),
        pltpu.VMEM((2, 2, D), F32),
        pltpu.VMEM((2, 2, 4, 1, 256), F32),
        pltpu.VMEM((MP, 2, D), F32),
        pltpu.VMEM((MP, 32, D), F32),
        pltpu.VMEM((64, D), F32),
        pltpu.VMEM((2, 8, 128), F32),
        pltpu.VMEM((4, 8, 128), F32),
        pltpu.VMEM((4, 8, 128), F32),
        pltpu.VMEM((4, 8, 128), F32),
        pltpu.VMEM((1, 1, 64, D), BF16),
        pltpu.VMEM((10, D), F32),
        pltpu.VMEM((32, 256), F32),
        pltpu.VMEM((8, 128), F32),
    ]
    scratch += [pltpu.VMEM((hi - lo, 4) + SHAPES[k], BF16) for k, _, (lo, hi), _, _ in SUM_GROUPS]
    for kind, _, _, parts, rows in SUM_GROUPS:
        width = SHAPES[kind][1]
        scratch += [pltpu.VMEM((3, hi - lo, 4, rows, width), BF16) for _, lo, hi in parts]
        scratch += [pltpu.VMEM((3, hi - lo, rows, width), BF16) for _, lo, hi in parts]
        scratch += [pltpu.VMEM((4, hi - lo, rows, width), BF16) for _, lo, hi in parts]
    for n in (7, 42, 42, 42, 42, 18, 7):
        scratch += [pltpu.SemaphoreType.DMA((n,)), pltpu.SemaphoreType.DMA((n,))]
    scratch += [pltpu.SemaphoreType.DMA((n,)) for n in (8, 2, 20)]
    return pl.pallas_call(
        backward_step,
        out_shape=[jax.ShapeDtypeStruct(s, t) for s, t in outs],
        in_specs=[hbm] * 12 + [vmem] * 17,
        out_specs=[vmem] * 5,
        scratch_shapes=scratch,
        compiler_params=pltpu.CompilerParams(
            collective_id=1, has_side_effects=True, vmem_limit_bytes=63 * 1024 * 1024
        ),
        name="backward_all",
    )(*operands)


def update_kernel(*refs):
    (
        att_w_hbm,
        att_m_hbm,
        att_a_hbm,
        ff_w_hbm,
        ff_m_hbm,
        ff_a_hbm,
        new_memory_hbm,
        att_sum_ref,
        ff_sum_ref,
        small_ref,
        parts_ref,
        att_rank_ref,
        ff_rank_ref,
        *rest,
    ) = refs[:25]
    embedding, head, inner, norm = (rest[3 * i : 3 * i + 3] for i in range(4))
    outs = refs[25:47]
    att_outs, ff_outs, new_memory_out = outs[0:4], outs[4:8], outs[8]
    embedding_outs, head_outs, inner_outs, norm_outs = (
        outs[9:12],
        outs[12:15],
        outs[15:18],
        outs[18:22],
    )
    att, ff = refs[47:51], refs[51:55]
    att_rank, ff_rank, memory_ref, load_sem, store_sem, memory_sem = refs[55:]
    loads, stores = [], []
    for l in range(2):
        for k, (sources, targets) in enumerate(
            (((ff_w_hbm, ff_m_hbm, ff_a_hbm), ff), ((att_w_hbm, att_m_hbm, att_a_hbm), att))
        ):
            for i in range(3):
                copy = pltpu.make_async_copy(
                    sources[i].at[l], targets[i].at[l], load_sem.at[6 * l + 3 * k + i]
                )
                copy.start()
                loads.append(copy)
    memory_in = pltpu.make_async_copy(new_memory_hbm, memory_ref, memory_sem.at[0])
    memory_in.start()
    att_rank[...] = spread_rank(att_rank_ref[...], D)
    ff_rank[...] = spread_rank(ff_rank_ref[...], 256)
    total = parts_ref[0]
    for m in range(1, MP):
        total = total + parts_ref[m]

    def rate(weight_square, direction_square):
        return RATE * (jnp.sqrt(weight_square) / jnp.sqrt(direction_square))

    def step(weight, direction, average, ratio):
        weight_next = weight - ratio * direction
        return weight_next, AVERAGE * average + (1.0 - AVERAGE) * weight_next

    ratios = [rate(total[i : i + 1, 0:1], total[4 + i : 5 + i, 0:1]) for i in range(4)]

    small = small_ref[lax.axis_index("mp") // 2, lax.axis_index("mp") % 2].astype(F32)
    for l in range(2):
        for k in range(2):
            at = (l * 2 + k) * HD
            row = (l, slice(k, k + 1))
            moment, direction = advance_one(small[34:35, at : at + HD], head[0][row], head[1][row])
            head_outs[1][row] = moment
            head_outs[0][row], head_outs[2][row] = step(
                head[0][row], direction, head[2][row], ratios[2]
            )
        row = slice(l, l + 1)
        moment, direction = advance_one(
            small[35:36, l * 256 : (l + 1) * 256], inner[0][row], inner[1][row]
        )
        inner_outs[1][row] = moment
        inner_outs[0][row], inner_outs[2][row] = step(
            inner[0][row], direction, inner[2][row], ratios[3]
        )
    squares = [jnp.zeros((1, D), F32), jnp.zeros((1, D), F32)]
    for i in range(5):
        for l in range(2):
            at = 8 * l + i
            row = (i, slice(l, l + 1))
            grad = small_ref[at // 4, at // 2 % 2, 32:34, :].astype(F32)[at % 2 : at % 2 + 1]
            moment, direction = advance_one(grad, norm[0][row], norm[1][row])
            norm_outs[0][row] = grad
            norm_outs[2][row] = moment
            squares[0] = squares[0] + norm[0][row] * norm[0][row]
            squares[1] = squares[1] + direction * direction
    ratio = rate(*[jnp.sum(value, axis=1, keepdims=True) for value in squares])
    for i in range(5):
        direction = norm_outs[0][i] + MOMENTUM * norm_outs[2][i]
        norm_outs[1][i], norm_outs[3][i] = step(norm[0][i], direction, norm[2][i], ratio)
    squares = [jnp.zeros((1, D), F32), jnp.zeros((1, D), F32)]
    for m in range(MP):
        rows = slice(m * 32, (m + 1) * 32)
        grad = small_ref[m // 2, m % 2, 0:32, :].astype(F32)
        moment, direction = advance_one(grad, embedding[0][rows], embedding[1][rows])
        embedding_outs[1][rows] = moment
        squares[0] = squares[0] + square_sum(embedding[0][rows])
        squares[1] = squares[1] + square_sum(direction)
    ratio = rate(*[jnp.sum(value, axis=1, keepdims=True) for value in squares])
    for m in range(MP):
        rows = slice(m * 32, (m + 1) * 32)
        grad = small_ref[m // 2, m % 2, 0:32, :].astype(F32)
        direction = grad + MOMENTUM * embedding_outs[1][rows]
        embedding_outs[0][rows], embedding_outs[2][rows] = step(
            embedding[0][rows], direction, embedding[2][rows], ratio
        )

    def advance(refs, at, total, rank, ratio):
        weight, moment, average, grad_ref = refs
        grad = masked(total.astype(F32), weight[at], rank)
        moment_next, direction = advance_one(grad, weight[at], moment[at])
        grad_ref[at] = grad
        moment[at] = moment_next
        weight[at], average[at] = step(weight[at], direction, average[at], ratio)

    for l in range(2):
        for k in range(2):
            for i in range(3):
                loads[6 * l + 3 * k + i].wait()
            if k == 0:

                def block(i, carry):
                    at = (l, i // 8, pl.ds(pl.multiple_of(i % 8 * 64, 64), 64))
                    rank = ff_rank[pl.ds(l * 16 + i, 1), :]
                    advance(ff, at, ff_sum_ref[at], rank, ratios[1])
                    return carry

                lax.fori_loop(0, 16, block, 0)
            else:

                def block(i, carry):
                    rank = att_rank[pl.ds(l * 5 + i, 1), :]
                    advance(att, (l, i), att_sum_ref[l, i], rank, ratios[0])
                    return carry

                lax.fori_loop(0, 5, block, 0)
            sources, targets = ((ff, ff_outs), (att, att_outs))[k]
            for i, source in enumerate((3, 0, 1, 2)):
                copy = pltpu.make_async_copy(
                    sources[source].at[l], targets[i].at[l], store_sem.at[8 * l + 4 * k + i]
                )
                copy.start()
                stores.append(copy)
    memory_in.wait()
    memory_back = pltpu.make_async_copy(memory_ref, new_memory_out, memory_sem.at[1])
    memory_back.start()
    for copy in stores:
        copy.wait()
    memory_back.wait()


def update(*operands):
    att, ff = (2, 5, HD, D), (2, 2, D, 256)
    shapes = [att] * 4 + [ff] * 4
    rest = [(VOCAB, D)] * 3 + [(2, 2, HD)] * 3 + [(2, 256)] * 3 + [(5, 2, D)] * 4
    return pl.pallas_call(
        update_kernel,
        out_shape=[jax.ShapeDtypeStruct(s, F32) for s in shapes]
        + [jax.ShapeDtypeStruct((2, 4, SEG, D), BF16)]
        + [jax.ShapeDtypeStruct(s, F32) for s in rest],
        in_specs=[ANY_SPEC] * 7 + [VMEM_SPEC] * 18,
        out_specs=[ANY_SPEC] * 9 + [VMEM_SPEC] * 13,
        scratch_shapes=[pltpu.VMEM(att, F32)] * 4
        + [pltpu.VMEM(ff, F32)] * 4
        + [
            pltpu.VMEM((10, D), F32),
            pltpu.VMEM((32, 256), F32),
            pltpu.VMEM((2, 4, SEG, D), BF16),
            pltpu.SemaphoreType.DMA((12,)),
            pltpu.SemaphoreType.DMA((16,)),
            pltpu.SemaphoreType.DMA((2,)),
        ],
        compiler_params=pltpu.CompilerParams(vmem_limit_bytes=62 * 1024 * 1024),
        name="update",
    )(*operands)


def body(
    inputs,
    targets,
    valid_mask,
    memory,
    attention_rank,
    feedforward_rank,
    attention_weight,
    attention_moment,
    attention_average,
    feedforward_weight,
    feedforward_moment,
    feedforward_average,
    embedding_weight,
    embedding_moment,
    embedding_average,
    head_bias_weight,
    head_bias_moment,
    head_bias_average,
    inner_bias_weight,
    inner_bias_moment,
    inner_bias_average,
    norm_weight,
    norm_moment,
    norm_average,
):
    def turned(value):
        return value.transpose(0, 1, 3, 2)

    def swapped(value):
        return value.transpose(1, 0, 2)

    att_rank = attention_rank.reshape(10, 8).astype(F32)
    ff_rank = feedforward_rank.reshape(32, 4).astype(F32)
    table = tables()
    (
        att_got,
        ff_got,
        new_memory,
        probs,
        bias_got,
        count_got,
        lows,
        query_u,
        query_w,
        mixed,
        normed_one,
        inverse_one,
        normed_two,
        inverse_two,
        grad_hidden,
        grad_embedding,
        ce_local,
    ) = forward_all(
        turned(attention_weight),
        feedforward_weight,
        att_rank,
        ff_rank,
        head_bias_weight,
        inner_bias_weight,
        embedding_weight,
        inputs,
        targets,
        valid_mask,
        memory,
        swapped(norm_weight),
        table,
    )
    valid_count = count_got[0, 0]
    grad_attention, grad_feedforward, grad_small, ce_got, parts = backward_all(
        att_got,
        ff_got,
        probs,
        memory,
        table,
        grad_hidden,
        grad_embedding,
        normed_two,
        turned(attention_weight),
        turned(attention_moment),
        feedforward_weight,
        feedforward_moment,
        att_rank,
        ff_rank,
        head_bias_weight,
        head_bias_moment,
        inner_bias_weight,
        inner_bias_moment,
        bias_got,
        swapped(norm_weight),
        inputs,
        ce_local,
        lows,
        query_u,
        query_w,
        mixed,
        normed_one,
        inverse_one,
        inverse_two,
    )
    updated = update(
        turned(attention_weight),
        turned(attention_moment),
        turned(attention_average),
        feedforward_weight,
        feedforward_moment,
        feedforward_average,
        new_memory,
        grad_attention,
        grad_feedforward,
        grad_small,
        parts,
        att_rank,
        ff_rank,
        embedding_weight,
        embedding_moment,
        embedding_average,
        head_bias_weight,
        head_bias_moment,
        head_bias_average,
        inner_bias_weight,
        inner_bias_moment,
        inner_bias_average,
        swapped(norm_weight),
        swapped(norm_moment),
        swapped(norm_average),
    )
    return (
        ce_got[0, 0],
        valid_count,
        updated[8],
        *[turned(value) for value in updated[0:4]],
        *updated[4:8],
        *updated[9:18],
        *[swapped(value) for value in updated[18:22]],
    )


def solution(mesh):
    rows = P("dp", None)
    matrix = P(None, None, None, "mp")
    split_two = P(None, None, "mp")
    split_one = P(None, "mp")
    whole = P()
    return jax.shard_map(
        body,
        mesh=mesh,
        in_specs=(
            (rows,) * 3
            + (P(None, "dp", None, None),)
            + (matrix,) * 8
            + (whole,) * 3
            + (split_two,) * 3
            + (split_one,) * 3
            + (whole,) * 3
        ),
        out_specs=(
            (whole,) * 2
            + (P(None, "dp", None, None),)
            + (matrix,) * 8
            + (whole,) * 3
            + (split_two,) * 3
            + (split_one,) * 3
            + (whole,) * 4
        ),
        check_vma=False,
    )
```

```python
import functools

import jax
import jax.numpy as jnp
import numpy as np
from jax import lax
from jax.experimental import pallas as pl
from jax.experimental.pallas import tpu as pltpu
from jax.sharding import PartitionSpec as P

HD = 64
D = 512
FF = 2048
SEG = 512
KLEN = 1024
OWN = 256
HEADS = 8
VOCAB = 256
MP = 8

EPSILON = 1e-05
MOMENTUM = 0.9
AVERAGE = 0.9
RATE = 0.3
PENALTY = 0.0001
WIDEN = 5.0
F32 = jnp.float32
BF16 = jnp.bfloat16
SCALE = HD ** (-0.5)


def dot_nn(a, b):
    return lax.dot_general(a, b, (((1,), (0,)), ((), ())), preferred_element_type=F32)


def dot_nt(a, b):
    return lax.dot_general(a, b, (((1,), (1,)), ((), ())), preferred_element_type=F32)


def smooth_unit(v):
    return 0.5 * v * (1.0 + jnp.tanh(0.7978845608028654 * (v + 0.044715 * v * v * v)))


def smooth_both(v):
    squared = v * v
    t = jnp.tanh(0.7978845608028654 * (v + 0.044715 * squared * v))
    half = 0.5 * (1.0 + t)
    slope = half + 0.5 * v * (1.0 - t * t) * (
        0.7978845608028654 * (1.0 + 3.0 * 0.044715 * squared)
    )
    return v * half, slope


def tables():
    freq = (1.0 / 10000.0 ** (np.arange(0, D, 2).astype(np.float32) / np.float32(D))).astype(
        np.float32
    )
    turned = []
    for half in range(2):
        distance = (SEG + half * OWN - np.arange(KLEN)) % KLEN
        angle = (distance.astype(np.float32)[:, None] * freq[None, :]).astype(np.float64)
        turned.append(np.concatenate([np.sin(angle), np.cos(angle)], axis=1).astype(np.float32))
    return jnp.asarray(np.stack(turned), BF16)


def norm_forward(values):
    centred = values - jnp.mean(values, axis=-1, keepdims=True)
    inverse = lax.rsqrt(jnp.mean(centred * centred, axis=-1, keepdims=True) + EPSILON)
    return centred * inverse, inverse


def norm_backward(grad, normed, inverse, gain):
    scaled = grad * gain
    grad_in = inverse * (
        scaled
        - jnp.mean(scaled, axis=-1, keepdims=True)
        - normed * jnp.mean(scaled * normed, axis=-1, keepdims=True)
    )
    return (
        grad_in,
        jnp.sum(grad * normed, axis=0, keepdims=True),
        jnp.sum(grad, axis=0, keepdims=True),
    )


def transposed(value):
    return value.astype(F32).T


ROWS = 64
VMEM_SPEC = pl.BlockSpec(memory_space=pltpu.VMEM)
VMEM_LIMIT = 60 * 1024 * 1024


ANY_SPEC = pl.BlockSpec(memory_space=pl.ANY)
MESH = pl.DeviceIdType.MESH

ATT, FFN, SMALL = 0, 1, 2
GROUPS = (
    (ATT, 0, (("z", 0, 3), ("x", 3, 5)), 16),
    (FFN, 0, (("z", 0, 1), ("x", 1, 2)), 128),
    (ATT, 1, (("z", 0, 2), ("x", 2, 5)), 16),
    (FFN, 1, (("z", 0, 1), ("x", 1, 2)), 128),
)
SUM_GROUPS = (
    (ATT, 0, (0, 4), (("z", 0, 2), ("x", 2, 4)), 16),
    (FFN, 0, (0, 2), (("z", 0, 1), ("x", 1, 2)), 128),
    (ATT, 1, (0, 4), (("z", 0, 2), ("x", 2, 4)), 16),
    (FFN, 1, (0, 2), (("z", 0, 1), ("x", 1, 2)), 128),
    (SMALL, 0, (0, 1), (("z", 0, 1),), 16),
    (ATT, 0, (4, 5), (("z", 0, 1),), 16),
    (ATT, 1, (4, 5), (("x", 0, 1),), 16),
)


class Place:
    def __init__(self):
        dp, mp = lax.axis_index("dp"), lax.axis_index("mp")
        self.x, self.z = dp // 4, dp % 4
        self.y, self.core = mp // 2, mp % 2

    def device(self, x=None, z=None, y=None, core=None):
        x = self.x if x is None else x
        z = self.z if z is None else z
        y = self.y if y is None else y
        core = self.core if core is None else core
        return {"dp": x * 4 + z, "mp": y * 2 + core}

    def along(self, axis, shift):
        return self.device(**{axis: (getattr(self, axis) + shift + 4) % 4})

    def sibling(self):
        return self.device(core=1 - self.core)

    def greet(self, more=()):
        partners = [self.along(axis, s) for axis in "xzy" for s in (1, 2, 3)]
        partners += [self.sibling(), *more]
        barrier = pltpu.get_barrier_semaphore()
        for partner in partners:
            pl.semaphore_signal(barrier, inc=1, device_id=partner, device_id_type=MESH)

    def greeted(self, count=10):
        pl.semaphore_wait(pltpu.get_barrier_semaphore(), count)


def send(source, target, sems, index, device):
    copy = pltpu.make_async_remote_copy(
        src_ref=source,
        dst_ref=target,
        send_sem=sems[0].at[index],
        recv_sem=sems[1].at[index],
        device_id=device,
        device_id_type=MESH,
    )
    copy.start()
    return copy


def spread_rank(rank, width):
    blocks = rank.shape[1]
    lane = lax.broadcasted_iota(jnp.int32, (blocks, width), 1) // (width // blocks)
    row = lax.broadcasted_iota(jnp.int32, (blocks, width), 0)
    return dot_nn(rank, jnp.where(lane == row, 1.0, 0.0))


def advance_one(grad, weight, moment):
    moment_next = MOMENTUM * moment + grad
    return moment_next, grad + MOMENTUM * moment_next


def masked(grad, weight, rank):
    coefficient = jnp.where(rank < 1.5, 1.0, jnp.where(rank < 2.5, WIDEN, 0.0))
    return jnp.where(rank < 2.5, grad, 0.0) + (2.0 * PENALTY) * weight * coefficient


def square_sum(value):
    return jnp.sum(value * value, axis=0, keepdims=True)


class Weights:
    def __init__(self, here, sources, targets, sems, local_sem):
        self.here, self.sources, self.targets = here, sources, targets
        self.sems, self.local_sem = sems, local_sem
        self.copies = [[None] * len(GROUPS) for _ in range(3)]
        self.local = [None] * len(GROUPS)

    def slice_at(self, axis, rows):
        return pl.ds(pl.multiple_of(getattr(self.here, axis) * rows, rows), rows)

    def one(self, g):
        kind, layer, parts, rows = GROUPS[g]
        source, target = self.sources[kind].at[layer], self.targets[kind].at[layer]
        self.local[g] = pltpu.make_async_copy(source, target.at[:, 0, 0], self.local_sem.at[g])
        self.local[g].start()
        self.copies[0][g] = [
            send(
                source.at[low:high, self.slice_at(axis, rows)],
                target.at[low:high, 0, r, self.slice_at(axis, rows)],
                self.sems[0],
                g * 6 + p * 3 + r - 1,
                self.here.along("y", -r),
            )
            for p, (axis, low, high) in enumerate(parts)
            for r in (1, 2, 3)
        ]

    def two(self, g):
        kind, layer, parts, rows = GROUPS[g]
        target = self.targets[kind].at[layer]
        for copy in self.copies[0][g]:
            copy.wait_recv()
        self.copies[1][g] = []
        for p, (axis, low, high) in enumerate(parts):
            part = target.at[low:high, 0, 1:4, self.slice_at(axis, rows)]
            for s in (1, 2, 3):
                self.copies[1][g].append(
                    send(part, part, self.sems[1], g * 6 + p * 3 + s - 1, self.here.along(axis, s))
                )

    def three(self, g):
        kind, layer, _, _ = GROUPS[g]
        target = self.targets[kind].at[layer]
        for copy in self.copies[1][g]:
            copy.wait_recv()
        self.local[g].wait()
        self.copies[2][g] = [
            send(target.at[:, 0], target.at[:, 1], self.sems[2], g, self.here.sibling())
        ]

    def load(self, g, buffer, sem):
        kind, layer, _, _ = GROUPS[g]
        self.copies[2][g][0].wait_recv()
        copy = pltpu.make_async_copy(self.targets[kind].at[layer], buffer, sem)
        copy.start()
        return copy

    def end(self):
        for stage in self.copies:
            for copies in stage:
                for copy in copies:
                    copy.wait_send()


def forward_step(
    att_weight_ref,
    ff_weight_ref,
    att_rank_ref,
    ff_rank_ref,
    head_bias_ref,
    inner_bias_ref,
    embedding_ref,
    inputs_ref,
    targets_ref,
    valid_ref,
    memory_ref,
    norm_ref,
    table_hbm,
    att_out,
    ff_out,
    new_memory_ref,
    prob_out,
    bias_out,
    count_out,
    low_out,
    query_u_out,
    query_w_out,
    mixed_out,
    normed_one_out,
    inverse_one_out,
    normed_two_out,
    inverse_two_out,
    grad_ref,
    grad_embedding_ref,
    ce_ref,
    att_ref,
    ff_ref,
    bias_ref,
    count_ref,
    rank_ref,
    block_rank_ref,
    count_z,
    count_x,
    att_w,
    ff_w,
    memory_w,
    table_ref,
    turned_ref,
    embed_ref,
    keys_ref,
    values_ref,
    rel_ref,
    score_ref,
    prob_ref,
    low_prob_ref,
    part_ref,
    hidden_ref,
    first_send,
    first_recv,
    second_send,
    second_recv,
    third_send,
    third_recv,
    extra_send,
    extra_recv,
    local_sem,
    load_sem,
    prob_sem,
):
    here = Place()
    here.greet()
    extra = (extra_send, extra_recv)
    rank_ref[...] = spread_rank(att_rank_ref[...], D)
    block_rank_ref[...] = spread_rank(ff_rank_ref[...], 256)

    def mask_attention(layer):
        for i in range(5):
            kept = rank_ref[layer * 5 + i : layer * 5 + i + 1, :] < 1.5
            att_ref[layer, i] = jnp.where(kept, att_weight_ref[layer, i], 0.0).astype(BF16)

    def mask_feedforward(layer):
        for i in range(16):
            kept = block_rank_ref[layer * 16 + i : layer * 16 + i + 1, :] < 1.5
            rows = slice(i % 8 * 64, i % 8 * 64 + 64)
            ff_ref[layer, i // 8, rows, :] = jnp.where(
                kept, ff_weight_ref[layer, i // 8, rows, :], 0.0
            ).astype(BF16)

    mask_attention(0)
    here.greeted()
    weights = Weights(
        here,
        (att_ref, ff_ref),
        (att_out, ff_out),
        ((first_send, first_recv), (second_send, second_recv), (third_send, third_recv)),
        local_sem,
    )
    weights.one(0)
    mask_feedforward(0)
    weights.one(1)
    counted = jnp.sum(valid_ref[...].astype(F32), axis=1, keepdims=True)
    count_ref[...] = jnp.broadcast_to(jnp.sum(counted, axis=0, keepdims=True), (8, 128))
    bias_ref[6:8, :] = jnp.zeros((2, 128), F32)
    for l in range(2):
        bias_ref[3 * l : 3 * l + 1, :] = jnp.concatenate(
            [head_bias_ref[l, k : k + 1, :] for k in range(2)], axis=1
        )
        for k in range(2):
            bias_ref[3 * l + 1 + k : 3 * l + 2 + k, :] = inner_bias_ref[
                l : l + 1, k * 128 : (k + 1) * 128
            ]
    count_z[here.z] = count_ref[...]
    count_copies = [
        send(count_ref, count_z.at[here.z], extra, s - 1, here.along("z", s)) for s in (1, 2, 3)
    ]
    bias_copies = [
        send(bias_ref, bias_out.at[0, r], extra, 2 + r, here.along("y", -r)) for r in (1, 2, 3)
    ]
    bias_out[0, 0] = bias_ref[...]
    mask_attention(1)
    weights.one(2)
    mask_feedforward(1)
    weights.one(3)
    loads = [
        pltpu.make_async_copy(table_hbm.at[here.core], table_ref, load_sem.at[0]),
        pltpu.make_async_copy(memory_ref.at[0, here.y], memory_w.at[0], load_sem.at[1]),
        pltpu.make_async_copy(memory_ref.at[1, here.y], memory_w.at[1], load_sem.at[2]),
    ]
    for copy in loads:
        copy.start()

    own_rows = pl.ds(pl.multiple_of(here.core * OWN, OWN), OWN)
    turned_ref[...] = jnp.zeros_like(turned_ref)
    turned_ref[0:4, :] = inputs_ref[...].astype(F32)
    turned_ref[8:12, :] = targets_ref[...].astype(F32)
    turned_ref[16:20, :] = valid_ref[...].astype(F32)
    columns = turned_ref[...].T
    turned_ref[:, 0:128] = columns[0:128]
    turned_ref[:, 128:256] = columns[128:256]
    turned_ref[:, 256:384] = columns[256:384]
    turned_ref[:, 384:512] = columns[384:512]
    embedding = embedding_ref[...]
    embedding_low = embedding.astype(BF16)
    vocab_id = lax.broadcasted_iota(jnp.int32, (128, VOCAB), 1).astype(F32)

    def onehot(column):
        return jnp.where(column == vocab_id, 1.0, 0.0)

    for segment in range(4):
        for b in range(4):
            tokens = turned_ref[:, b * 128 + segment : b * 128 + segment + 1]
            embed_ref[segment, b * 128 : (b + 1) * 128, :] = dot_nn(
                onehot(tokens).astype(BF16), embedding_low
            ).astype(BF16)
    memory_zero = pltpu.make_async_copy(embed_ref, new_memory_ref.at[0], load_sem.at[3])
    memory_zero.start()
    weights.two(0)
    low_out[0] = embed_ref[here.y]
    rest_one = embedding - embedding_low.astype(F32)
    middle_part = rest_one.astype(BF16)
    rest_two = (rest_one - middle_part.astype(F32)).astype(BF16)
    lane = lax.broadcasted_iota(jnp.int32, (128, 128), 1)
    own_targets, own_valid = [], []
    for b in range(2):
        block = turned_ref[:, pl.ds(pl.multiple_of(here.core * 256 + b * 128, 128), 128)]

        def column(at):
            return jnp.sum(jnp.where(lane == here.y + at, block, 0.0), axis=1, keepdims=True)

        mine = onehot(column(0)).astype(BF16)
        hidden_ref[b * 128 : (b + 1) * 128, :] = (
            dot_nn(mine, embedding_low) + dot_nn(mine, middle_part)
        ) + dot_nn(mine, rest_two)
        own_targets.append(onehot(column(8)))
        own_valid.append(column(16))
    weights.three(0)
    for copy in bias_copies:
        copy.wait_recv()
    bias_last = send(bias_out.at[0], bias_out.at[1], extra, 6, here.sibling())
    for copy in count_copies:
        copy.wait_recv()
    count_x[here.x] = (count_z[0] + count_z[1]) + (count_z[2] + count_z[3])
    count_last = [
        send(count_x.at[here.x], count_x.at[here.x], extra, 6 + s, here.along("x", s))
        for s in (1, 2, 3)
    ]
    weights.two(1)
    for copy in loads:
        copy.wait()
    bias_last.wait_recv()
    pending = []
    offset = here.core * OWN
    lane_head = lax.broadcasted_iota(jnp.int32, (OWN, 256), 1) // HD

    def project(layer):
        own_low = hidden_ref[...].astype(BF16)
        query = dot_nt(own_low, att_w[layer, 0].reshape(D, D))
        for which, target in ((0, query_u_out), (1, query_w_out)):
            bias = jnp.concatenate(
                [
                    bias_out[cc, r, 3 * layer : 3 * layer + 1, which * HD : (which + 1) * HD]
                    for cc in range(2)
                    for r in range(4)
                ],
                axis=1,
            )
            target[layer] = (query + bias).astype(BF16)
        key_w, value_w = att_w[layer, 1].reshape(D, D), att_w[layer, 2].reshape(D, D)
        for half in range(2):
            rows = memory_w[layer] if half == 0 else low_out[layer]
            cols = slice(half * SEG, (half + 1) * SEG)
            keys_ref[:, cols] = dot_nt(key_w, rows).astype(BF16)
            values = dot_nt(rows, value_w).astype(BF16)
            values_ref[0, cols, :] = values[:, 0:256]
            values_ref[1, cols, :] = values[:, 256:512]
        rel_ref[...] = dot_nt(att_w[layer, 3].reshape(D, D), table_ref[...]).astype(BF16)
        part_ref[...] = jnp.zeros_like(part_ref)

    def head(layer):
        def run(h, carry):
            group = h // 4
            slot = h % 2
            mine = lane_head == h % 4
            lanes = pl.ds(pl.multiple_of(group * 256, 256), 256)
            query_u = query_u_out[layer, :, lanes].astype(F32) * SCALE
            query_u = jnp.where(mine, query_u, 0.0).astype(BF16)
            query_w = query_w_out[layer, :, lanes].astype(F32) * SCALE
            query_w = jnp.where(mine, query_w, 0.0).astype(BF16)
            score_ref[...] = dot_nn(query_w, rel_ref[lanes, :])

            @pl.when(h >= 2)
            def _():
                pltpu.make_async_copy(
                    prob_ref.at[slot], prob_out.at[layer, h], prob_sem.at[slot]
                ).wait()

            prob_ref[slot] = dot_nn(query_u, keys_ref[lanes, :])
            for b in range(0, OWN, ROWS):
                rows = slice(b, b + ROWS)
                moved = pltpu.roll(score_ref[rows, :], b, 1, stride=1, stride_axis=0)
                score = prob_ref[slot, rows, :] + moved
                key_id = lax.broadcasted_iota(jnp.int32, (ROWS, SEG), 1)
                query_id = lax.broadcasted_iota(jnp.int32, (ROWS, SEG), 0) + (offset + b)
                near = jnp.where(key_id <= query_id, score[:, SEG:], -1e30)
                score = jnp.concatenate([score[:, :SEG], near], axis=1)
                expo = jnp.exp(score - jnp.max(score, axis=-1, keepdims=True))
                prob = expo * (1.0 / jnp.sum(expo, axis=-1, keepdims=True))
                prob_ref[slot, rows, :] = prob
                low_prob_ref[rows, :] = prob.astype(BF16)
            pltpu.make_async_copy(
                prob_ref.at[slot], prob_out.at[layer, h], prob_sem.at[slot]
            ).start()
            mixed = dot_nn(low_prob_ref[...], values_ref[group])
            part_ref[group] = part_ref[group] + jnp.where(mine, mixed, 0.0)
            return carry

        return run

    def attend(layer):
        for slot in range(2):
            pltpu.make_async_copy(
                prob_ref.at[slot], prob_out.at[layer, 6 + slot], prob_sem.at[slot]
            ).wait()
        mixed_out[layer, :, 0:256] = part_ref[0].astype(BF16)
        mixed_out[layer, :, 256:512] = part_ref[1].astype(BF16)
        attended = dot_nn(mixed_out[layer], att_w[layer, 4].reshape(D, D))
        normed_one, inverse_one = norm_forward(hidden_ref[...] + attended)
        normed_one_out[layer] = normed_one
        inverse_one_out[layer] = inverse_one
        return normed_one * norm_ref[0, layer : layer + 1, :] + norm_ref[1, layer : layer + 1, :]

    def feed(layer, middle):
        middle_low = middle.astype(BF16)
        branch = jnp.zeros((OWN, D), F32)
        for cc in range(2):
            for r in range(4):
                bias = jnp.concatenate(
                    [bias_out[cc, r, 3 * layer + 1 + i : 3 * layer + 2 + i, :] for i in range(2)],
                    axis=1,
                )
                inner = dot_nn(middle_low, ff_w[layer, 0, cc, r]) + bias
                branch = branch + dot_nt(smooth_unit(inner).astype(BF16), ff_w[layer, 1, cc, r])
        normed_two, inverse_two = norm_forward(middle + (branch + norm_ref[4, layer : layer + 1, :]))
        normed_two_out[layer] = normed_two
        inverse_two_out[layer] = inverse_two
        hidden_ref[...] = normed_two * norm_ref[2, layer : layer + 1, :] + norm_ref[3, layer : layer + 1, :]

    weights.load(0, att_w.at[0], load_sem.at[4]).wait()
    project(0)
    weights.two(2)
    lax.fori_loop(0, 4, head(0), 0)
    weights.three(1)
    weights.two(3)
    lax.fori_loop(4, 8, head(0), 0)
    weights.three(2)
    feed_load = weights.load(1, ff_w.at[0], load_sem.at[5])
    middle = attend(0)
    feed_load.wait()
    feed(0, middle)
    low_out[1, own_rows, :] = hidden_ref[...].astype(BF16)
    own_low = low_out.at[1, own_rows]
    swap = send(own_low, own_low, extra, 10, here.sibling())
    spread_at = new_memory_ref.at[1, here.y, own_rows]
    spread = [send(own_low, spread_at, extra, 10 + s, here.along("y", s)) for s in (1, 2, 3)]
    spread_own = pltpu.make_async_copy(own_low, spread_at, load_sem.at[6])
    spread_own.start()
    attention_one = weights.load(2, att_w.at[1], load_sem.at[7])
    swap.wait_recv()
    attention_one.wait()
    project(1)
    lax.fori_loop(0, 4, head(1), 0)
    weights.three(3)
    for copy in spread:
        copy.wait_recv()
    spread_own.wait()
    spread_all = new_memory_ref.at[1, :, own_rows]
    spread_last = send(spread_all, spread_all, extra, 14, here.sibling())
    lax.fori_loop(4, 8, head(1), 0)
    feed_load = weights.load(3, ff_w.at[1], load_sem.at[5])
    middle = attend(1)
    feed_load.wait()
    feed(1, middle)
    for copy in count_last:
        copy.wait_recv()
    count_all = (count_x[0] + count_x[1]) + (count_x[2] + count_x[3])
    count_out[...] = count_all

    final_low = hidden_ref[...].astype(BF16)
    logit_scale = D ** (-0.5)
    logits = dot_nt(final_low, embedding_low) * logit_scale
    picked = jnp.concatenate(own_targets, axis=0)
    valid = jnp.concatenate(own_valid, axis=0)
    peak = jnp.max(logits, axis=-1, keepdims=True)
    log_total = peak + jnp.log(jnp.sum(jnp.exp(logits - peak), axis=-1, keepdims=True))
    losses = valid * (log_total - jnp.sum(logits * picked, axis=-1, keepdims=True))
    ce_ref[...] = jnp.broadcast_to(jnp.sum(losses, axis=0, keepdims=True), (8, 128))
    grad_logits = (valid * (jnp.exp(logits - log_total) - picked) / count_all[0:1, 0:1]).astype(
        BF16
    )
    grad_ref[...] = dot_nn(grad_logits, embedding_low) * logit_scale
    grad_embedding_ref[...] = (
        dot_nn(transposed(grad_logits).astype(BF16), final_low) * logit_scale
    ).reshape(MP, 32, D)
    memory_zero.wait()
    spread_last.wait()
    for copy in count_copies + bias_copies + [bias_last] + count_last + [swap] + spread:
        copy.wait_send()
    weights.end()


def forward_all(*operands):
    vmem, hbm = VMEM_SPEC, ANY_SPEC
    outs = [
        (hbm, (2, 5, 2, 4, HD, D), BF16),
        (hbm, (2, 2, 2, 4, D, 256), BF16),
        (hbm, (2, 4, SEG, D), BF16),
        (hbm, (2, HEADS, OWN, KLEN), F32),
        (vmem, (2, 4, 8, 128), F32),
        (vmem, (8, 128), F32),
        (vmem, (2, SEG, D), BF16),
        (vmem, (2, OWN, D), BF16),
        (vmem, (2, OWN, D), BF16),
        (vmem, (2, OWN, D), BF16),
        (vmem, (2, OWN, D), F32),
        (vmem, (2, OWN, 1), F32),
        (vmem, (2, OWN, D), F32),
        (vmem, (2, OWN, 1), F32),
        (vmem, (OWN, D), F32),
        (vmem, (MP, 32, D), F32),
        (vmem, (8, 128), F32),
    ]
    return pl.pallas_call(
        forward_step,
        out_shape=[jax.ShapeDtypeStruct(s, t) for _, s, t in outs],
        in_specs=[vmem] * 10 + [hbm, vmem, hbm],
        out_specs=[m for m, _, _ in outs],
        scratch_shapes=[
            pltpu.VMEM((2, 5, HD, D), BF16),
            pltpu.VMEM((2, 2, D, 256), BF16),
            pltpu.VMEM((8, 128), F32),
            pltpu.VMEM((8, 128), F32),
            pltpu.VMEM((10, D), F32),
            pltpu.VMEM((32, 256), F32),
            pltpu.VMEM((4, 8, 128), F32),
            pltpu.VMEM((4, 8, 128), F32),
            pltpu.VMEM((2, 5, 2, 4, HD, D), BF16),
            pltpu.VMEM((2, 2, 2, 4, D, 256), BF16),
            pltpu.VMEM((2, SEG, D), BF16),
            pltpu.VMEM((KLEN, D), BF16),
            pltpu.VMEM((128, SEG), F32),
            pltpu.VMEM((4, SEG, D), BF16),
            pltpu.VMEM((D, KLEN), BF16),
            pltpu.VMEM((2, KLEN, 256), BF16),
            pltpu.VMEM((D, KLEN), BF16),
            pltpu.VMEM((OWN, KLEN), F32),
            pltpu.VMEM((2, OWN, KLEN), F32),
            pltpu.VMEM((OWN, KLEN), BF16),
            pltpu.VMEM((2, OWN, 256), F32),
            pltpu.VMEM((OWN, D), F32),
            pltpu.SemaphoreType.DMA((24,)),
            pltpu.SemaphoreType.DMA((24,)),
            pltpu.SemaphoreType.DMA((24,)),
            pltpu.SemaphoreType.DMA((24,)),
            pltpu.SemaphoreType.DMA((4,)),
            pltpu.SemaphoreType.DMA((4,)),
            pltpu.SemaphoreType.DMA((15,)),
            pltpu.SemaphoreType.DMA((15,)),
            pltpu.SemaphoreType.DMA((4,)),
            pltpu.SemaphoreType.DMA((8,)),
            pltpu.SemaphoreType.DMA((2,)),
        ],
        compiler_params=pltpu.CompilerParams(
            collective_id=0, has_side_effects=True, vmem_limit_bytes=VMEM_LIMIT
        ),
        name="forward_all",
    )(*operands)


SHAPES = {ATT: (HD, D), FFN: (D, 256), SMALL: (64, D)}


class Sums:
    def __init__(self, here, arrays, outs, buffers, sems):
        self.here, self.arrays, self.outs = here, arrays, outs
        self.pairs, self.ones, self.twos, self.threes = buffers
        self.sems = sems
        self.copies = [[[] for _ in SUM_GROUPS] for _ in range(5)]

    def slice_at(self, index, rows):
        return pl.ds(pl.multiple_of(index * rows, rows), rows)

    def arrived(self, stage, g):
        for copy in self.copies[stage][g]:
            copy.wait_recv()

    def pair(self, g):
        kind, layer, (base, end), _, _ = SUM_GROUPS[g]
        self.copies[0][g].append(
            send(
                self.arrays[kind].at[layer, base:end, 1],
                self.pairs[g],
                self.sems[0],
                g,
                self.here.sibling(),
            )
        )

    def one(self, g):
        kind, layer, (base, _), parts, rows = SUM_GROUPS[g]
        self.arrived(0, g)
        pair = self.pairs[g]
        for m in range(pair.shape[0]):
            for r in range(4):
                pair[m, r] = (
                    pair[m, r].astype(F32) + self.arrays[kind][layer, base + m, 0, r].astype(F32)
                ).astype(BF16)
        for p, (axis, low, high) in enumerate(parts):
            for s in (1, 2, 3):
                goal = (getattr(self.here, axis) + s) % 4
                self.copies[1][g].append(
                    send(
                        pair.at[low:high, :, self.slice_at(goal, rows)],
                        self.ones[g][p].at[s - 1],
                        self.sems[1],
                        g * 6 + p * 3 + s - 1,
                        self.here.along(axis, s),
                    )
                )

    def two(self, g):
        kind, layer, (base, _), parts, rows = SUM_GROUPS[g]
        self.arrived(1, g)
        for p, (axis, low, high) in enumerate(parts):
            got = self.ones[g][p]
            own = self.pairs[g].at[low:high, :, self.slice_at(getattr(self.here, axis), rows)]
            for m in range(high - low):
                for r in range(4):
                    got[0, m, r] = (
                        (own[m, r].astype(F32) + got[0, m, r].astype(F32))
                        + (got[1, m, r].astype(F32) + got[2, m, r].astype(F32))
                    ).astype(BF16)
            for r in (1, 2, 3):
                self.copies[2][g].append(
                    send(
                        got.at[0, :, r],
                        self.twos[g][p].at[r - 1],
                        self.sems[2],
                        g * 6 + p * 3 + r - 1,
                        self.here.along("y", r),
                    )
                )

    def three(self, g):
        kind, layer, (base, _), parts, rows = SUM_GROUPS[g]
        self.arrived(2, g)
        for p, (axis, low, high) in enumerate(parts):
            other = "x" if axis == "z" else "z"
            got, every = self.twos[g][p], self.threes[g][p]
            index = getattr(self.here, other)
            for m in range(high - low):
                every[index, m] = (
                    (self.ones[g][p][0, m, 0].astype(F32) + got[0, m].astype(F32))
                    + (got[1, m].astype(F32) + got[2, m].astype(F32))
                ).astype(BF16)
            for s in (1, 2, 3):
                self.copies[3][g].append(
                    send(
                        every.at[index],
                        every.at[index],
                        self.sems[3],
                        g * 6 + p * 3 + s - 1,
                        self.here.along(other, s),
                    )
                )

    def four(self, g):
        kind, layer, (base, _), parts, rows = SUM_GROUPS[g]
        self.arrived(3, g)
        for p, (axis, low, high) in enumerate(parts):
            every = self.threes[g][p]
            part = self.slice_at(getattr(self.here, axis), rows)
            for m in range(high - low):
                self.outs[kind][layer, base + low + m, part] = (
                    (every[0, m].astype(F32) + every[1, m].astype(F32))
                    + (every[2, m].astype(F32) + every[3, m].astype(F32))
                ).astype(BF16)
            target = self.outs[kind].at[layer, base + low : base + high, part]
            for s in (1, 2, 3):
                self.copies[4][g].append(
                    send(
                        target,
                        target,
                        self.sems[4],
                        g * 6 + p * 3 + s - 1,
                        self.here.along(axis, s),
                    )
                )

    def end(self):
        for stage in self.copies:
            for copies in stage:
                for copy in copies:
                    copy.wait_send()


def backward_step(
    att_hbm,
    ff_hbm,
    prob_hbm,
    memory_hbm,
    table_hbm,
    grad_hbm,
    grad_embedding_hbm,
    normed_two_hbm,
    att_weight_hbm,
    att_moment_hbm,
    ff_weight_hbm,
    ff_moment_hbm,
    att_rank_ref,
    ff_rank_ref,
    head_weight_ref,
    head_moment_ref,
    inner_weight_ref,
    inner_moment_ref,
    bias_ref,
    norm_ref,
    inputs_ref,
    ce_ref,
    low_ref,
    query_u_ref,
    query_w_ref,
    mixed_ref,
    normed_one_ref,
    inverse_one_ref,
    inverse_two_ref,
    att_out,
    ff_out,
    small_out,
    ce_out,
    parts_out,
    att_w,
    ff_w,
    memory_w,
    table_ref,
    prob_ref,
    grad_att_ref,
    grad_ff_ref,
    grad_small_ref,
    grad_ref,
    keys_ref,
    values_ref,
    rel_ref,
    gmix_ref,
    gmix_t_ref,
    query_t_ref,
    flip_t_ref,
    prob_grad_ref,
    score_grad_ref,
    low_prob_ref,
    flipped_ref,
    gquery_ref,
    gmemory_ref,
    ghidden_ref,
    got_ref,
    grel_ref,
    grad_bias_ref,
    grad_inner_ref,
    grad_norm_ref,
    ranked_ref,
    block_ref,
    ce_pair,
    ce_z,
    ce_y,
    ce_x,
    small_own,
    rank_ref,
    block_rank_ref,
    part_ref,
    *scratch,
):
    here = Place()
    scratch = list(scratch)
    pairs = [scratch.pop(0) for _ in SUM_GROUPS]
    ones, twos, threes = [], [], []
    for group in SUM_GROUPS:
        for buffers in (ones, twos, threes):
            buffers.append([scratch.pop(0) for _ in group[3]])
    sems = [(scratch.pop(0), scratch.pop(0)) for _ in range(7)]
    load_sem, prob_sem, stage_sem = scratch
    extra = sems[5]
    sums = Sums(
        here,
        (grad_att_ref, grad_ff_ref, grad_small_ref),
        (att_out, ff_out, small_own),
        (pairs, ones, twos, threes),
        sems,
    )
    load_ff = pltpu.make_async_copy(ff_hbm.at[1], ff_w, load_sem.at[0])
    load_att = pltpu.make_async_copy(att_hbm.at[1], att_w, load_sem.at[1])
    loads = [
        pltpu.make_async_copy(memory_hbm.at[0, here.y], memory_w.at[0], load_sem.at[2]),
        pltpu.make_async_copy(memory_hbm.at[1, here.y], memory_w.at[1], load_sem.at[3]),
        pltpu.make_async_copy(table_hbm.at[here.core], table_ref, load_sem.at[4]),
        pltpu.make_async_copy(grad_embedding_hbm, ranked_ref, load_sem.at[5]),
    ]
    load_grad = pltpu.make_async_copy(grad_hbm, grad_ref, load_sem.at[6])
    load_grad.start()
    load_normed = pltpu.make_async_copy(
        normed_two_hbm.at[1], prob_grad_ref.at[:, 0:D], load_sem.at[7]
    )
    load_normed.start()
    load_ff.start()
    load_att.start()
    for copy in loads:
        copy.start()
    others = [
        here.device(y=(here.y + s) % 4, core=(here.core + k) % 2)
        for s in range(4)
        for k in range(2)
        if s or k
    ]
    here.greet(others[2::2])
    rank_ref[...] = spread_rank(att_rank_ref[...], D)
    block_rank_ref[...] = spread_rank(ff_rank_ref[...], 256)
    here.greeted(13)
    own_rows = pl.ds(pl.multiple_of(here.core * OWN, OWN), OWN)
    their_rows = pl.ds(pl.multiple_of(OWN - here.core * OWN, OWN), OWN)
    ce_pair[here.core] = ce_ref[...]
    ce_copies = [send(ce_ref, ce_pair.at[here.core], extra, 0, here.sibling())]
    flip = (
        lax.broadcasted_iota(jnp.int32, (OWN, OWN), 0)
        + lax.broadcasted_iota(jnp.int32, (OWN, OWN), 1)
        == OWN - 1
    )
    flip = jnp.where(flip, 1.0, 0.0).astype(BF16)
    lane_head = lax.broadcasted_iota(jnp.int32, (OWN, 256), 1) // HD
    load_grad.wait()

    def spread_ce(step):
        source, target, axis, base = (
            (ce_pair, ce_z, "z", 1),
            (ce_z, ce_y, "y", 4),
            (ce_y, ce_x, "x", 7),
        )[step]
        for copy in ce_copies[-1:] if step == 0 else ce_copies[-3:]:
            copy.wait_recv()
        total = source[0] + source[1]
        if step:
            total = total + (source[2] + source[3])
        index = getattr(here, axis)
        target[index] = total
        for s in (1, 2, 3):
            ce_copies.append(
                send(target.at[index], target.at[index], extra, base + s - 1, here.along(axis, s))
            )

    def feed(layer):
        load_normed.wait()
        gsum, ggain, goffset = norm_backward(
            grad_ref[...], prob_grad_ref[:, 0:D], inverse_two_ref[layer], norm_ref[2, layer : layer + 1, :]
        )
        middle = normed_one_ref[layer] * norm_ref[0, layer : layer + 1, :] + norm_ref[1, layer : layer + 1, :]
        middle_low = middle.astype(BF16)
        middle_t = transposed(middle_low).astype(BF16)
        gbranch = gsum.astype(BF16)
        gbranch_t = transposed(gbranch).astype(BF16)
        gmiddle = gsum
        load_ff.wait()
        for cc in (1, 0):
            if cc == 0:
                sums.pair(1 if layer == 0 else 3)
            for r in range(4):
                bias = jnp.concatenate(
                    [bias_ref[cc, r, 3 * layer + 1 + i : 3 * layer + 2 + i, :] for i in range(2)],
                    axis=1,
                )
                inner = dot_nn(middle_low, ff_w[0, cc, r]) + bias
                active, slope = smooth_both(inner)
                ginner = (dot_nn(gbranch, ff_w[1, cc, r]) * slope).astype(BF16)
                grad_ff_ref[layer, 0, cc, r] = dot_nn(middle_t, ginner).astype(BF16)
                grad_ff_ref[layer, 1, cc, r] = dot_nn(gbranch_t, active.astype(BF16)).astype(BF16)
                grad_inner_ref[layer, cc, r] = jnp.sum(
                    ginner.astype(F32), axis=0, keepdims=True
                )
                gmiddle = gmiddle + dot_nt(ginner, ff_w[0, cc, r])
        rows = [jnp.sum(gsum, axis=0, keepdims=True)]
        gsum, ggain_one, goffset_one = norm_backward(
            gmiddle, normed_one_ref[layer], inverse_one_ref[layer], norm_ref[0, layer : layer + 1, :]
        )
        rows = [ggain_one, goffset_one, ggain, goffset] + rows
        for i, row in enumerate(rows):
            at = 8 * layer + i
            grad_norm_ref[at // 2, at % 2 : at % 2 + 1, :] = row
        grad_ref[...] = gsum

    def prepare(layer):
        gattended = grad_ref[...].astype(BF16)
        wide = dot_nn(transposed(mixed_ref[layer]).astype(BF16), gattended).astype(BF16)
        grad_att_ref[layer, 4] = wide.reshape(2, 4, HD, D)
        sums.pair(5 + layer)
        load_att.wait()
        gmix = dot_nt(gattended, att_w[4].reshape(D, D))
        gmix_ref[...] = gmix.astype(BF16)
        gmix_t_ref[...] = gmix.T.astype(BF16)
        query_t_ref[...] = transposed(query_u_ref[layer]).astype(BF16)
        flip_t_ref[...] = dot_nn(transposed(query_w_ref[layer]).astype(BF16), flip).astype(BF16)
        key_w, value_w = att_w[1].reshape(D, D), att_w[2].reshape(D, D)
        for half in range(2):
            rows = memory_w[layer] if half == 0 else low_ref[layer]
            cols = slice(half * SEG, (half + 1) * SEG)
            values_ref[:, cols] = dot_nt(value_w, rows).astype(BF16)
            keys = dot_nt(rows, key_w).astype(BF16)
            keys_ref[0, cols, :] = keys[:, 0:256]
            keys_ref[1, cols, :] = keys[:, 256:512]
        rel = dot_nt(table_ref[...], att_w[3].reshape(D, D)).astype(BF16)
        rel_ref[0] = rel[:, 0:256]
        rel_ref[1] = rel[:, 256:512]
        gquery_ref[...] = jnp.zeros_like(gquery_ref)

    def fetch(layer, n, slot):
        h = (n + 4) % HEADS
        return pltpu.make_async_copy(prob_hbm.at[layer, h], prob_ref.at[slot], prob_sem.at[slot])

    def head(layer):
        def run(n, carry):
            h = (n + 4) % HEADS
            group = h // 4
            slot = n % 2
            mine = lane_head == h % 4
            lanes = pl.ds(pl.multiple_of(group * 256, 256), 256)
            row = pl.ds(pl.multiple_of(h * HD, HD), HD)
            gmix_h = jnp.where(mine, gmix_ref[:, lanes].astype(F32), 0.0).astype(BF16)
            prob_grad_ref[...] = dot_nn(gmix_h, values_ref[lanes, :])
            fetch(layer, n, slot).wait()
            for b in range(0, OWN, ROWS):
                rows = slice(b, b + ROWS)
                prob = prob_ref[slot, rows, :]
                gprob = prob_grad_ref[rows, :]
                inner = jnp.sum(prob * gprob, axis=-1, keepdims=True)
                score_grad_ref[rows, :] = (prob * (gprob - inner)).astype(BF16)
                low_prob_ref[rows, :] = prob.astype(BF16)

            @pl.when(n < HEADS - 2)
            def _():
                fetch(layer, n + 2, slot).start()

            if layer == 1:
                @pl.when(n >= HEADS - 2)
                def _():
                    fetch(0, n + 2 - HEADS, slot).start()

            sgrad = score_grad_ref[...]
            gquery_ref[0, group] = gquery_ref[0, group] + jnp.where(
                mine, dot_nn(sgrad, keys_ref[group]), 0.0
            )
            gkey = dot_nn(query_t_ref[row, :], sgrad) * SCALE
            gvalue = dot_nn(gmix_t_ref[row, :], low_prob_ref[...])
            gmemory_ref[0, row, :] = gkey[:, 0:SEG].astype(BF16)
            gmemory_ref[1, row, :] = gvalue[:, 0:SEG].astype(BF16)
            ghidden_ref[0, row, :] = gkey[:, SEG:]
            ghidden_ref[1, row, :] = gvalue[:, SEG:]
            flipped = dot_nn(flip, sgrad).astype(BF16)
            flipped_ref[...] = pltpu.roll(flipped, KLEN - OWN + 1, 1, stride=1, stride_axis=0)
            gquery_ref[1, group] = gquery_ref[1, group] + jnp.where(
                mine, dot_nn(flipped_ref[...], rel_ref[group]), 0.0
            )
            grel_ref[row, :] = (dot_nn(flip_t_ref[row, :], flipped_ref[...]) * SCALE).astype(BF16)
            return carry

        return run

    def swap(layer, i):
        return send(
            ghidden_ref.at[:, 256 * i : 256 * i + 256, their_rows],
            got_ref.at[:, 256 - 256 * i : 512 - 256 * i],
            extra,
            10 + 2 * layer + i,
            here.sibling(),
        )

    def half(layer, group):
        own_low = low_ref[layer, own_rows, :]
        lanes = slice(group * 256, (group + 1) * 256)
        gquery_u = (gquery_ref[0, group] * SCALE).astype(BF16)
        gquery_w = dot_nn(flip, (gquery_ref[1, group] * SCALE).astype(BF16))
        grad_bias_ref[layer, 0:1, lanes] = jnp.sum(gquery_u.astype(F32), axis=0, keepdims=True)
        grad_bias_ref[layer, 1:2, lanes] = jnp.sum(gquery_w, axis=0, keepdims=True)
        gquery = gquery_u.astype(F32) + gquery_w
        grad_att_ref[layer, 0, group] = (
            dot_nn(gquery.T.astype(BF16), own_low).astype(BF16).reshape(4, HD, D)
        )
        grad_att_ref[layer, 3, group] = (
            dot_nn(grel_ref[lanes, :], table_ref[...]).astype(BF16).reshape(4, HD, D)
        )
        for i in range(2):
            part = dot_nn(gmemory_ref[i, lanes, :], memory_w[layer]) + dot_nn(
                ghidden_ref[i, lanes, :].astype(BF16), low_ref[layer]
            )
            grad_att_ref[layer, 1 + i, group] = part.astype(BF16).reshape(4, HD, D)
        return dot_nn(gquery.astype(BF16), att_w[0, group].reshape(256, D))

    def finish(swaps):
        for copy in swaps:
            copy.wait_recv()
        for i in range(2):
            total = (ghidden_ref[i, :, own_rows] + got_ref[i]).astype(BF16)
            grad_ref[...] += dot_nn(transposed(total).astype(BF16), att_w[1 + i].reshape(D, D))

    fetch(1, 0, 0).start()
    fetch(1, 1, 1).start()
    feed(1)
    load_ff = pltpu.make_async_copy(ff_hbm.at[0], ff_w, load_sem.at[0])
    load_ff.start()
    spread_ce(0)
    for copy in loads:
        copy.wait()
    prepare(1)
    sums.one(3)
    sums.one(6)
    lax.fori_loop(0, 4, head(1), 0)
    swaps_one = [swap(1, 1)]
    grad_ref[...] += half(1, 1)
    sums.pair(2)
    lax.fori_loop(4, HEADS, head(1), 0)
    swaps_one.append(swap(1, 0))
    load_normed = pltpu.make_async_copy(
        normed_two_hbm.at[0], prob_grad_ref.at[:, 0:D], load_sem.at[7]
    )
    load_normed.start()
    spread_ce(1)
    grad_ref[...] += half(1, 0)
    sums.one(2)
    sums.two(3)
    sums.two(6)
    finish(swaps_one)
    load_att = pltpu.make_async_copy(att_hbm.at[0], att_w, load_sem.at[1])
    load_att.start()
    feed(0)
    spread_ce(2)
    for copy in swaps_one:
        copy.wait_send()
    prepare(0)
    sums.one(1)
    sums.one(5)
    sums.two(2)
    lax.fori_loop(0, 4, head(0), 0)
    swaps_zero = [swap(0, 1)]
    grad_ref[...] += half(0, 1)
    sums.pair(0)
    sums.three(3)
    sums.three(6)
    lax.fori_loop(4, HEADS, head(0), 0)
    swaps_zero.append(swap(0, 0))
    grad_ref[...] += half(0, 0)
    sums.one(0)
    sums.two(1)
    sums.two(5)
    sums.three(2)
    finish(swaps_zero)

    def stage(pairs, slot):
        copies = []
        for i, (source, target) in enumerate(pairs):
            copies.append(pltpu.make_async_copy(source, target, stage_sem.at[10 * slot + i]))
            copies[-1].start()
        return copies

    def stage_ff(layer, mat):
        return stage(
            [
                (
                    source.at[layer, mat, 256 * i : 256 * i + 256],
                    prob_ref.at[mat, :, 512 * k + 256 * i : 512 * k + 256 * i + 256],
                )
                for k, source in enumerate((ff_weight_hbm, ff_moment_hbm))
                for i in range(2)
            ],
            mat,
        )

    def stage_att(layer):
        pairs = []
        for k, source in enumerate((att_weight_hbm, att_moment_hbm)):
            cols = slice(512 * k, 512 * k + 512)
            for i in range(4):
                pairs.append(
                    (source.at[layer, i], prob_ref.at[layer, 64 * i : 64 * i + 64, cols])
                )
            rows = slice(64 * layer, 64 * layer + 64)
            pairs.append((source.at[layer, 4], prob_grad_ref.at[rows, cols]))
        return stage(pairs, layer)

    squares = {ATT: [jnp.zeros((1, D), F32)] * 2, FFN: [jnp.zeros((1, 256), F32)] * 2}

    def add_squares(kind, total, weight, moment, rank):
        grad = masked(total.astype(F32), weight, rank)
        _, direction = advance_one(grad, weight, moment)
        first, second = squares[kind]
        squares[kind] = [first + square_sum(weight), second + square_sum(direction)]

    def square_ff(layer, copies):
        for copy in copies:
            copy.wait()
        for mat in range(2):
            for i in range(8):
                rows = slice(i % 4 * 64, i % 4 * 64 + 64)
                col = i // 4 * 256
                rank_at = layer * 16 + mat * 8 + i
                add_squares(
                    FFN,
                    ff_out[layer, mat, i * 64 : i * 64 + 64, :],
                    prob_ref[mat, rows, col : col + 256],
                    prob_ref[mat, rows, 512 + col : 768 + col],
                    block_rank_ref[rank_at : rank_at + 1, :],
                )

    def square_att(layer, copies):
        for copy in copies:
            copy.wait()
        for i in range(5):
            rows = slice(64 * i, 64 * i + 64) if i < 4 else slice(64 * layer, 64 * layer + 64)
            block = prob_ref.at[layer, rows] if i < 4 else prob_grad_ref.at[rows]
            add_squares(
                ATT,
                att_out[layer, i],
                block[:, 0:512],
                block[:, 512:1024],
                rank_ref[layer * 5 + i : layer * 5 + i + 1, :],
            )

    staged = stage_ff(1, 0) + stage_ff(1, 1)

    tokens = inputs_ref[pl.ds(here.y, 1), own_rows]
    onehot = jnp.where(
        tokens == lax.broadcasted_iota(jnp.int32, (VOCAB, OWN), 0), 1.0, 0.0
    ).astype(BF16)
    grad = grad_ref[...]
    high = grad.astype(BF16)
    rest = (grad - high.astype(F32)).astype(BF16)
    ranked_ref[...] += (dot_nn(onehot, high) + dot_nn(onehot, rest)).reshape(MP, 32, D)
    block_ref[...] = jnp.zeros_like(block_ref)
    for cc in range(2):
        for r in range(4):
            device = ((here.y + r) % 4) * 2 + (here.core + cc) % 2
            first = (cc * 4 + r) * HD
            block_ref[0:32, :] = ranked_ref[device]
            block_ref[32:34, :] = grad_norm_ref[device]
            block_ref[34:35, 0:256] = jnp.concatenate(
                [
                    grad_bias_ref[l, k : k + 1, first : first + HD]
                    for l in range(2)
                    for k in range(2)
                ],
                axis=1,
            )
            block_ref[35:36, :] = jnp.concatenate(
                [grad_inner_ref[l, cc, r] for l in range(2)], axis=1
            )
            grad_small_ref[0, 0, cc, r] = block_ref[...].astype(BF16)
    sums.pair(4)
    sums.four(3)
    sums.four(6)
    sums.one(4)
    sums.two(0)
    sums.three(1)
    sums.three(5)
    sums.two(4)
    sums.four(2)
    sums.arrived(4, 3)
    square_ff(1, staged)
    staged = stage_ff(0, 0) + stage_ff(0, 1)
    sums.three(0)
    sums.three(4)
    sums.four(1)
    sums.four(5)
    for copy in ce_copies[-3:]:
        copy.wait_recv()
    ce_out[...] = (ce_x[0] + ce_x[1]) + (ce_x[2] + ce_x[3])
    sums.four(4)
    sums.four(0)
    sums.arrived(4, 1)
    square_ff(0, staged)
    staged_one, staged_zero = stage_att(1), stage_att(0)
    sums.arrived(4, 4)
    small_out[here.y, here.core] = small_own[0, 0]
    piece = small_out.at[here.y, here.core]
    small_copies = [send(piece, piece, extra, 13 + r, here.along("y", r)) for r in (1, 2, 3)]
    small = small_own[0, 0].astype(F32)
    head_sums = [jnp.zeros((1, HD), F32)] * 2
    inner_sums = [jnp.zeros((1, 256), F32)] * 2
    for l in range(2):
        for k in range(2):
            at = (l * 2 + k) * HD
            weight = head_weight_ref[l, k : k + 1, :]
            _, direction = advance_one(
                small[34:35, at : at + HD], weight, head_moment_ref[l, k : k + 1, :]
            )
            head_sums = [head_sums[0] + weight * weight, head_sums[1] + direction * direction]
        weight = inner_weight_ref[l : l + 1, :]
        _, direction = advance_one(
            small[35:36, l * 256 : (l + 1) * 256], weight, inner_moment_ref[l : l + 1, :]
        )
        inner_sums = [inner_sums[0] + weight * weight, inner_sums[1] + direction * direction]
    sums.arrived(4, 2)
    sums.arrived(4, 6)
    square_att(1, staged_one)
    for copy in small_copies:
        copy.wait_recv()
    piece = small_out.at[:, here.core]
    last = send(piece, piece, extra, 17, here.sibling())
    sums.arrived(4, 5)
    sums.arrived(4, 0)
    square_att(0, staged_zero)
    for k in range(2):
        for i, value in enumerate((squares[ATT], squares[FFN], head_sums, inner_sums)):
            part_ref[4 * k + i : 4 * k + i + 1, :] = jnp.broadcast_to(
                jnp.sum(value[k], axis=1, keepdims=True), (1, 128)
            )
    index = here.y * 2 + here.core
    parts_out[index] = part_ref[...]
    norm_copies = [
        send(part_ref, parts_out.at[index], sems[6], i, partner)
        for i, partner in enumerate(others)
    ]
    last.wait()
    for copy in norm_copies:
        copy.wait()
    for copy in ce_copies + swaps_zero + small_copies:
        copy.wait_send()
    sums.end()


def backward_all(*operands):
    vmem, hbm = VMEM_SPEC, ANY_SPEC
    outs = [
        ((2, 5, HD, D), BF16),
        ((2, 2, D, 256), BF16),
        ((4, 2, 64, D), BF16),
        ((8, 128), F32),
        ((MP, 8, 128), F32),
    ]
    scratch = [
        pltpu.VMEM((5, 2, 4, HD, D), BF16),
        pltpu.VMEM((2, 2, 4, D, 256), BF16),
        pltpu.VMEM((2, SEG, D), BF16),
        pltpu.VMEM((KLEN, D), BF16),
        pltpu.VMEM((2, OWN, KLEN), F32),
        pltpu.VMEM((2, 5, 2, 4, HD, D), BF16),
        pltpu.VMEM((2, 2, 2, 4, D, 256), BF16),
        pltpu.VMEM((1, 1, 2, 4, 64, D), BF16),
        pltpu.VMEM((OWN, D), F32),
        pltpu.VMEM((2, KLEN, 256), BF16),
        pltpu.VMEM((D, KLEN), BF16),
        pltpu.VMEM((2, KLEN, 256), BF16),
        pltpu.VMEM((OWN, D), BF16),
        pltpu.VMEM((D, OWN), BF16),
        pltpu.VMEM((D, OWN), BF16),
        pltpu.VMEM((D, OWN), BF16),
        pltpu.VMEM((OWN, KLEN), F32),
        pltpu.VMEM((OWN, KLEN), BF16),
        pltpu.VMEM((OWN, KLEN), BF16),
        pltpu.VMEM((OWN, KLEN), BF16),
        pltpu.VMEM((2, 2, OWN, 256), F32),
        pltpu.VMEM((2, D, SEG), BF16),
        pltpu.VMEM((2, D, SEG), F32),
        pltpu.VMEM((2, D, OWN), F32),
        pltpu.VMEM((D, KLEN), BF16),
        pltpu.VMEM((2, 2, D), F32),
        pltpu.VMEM((2, 2, 4, 1, 256), F32),
        pltpu.VMEM((MP, 2, D), F32),
        pltpu.VMEM((MP, 32, D), F32),
        pltpu.VMEM((64, D), F32),
        pltpu.VMEM((2, 8, 128), F32),
        pltpu.VMEM((4, 8, 128), F32),
        pltpu.VMEM((4, 8, 128), F32),
        pltpu.VMEM((4, 8, 128), F32),
        pltpu.VMEM((1, 1, 64, D), BF16),
        pltpu.VMEM((10, D), F32),
        pltpu.VMEM((32, 256), F32),
        pltpu.VMEM((8, 128), F32),
    ]
    scratch += [pltpu.VMEM((hi - lo, 4) + SHAPES[k], BF16) for k, _, (lo, hi), _, _ in SUM_GROUPS]
    for kind, _, _, parts, rows in SUM_GROUPS:
        width = SHAPES[kind][1]
        scratch += [pltpu.VMEM((3, hi - lo, 4, rows, width), BF16) for _, lo, hi in parts]
        scratch += [pltpu.VMEM((3, hi - lo, rows, width), BF16) for _, lo, hi in parts]
        scratch += [pltpu.VMEM((4, hi - lo, rows, width), BF16) for _, lo, hi in parts]
    for n in (7, 42, 42, 42, 42, 18, 7):
        scratch += [pltpu.SemaphoreType.DMA((n,)), pltpu.SemaphoreType.DMA((n,))]
    scratch += [pltpu.SemaphoreType.DMA((n,)) for n in (8, 2, 20)]
    return pl.pallas_call(
        backward_step,
        out_shape=[jax.ShapeDtypeStruct(s, t) for s, t in outs],
        in_specs=[hbm] * 12 + [vmem] * 17,
        out_specs=[vmem] * 5,
        scratch_shapes=scratch,
        compiler_params=pltpu.CompilerParams(
            collective_id=1, has_side_effects=True, vmem_limit_bytes=63 * 1024 * 1024
        ),
        name="backward_all",
    )(*operands)


def update_kernel(*refs):
    (
        att_w_hbm,
        att_m_hbm,
        att_a_hbm,
        ff_w_hbm,
        ff_m_hbm,
        ff_a_hbm,
        new_memory_hbm,
        att_sum_ref,
        ff_sum_ref,
        small_ref,
        parts_ref,
        att_rank_ref,
        ff_rank_ref,
        ce_ref,
        count_ref,
        *rest,
    ) = refs[:27]
    embedding, head, inner, norm = (rest[3 * i : 3 * i + 3] for i in range(4))
    outs = refs[27:51]
    outs[22][...] = ce_ref[0:1, 0:1]
    outs[23][...] = count_ref[0:1, 0:1]
    att_outs, ff_outs, new_memory_out = outs[0:4], outs[4:8], outs[8]
    embedding_outs, head_outs, inner_outs, norm_outs = (
        outs[9:12],
        outs[12:15],
        outs[15:18],
        outs[18:22],
    )
    att, ff = refs[51:55], refs[55:59]
    att_rank, ff_rank, memory_ref, load_sem, store_sem, memory_sem = refs[59:]
    loads, stores = [], []
    for l in range(2):
        for k, (sources, targets) in enumerate(
            (((ff_w_hbm, ff_m_hbm, ff_a_hbm), ff), ((att_w_hbm, att_m_hbm, att_a_hbm), att))
        ):
            for i in range(3):
                copy = pltpu.make_async_copy(
                    sources[i].at[l], targets[i].at[l], load_sem.at[6 * l + 3 * k + i]
                )
                copy.start()
                loads.append(copy)
    memory_in = pltpu.make_async_copy(new_memory_hbm, memory_ref, memory_sem.at[0])
    memory_in.start()
    att_rank[...] = spread_rank(att_rank_ref[...], D)
    ff_rank[...] = spread_rank(ff_rank_ref[...], 256)
    total = parts_ref[0]
    for m in range(1, MP):
        total = total + parts_ref[m]

    def rate(weight_square, direction_square):
        return RATE * (jnp.sqrt(weight_square) / jnp.sqrt(direction_square))

    def step(weight, direction, average, ratio):
        weight_next = weight - ratio * direction
        return weight_next, AVERAGE * average + (1.0 - AVERAGE) * weight_next

    ratios = [rate(total[i : i + 1, 0:1], total[4 + i : 5 + i, 0:1]) for i in range(4)]

    small = small_ref[lax.axis_index("mp") // 2, lax.axis_index("mp") % 2].astype(F32)
    for l in range(2):
        for k in range(2):
            at = (l * 2 + k) * HD
            row = (l, slice(k, k + 1))
            moment, direction = advance_one(small[34:35, at : at + HD], head[0][row], head[1][row])
            head_outs[1][row] = moment
            head_outs[0][row], head_outs[2][row] = step(
                head[0][row], direction, head[2][row], ratios[2]
            )
        row = slice(l, l + 1)
        moment, direction = advance_one(
            small[35:36, l * 256 : (l + 1) * 256], inner[0][row], inner[1][row]
        )
        inner_outs[1][row] = moment
        inner_outs[0][row], inner_outs[2][row] = step(
            inner[0][row], direction, inner[2][row], ratios[3]
        )
    squares = [jnp.zeros((1, D), F32), jnp.zeros((1, D), F32)]
    for i in range(5):
        for l in range(2):
            at = 8 * l + i
            row = (i, slice(l, l + 1))
            grad = small_ref[at // 4, at // 2 % 2, 32:34, :].astype(F32)[at % 2 : at % 2 + 1]
            moment, direction = advance_one(grad, norm[0][row], norm[1][row])
            norm_outs[0][row] = grad
            norm_outs[2][row] = moment
            squares[0] = squares[0] + norm[0][row] * norm[0][row]
            squares[1] = squares[1] + direction * direction
    ratio = rate(*[jnp.sum(value, axis=1, keepdims=True) for value in squares])
    for i in range(5):
        direction = norm_outs[0][i] + MOMENTUM * norm_outs[2][i]
        norm_outs[1][i], norm_outs[3][i] = step(norm[0][i], direction, norm[2][i], ratio)
    squares = [jnp.zeros((1, D), F32), jnp.zeros((1, D), F32)]
    for m in range(MP):
        rows = slice(m * 32, (m + 1) * 32)
        grad = small_ref[m // 2, m % 2, 0:32, :].astype(F32)
        moment, direction = advance_one(grad, embedding[0][rows], embedding[1][rows])
        embedding_outs[1][rows] = moment
        squares[0] = squares[0] + square_sum(embedding[0][rows])
        squares[1] = squares[1] + square_sum(direction)
    ratio = rate(*[jnp.sum(value, axis=1, keepdims=True) for value in squares])
    for m in range(MP):
        rows = slice(m * 32, (m + 1) * 32)
        grad = small_ref[m // 2, m % 2, 0:32, :].astype(F32)
        direction = grad + MOMENTUM * embedding_outs[1][rows]
        embedding_outs[0][rows], embedding_outs[2][rows] = step(
            embedding[0][rows], direction, embedding[2][rows], ratio
        )

    def advance(refs, at, total, rank, ratio):
        weight, moment, average, grad_ref = refs
        grad = masked(total.astype(F32), weight[at], rank)
        moment_next, direction = advance_one(grad, weight[at], moment[at])
        grad_ref[at] = grad
        moment[at] = moment_next
        weight[at], average[at] = step(weight[at], direction, average[at], ratio)

    for l in range(2):
        for k in range(2):
            for i in range(3):
                loads[6 * l + 3 * k + i].wait()
            if k == 0:

                def block(i, carry):
                    at = (l, i // 8, pl.ds(pl.multiple_of(i % 8 * 64, 64), 64))
                    rank = ff_rank[pl.ds(l * 16 + i, 1), :]
                    advance(ff, at, ff_sum_ref[at], rank, ratios[1])
                    return carry

                lax.fori_loop(0, 16, block, 0)
            else:

                def block(i, carry):
                    rank = att_rank[pl.ds(l * 5 + i, 1), :]
                    advance(att, (l, i), att_sum_ref[l, i], rank, ratios[0])
                    return carry

                lax.fori_loop(0, 5, block, 0)
            sources, targets = ((ff, ff_outs), (att, att_outs))[k]
            for i, source in enumerate((3, 0, 1, 2)):
                copy = pltpu.make_async_copy(
                    sources[source].at[l], targets[i].at[l], store_sem.at[8 * l + 4 * k + i]
                )
                copy.start()
                stores.append(copy)
    memory_in.wait()
    memory_back = pltpu.make_async_copy(memory_ref, new_memory_out, memory_sem.at[1])
    memory_back.start()
    for copy in stores:
        copy.wait()
    memory_back.wait()


def update(*operands):
    att, ff = (2, 5, HD, D), (2, 2, D, 256)
    shapes = [att] * 4 + [ff] * 4
    rest = [(VOCAB, D)] * 3 + [(2, 2, HD)] * 3 + [(2, 256)] * 3 + [(5, 2, D)] * 4 + [(1, 1)] * 2
    return pl.pallas_call(
        update_kernel,
        out_shape=[jax.ShapeDtypeStruct(s, F32) for s in shapes]
        + [jax.ShapeDtypeStruct((2, 4, SEG, D), BF16)]
        + [jax.ShapeDtypeStruct(s, F32) for s in rest],
        in_specs=[ANY_SPEC] * 7 + [VMEM_SPEC] * 20,
        out_specs=[ANY_SPEC] * 9 + [VMEM_SPEC] * 15,
        scratch_shapes=[pltpu.VMEM(att, F32)] * 4
        + [pltpu.VMEM(ff, F32)] * 4
        + [
            pltpu.VMEM((10, D), F32),
            pltpu.VMEM((32, 256), F32),
            pltpu.VMEM((2, 4, SEG, D), BF16),
            pltpu.SemaphoreType.DMA((12,)),
            pltpu.SemaphoreType.DMA((16,)),
            pltpu.SemaphoreType.DMA((2,)),
        ],
        compiler_params=pltpu.CompilerParams(vmem_limit_bytes=62 * 1024 * 1024),
        name="update",
    )(*operands)


def body(
    inputs,
    targets,
    valid_mask,
    memory,
    attention_rank,
    feedforward_rank,
    attention_weight,
    attention_moment,
    attention_average,
    feedforward_weight,
    feedforward_moment,
    feedforward_average,
    embedding_weight,
    embedding_moment,
    embedding_average,
    head_bias_weight,
    head_bias_moment,
    head_bias_average,
    inner_bias_weight,
    inner_bias_moment,
    inner_bias_average,
    norm_weight,
    norm_moment,
    norm_average,
):
    def turned(value):
        return value.transpose(0, 1, 3, 2)

    def swapped(value):
        return value.transpose(1, 0, 2)

    att_rank = attention_rank.reshape(10, 8).astype(F32)
    ff_rank = feedforward_rank.reshape(32, 4).astype(F32)
    table = tables()
    (
        att_got,
        ff_got,
        new_memory,
        probs,
        bias_got,
        count_got,
        lows,
        query_u,
        query_w,
        mixed,
        normed_one,
        inverse_one,
        normed_two,
        inverse_two,
        grad_hidden,
        grad_embedding,
        ce_local,
    ) = forward_all(
        turned(attention_weight),
        feedforward_weight,
        att_rank,
        ff_rank,
        head_bias_weight,
        inner_bias_weight,
        embedding_weight,
        inputs,
        targets,
        valid_mask,
        memory,
        swapped(norm_weight),
        table,
    )
    grad_attention, grad_feedforward, grad_small, ce_got, parts = backward_all(
        att_got,
        ff_got,
        probs,
        memory,
        table,
        grad_hidden,
        grad_embedding,
        normed_two,
        turned(attention_weight),
        turned(attention_moment),
        feedforward_weight,
        feedforward_moment,
        att_rank,
        ff_rank,
        head_bias_weight,
        head_bias_moment,
        inner_bias_weight,
        inner_bias_moment,
        bias_got,
        swapped(norm_weight),
        inputs,
        ce_local,
        lows,
        query_u,
        query_w,
        mixed,
        normed_one,
        inverse_one,
        inverse_two,
    )
    updated = update(
        turned(attention_weight),
        turned(attention_moment),
        turned(attention_average),
        feedforward_weight,
        feedforward_moment,
        feedforward_average,
        new_memory,
        grad_attention,
        grad_feedforward,
        grad_small,
        parts,
        att_rank,
        ff_rank,
        ce_got,
        count_got,
        embedding_weight,
        embedding_moment,
        embedding_average,
        head_bias_weight,
        head_bias_moment,
        head_bias_average,
        inner_bias_weight,
        inner_bias_moment,
        inner_bias_average,
        swapped(norm_weight),
        swapped(norm_moment),
        swapped(norm_average),
    )
    return (
        updated[22].reshape(()),
        updated[23].reshape(()),
        updated[8],
        *[turned(value) for value in updated[0:4]],
        *updated[4:8],
        *updated[9:18],
        *[swapped(value) for value in updated[18:22]],
    )


def solution(mesh):
    rows = P("dp", None)
    matrix = P(None, None, None, "mp")
    split_two = P(None, None, "mp")
    split_one = P(None, "mp")
    whole = P()
    return jax.shard_map(
        body,
        mesh=mesh,
        in_specs=(
            (rows,) * 3
            + (P(None, "dp", None, None),)
            + (matrix,) * 8
            + (whole,) * 3
            + (split_two,) * 3
            + (split_one,) * 3
            + (whole,) * 3
        ),
        out_specs=(
            (whole,) * 2
            + (P(None, "dp", None, None),)
            + (matrix,) * 8
            + (whole,) * 3
            + (split_two,) * 3
            + (split_one,) * 3
            + (whole,) * 4
        ),
        check_vma=False,
    )
```
